512 devices in a mesh: dp: 16 (over y, z_lo), fsdp: 32 (over x, z_hi, core).
Axes of the slice: x: 4, y: 8, z: 8 (z_hi: 4, z_lo: 2; z = z_hi * 2 + z_lo), core: 2. Of those that a mesh axis runs over, the one named last changes fastest.
Arguments:
- signal: bfloat16 [131072, 1024], P(('dp', 'fsdp')), may hold values from -6 to 6
- grad_gated: bfloat16 [131072, 512], P(('dp', 'fsdp')), may hold values from -24 to 24
- conv_weight: bfloat16 [1024, 3072], P('fsdp'), may hold values from -0.109375 to 0.109375
- source_seg: int32 [512, 32], P(('dp', 'fsdp')), may hold values from -1 to 1023, as said below
Outputs:
- gated_out: bfloat16 [131072, 512], P(('dp', 'fsdp'))
- grad_in: bfloat16 [131072, 1024], P(('dp', 'fsdp'))
- grad_weight: float32 [1024, 3072], P('fsdp')
The draws below stay inside these ranges and needn't reach their ends.
Inputs may be any that keep to these rules, and one draw needn't show every extreme that they name: `source_seg`: -1 where a stream begins. The preceding segment holds the same position on its device as g on its own, no two segments of one device take their left context from the same device, and every segment precedes at most one segment.
All inputs are finite; a program needn't handle non-finite values.
Results may differ from the reference program's by a relative error of at most 0.0049.
Values may be sent and summed in bfloat16 or wider, within the bound.
A program may use at most 64 MiB of HBM per device.

```python
import math
import jax
import jax.numpy as jnp
from jax import lax

C = 1024
H = 512
DILATION_SIZE = 4
CONTEXT_ROWS = 8
SEG_LEN = 8
SEGS = 32
TOKENS = 131072
N_DP = 16
N_FSDP = 32


def one_permutation(subkey):
    return jax.random.permutation(subkey, N_FSDP)


def draw_source_seg(key, part):
    base = jax.random.fold_in(key, 7)
    perm_keys = jax.random.split(jax.random.fold_in(base, 1), N_DP)
    shift_amounts = jax.vmap(one_permutation)(perm_keys).astype(jnp.int32)
    begins = jax.random.randint(jax.random.fold_in(base, 2), (N_DP, N_FSDP, SEGS), 0, 5) == 0
    device = jnp.arange(N_FSDP, dtype=jnp.int32)[None, :, None]
    position = jnp.arange(SEGS, dtype=jnp.int32)[None, None, :]
    shift_rows_down = shift_amounts[:, None, :]
    source_dev = (device - shift_rows_down) % N_FSDP
    source = jnp.where(begins, -1, source_dev * SEGS + position)
    return source.reshape(N_DP * N_FSDP, SEGS).astype(jnp.int32)


def spiked(array, rng, source, target, shards_of, factor):
    def block_of(dim):
        return (jnp.arange(array.shape[dim]) // (array.shape[dim] // shards_of)).reshape((-1,) + (1,) * (array.ndim - 1 - dim))

    near = jax.random.permutation(rng, shards_of)[block_of(target)]
    other_side = (block_of(target) + shards_of // 2) % shards_of
    return jnp.where((block_of(source) == near) | (block_of(source) == other_side), factor * array, array)


def block_levels(key, extent, cuts, smallest, largest):
    level, own = 1.0, jax.random.fold_in(key, 6)
    for dim, blocks in cuts:
        draws = jnp.exp(jax.random.uniform(jax.random.fold_in(own, dim), (blocks,), jnp.float32, smallest / len(cuts), largest / len(cuts)))
        level = level * jnp.repeat(draws, extent[dim] // blocks).reshape([-1 if axis == dim else 1 for axis in range(len(extent))])
    return level


def scatter_about(rng, shape, spread, limit, cuts=(), held_as=jnp.bfloat16):
    values = jax.random.normal(rng, shape, jnp.float32) * spread
    if len(cuts) > 0:
        values = block_levels(rng, shape, cuts, -0.22, 0.18) * values
    return jnp.clip(values, min=-limit, max=limit).astype(held_as)


def noise_with(stream_key, extent, deviation, reach, cuts, heavy, kind=jnp.bfloat16):
    values = deviation * jax.random.normal(stream_key, extent, jnp.float32)
    if cuts:
        values = values * block_levels(stream_key, extent, cuts, -0.22, 0.18)
    return jnp.clip(spiked(values, jax.random.fold_in(stream_key, 3), *heavy), -reach, reach).astype(kind)


def setup_inputs(seed: int = 0) -> dict:
    arg_keys = jax.random.split(jax.random.key(seed), 5)
    signal = scatter_about(arg_keys[0], (TOKENS, C), 1.0, 6.0, ((0, 512),))
    grad_gated = noise_with(arg_keys[1], (TOKENS, H), 1.0, 24.0, ((0, 512),), (0, 1, 512, 6.0))
    conv_weight = scatter_about(arg_keys[2], (2 * H, 3 * C), (3 * C) ** -0.5, 0.109375, ((0, 32),))
    source_seg = draw_source_seg(jax.random.fold_in(arg_keys[4], 71), 0)
    return {"signal": signal, "grad_gated": grad_gated, "conv_weight": conv_weight, "source_seg": source_seg}


def tap_starts():
    return [CONTEXT_ROWS - (2 - selected_index) * DILATION_SIZE for selected_index in range(3)]

def reference(signal, grad_gated, conv_weight, source_seg):
    group_segs = N_FSDP * SEGS
    signal_groups = signal.reshape(N_DP, group_segs, SEG_LEN, C)
    grad_groups = grad_gated.reshape(N_DP, group_segs * SEG_LEN, H)
    source_groups = source_seg.reshape(N_DP, group_segs)
    starts = tap_starts()

    def one_group(operands):
        segments, upstream, sources = operands
        tail_rows = segments[:, SEG_LEN - CONTEXT_ROWS:, :]
        has_source = sources >= 0
        picked = jnp.take(tail_rows, jnp.maximum(sources, 0).astype(jnp.int32), axis=0)
        carries = jnp.where(has_source[:, None, None], picked, jnp.zeros_like(picked))
        extended = jnp.concatenate([carries, segments], axis=1)
        stacked = jnp.concatenate([extended[:, start:start + SEG_LEN, :] for start in starts], axis=2)
        stacked = stacked.reshape(group_segs * SEG_LEN, 3 * C)
        preact = jnp.dot(stacked, conv_weight.T, preferred_element_type=jnp.float32)
        filter_act = jnp.tanh(preact[:, :H])
        gate_act = jax.nn.sigmoid(preact[:, H:])
        gated_out = (filter_act * gate_act).astype(jnp.bfloat16)
        upstream_wide = upstream.astype(jnp.float32)
        grad_pre = jnp.concatenate([upstream_wide * gate_act * (1.0 - filter_act * filter_act), upstream_wide * filter_act * gate_act * (1.0 - gate_act)], axis=1).astype(jnp.bfloat16)
        partials = jnp.einsum('drj,drc->djc', grad_pre.reshape(N_FSDP, SEGS * SEG_LEN, 2 * H).astype(jnp.float32), stacked.reshape(N_FSDP, SEGS * SEG_LEN, 3 * C).astype(jnp.float32))
        rounded = lax.optimization_barrier(partials.astype(jnp.bfloat16))
        group_sum = lax.optimization_barrier(jnp.sum(rounded.astype(jnp.float32), axis=0))
        back_proj = jnp.dot(grad_pre, conv_weight, preferred_element_type=jnp.float32)
        back_proj = back_proj.reshape(group_segs, SEG_LEN, 3 * C)
        grad_ext = jnp.zeros((group_segs, CONTEXT_ROWS + SEG_LEN, C), jnp.float32)
        for selected_index, start in enumerate(starts):
            grad_ext = grad_ext.at[:, start:start + SEG_LEN, :].add(back_proj[:, :, selected_index * C:(selected_index + 1) * C])
        carry_grad = jnp.where(has_source[:, None, None], grad_ext[:, :CONTEXT_ROWS, :], jnp.zeros_like(grad_ext[:, :CONTEXT_ROWS, :]))
        target = jnp.where(has_source, sources, group_segs).astype(jnp.int32)
        tail_grad = jax.ops.segment_sum(carry_grad, target, num_segments=group_segs + 1)[:group_segs]
        grad_in = grad_ext[:, CONTEXT_ROWS:, :].at[:, SEG_LEN - CONTEXT_ROWS:, :].add(tail_grad)
        return (gated_out, grad_in.reshape(group_segs * SEG_LEN, C).astype(jnp.bfloat16), group_sum)
    gated_out, grad_in, group_sums = lax.map(one_group, (signal_groups, grad_groups, source_groups))
    grad_weight = lax.optimization_barrier(jnp.sum(group_sums, axis=0)) * (1.0 / math.sqrt(TOKENS))
    return (gated_out.reshape(TOKENS, H), grad_in.reshape(TOKENS, C), grad_weight)
```

```python
import functools
import math

import jax
import jax.numpy as jnp
from jax import lax
from jax.experimental import pallas as pl
from jax.experimental.pallas import tpu as pltpu
from jax.sharding import PartitionSpec as P

MESH = pl.DeviceIdType.MESH

C = 1024
H = 512
DILATION_SIZE = 4


def all_reduce_kernel(axis, n, x_ref, out_ref, gathered, summed, send_sems, recv_sems, out_send, out_recv):
    me = lax.axis_index(axis)
    barrier = pltpu.get_barrier_semaphore()
    for k in range(1, n):
        peer = lax.rem(me + k, n)
        pl.semaphore_signal(barrier, inc=1, device_id={axis: peer}, device_id_type=MESH)
    pl.semaphore_wait(barrier, n - 1)
    sends = []
    for k in range(1, n):
        peer = lax.rem(me + k, n)
        copy = pltpu.make_async_remote_copy(
            src_ref=x_ref.at[peer],
            dst_ref=gathered.at[me],
            send_sem=send_sems.at[peer],
            recv_sem=recv_sems.at[me],
            device_id={axis: peer},
            device_id_type=MESH,
        )
        copy.start()
        sends.append(copy)
    gathered[me] = x_ref[me]
    for k in range(1, n):
        peer = lax.rem(me + k, n)
        pltpu.make_async_remote_copy(
            src_ref=x_ref.at[peer],
            dst_ref=gathered.at[peer],
            send_sem=send_sems.at[peer],
            recv_sem=recv_sems.at[peer],
            device_id={axis: peer},
            device_id_type=MESH,
        ).wait_recv()
    for copy in sends:
        copy.wait_send()
    total = gathered[0]
    for k in range(1, n):
        total = total + gathered[k]
    summed[...] = total
    out_ref[me] = total
    shares = []
    for k in range(1, n):
        peer = lax.rem(me + k, n)
        copy = pltpu.make_async_remote_copy(
            src_ref=summed,
            dst_ref=out_ref.at[me],
            send_sem=out_send.at[peer],
            recv_sem=out_recv.at[me],
            device_id={axis: peer},
            device_id_type=MESH,
        )
        copy.start()
        shares.append(copy)
    for k in range(1, n):
        peer = lax.rem(me + k, n)
        pltpu.make_async_remote_copy(
            src_ref=summed,
            dst_ref=out_ref.at[peer],
            send_sem=out_send.at[peer],
            recv_sem=out_recv.at[peer],
            device_id={axis: peer},
            device_id_type=MESH,
        ).wait_recv()
    for copy in shares:
        copy.wait_send()


def all_reduce(x, axis):
    n = lax.axis_size(axis)
    shape = x.shape
    blocks = x.reshape(n, -1, 128)
    block_shape = blocks.shape[1:]
    out = pl.pallas_call(
        functools.partial(all_reduce_kernel, axis, n),
        out_shape=jax.ShapeDtypeStruct(blocks.shape, x.dtype),
        in_specs=[pl.BlockSpec(memory_space=pltpu.VMEM)],
        out_specs=pl.BlockSpec(memory_space=pltpu.VMEM),
        scratch_shapes=[
            pltpu.VMEM(blocks.shape, x.dtype),
            pltpu.VMEM(block_shape, x.dtype),
            pltpu.SemaphoreType.DMA((n,)),
            pltpu.SemaphoreType.DMA((n,)),
            pltpu.SemaphoreType.DMA((n,)),
            pltpu.SemaphoreType.DMA((n,)),
        ],
        compiler_params=pltpu.CompilerParams(collective_id=0, has_side_effects=True),
    )(blocks)
    return out.reshape(shape)


def tap_starts(context_row_block):
    return [context_row_block - (2 - selected_index) * DILATION_SIZE for selected_index in range(3)]


def per_device(signal, grad_gated, conv_weight, source_seg):
    peer_count = lax.axis_size("fsdp")
    seg_count = source_seg.shape[1]
    row_count = signal.shape[0]
    seg_rows = row_count // seg_count
    context_row_block = 2 * DILATION_SIZE
    starts = tap_starts(context_row_block)
    segments = signal.reshape(seg_count, seg_rows, C)
    sources = source_seg[0]
    source_dev = jnp.where(sources >= 0, sources // seg_count, -1)
    peers = jnp.arange(peer_count, dtype=jnp.int32)
    request_mask = (source_dev[None, :] == peers[:, None]).astype(jnp.int32)
    asked = lax.all_to_all(request_mask, "fsdp", split_axis=0, concat_axis=0, tiled=True)
    send_table = asked.astype(jnp.bfloat16)
    recv_table = (source_dev[:, None] == peers[None, :]).astype(jnp.bfloat16)
    outgoing = jnp.einsum(
        "ns,slc->nlc", send_table, segments, preferred_element_type=jnp.float32
    ).astype(jnp.bfloat16)
    incoming = lax.all_to_all(outgoing, "fsdp", split_axis=0, concat_axis=0, tiled=True)
    carries = jnp.einsum(
        "sn,nlc->slc", recv_table, incoming, preferred_element_type=jnp.float32
    ).astype(jnp.bfloat16)
    extended = jnp.concatenate([carries, segments], axis=1)
    full_weight = lax.all_gather(conv_weight, "fsdp", axis=0, tiled=True)
    contract_final_axis = (((1,), (1,)), ((), ()))
    contract_first = (((0,), (0,)), ((), ()))
    windows = [extended[:, start : start + seg_rows, :].reshape(row_count, C) for start in starts]
    preact = sum(
        (
            lax.dot_general(
                windows[selected_index],
                full_weight[:, selected_index * C : (selected_index + 1) * C],
                contract_final_axis,
                preferred_element_type=jnp.float32,
            )
            for selected_index in range(3)
        )
    )
    filter_act = jnp.tanh(preact[:, :H])
    gate_act = jax.nn.sigmoid(preact[:, H:])
    gated_out = (filter_act * gate_act).astype(jnp.bfloat16)
    upstream_wide = grad_gated.astype(jnp.float32)
    grad_pre = jnp.concatenate(
        [
            upstream_wide * gate_act * (1.0 - filter_act * filter_act),
            upstream_wide * filter_act * gate_act * (1.0 - gate_act),
        ],
        axis=1,
    ).astype(jnp.bfloat16)
    partial_value = jnp.concatenate(
        [
            lax.dot_general(
                grad_pre,
                windows[selected_index],
                contract_first,
                preferred_element_type=jnp.float32,
            ).astype(jnp.bfloat16)
            for selected_index in range(3)
        ],
        axis=1,
    )
    arrived = lax.all_to_all(partial_value, "fsdp", split_axis=0, concat_axis=0, tiled=True)
    shard_sum = jnp.sum(arrived.reshape(peer_count, -1, 3 * C), axis=0, dtype=jnp.float32)
    group_total = all_reduce(shard_sum, "dp")
    total_token_count = row_count * peer_count * lax.axis_size("dp")
    grad_weight = group_total * (1.0 / math.sqrt(total_token_count))
    back_proj = jnp.dot(grad_pre, full_weight, preferred_element_type=jnp.float32)
    back_proj = back_proj.reshape(seg_count, seg_rows, 3 * C)
    grad_ext = jnp.zeros((seg_count, context_row_block + seg_rows, C), jnp.float32)
    for selected_index, start in enumerate(starts):
        grad_ext = grad_ext.at[:, start : start + seg_rows, :].add(
            back_proj[:, :, selected_index * C : (selected_index + 1) * C]
        )
    outgoing_grad = jnp.einsum(
        "sn,slc->nlc",
        recv_table.astype(jnp.float32),
        grad_ext[:, :context_row_block, :],
        precision=lax.Precision.HIGHEST,
    )
    incoming_grad = lax.all_to_all(outgoing_grad, "fsdp", split_axis=0, concat_axis=0, tiled=True)
    tail_grad = jnp.einsum(
        "ns,nlc->slc",
        send_table.astype(jnp.float32),
        incoming_grad,
        precision=lax.Precision.HIGHEST,
    )
    grad_in = (
        grad_ext[:, context_row_block:, :].at[:, seg_rows - context_row_block :, :].add(tail_grad)
    )
    grad_in = grad_in.reshape(row_count, C).astype(jnp.bfloat16)
    return (gated_out, grad_in, grad_weight)


def solution(mesh):
    placed = (
        P(("dp", "fsdp"), None),
        P(("dp", "fsdp"), None),
        P("fsdp", None),
        P(("dp", "fsdp"), None),
    )
    return jax.shard_map(
        per_device,
        mesh=mesh,
        in_specs=placed,
        out_specs=(P(("dp", "fsdp"), None), P(("dp", "fsdp"), None), P("fsdp", None)),
        check_vma=False,
    )
```

```python
import functools
import math

import jax
import jax.numpy as jnp
from jax import lax
from jax.experimental import pallas as pl
from jax.experimental.pallas import tpu as pltpu
from jax.sharding import PartitionSpec as P

MESH = pl.DeviceIdType.MESH

C = 1024
H = 512
DILATION_SIZE = 4
Z_HI = 4


def all_reduce_kernel(axis, n, x_ref, out_ref, gathered, summed, send_sems, recv_sems, out_send, out_recv):
    me = lax.axis_index(axis)
    barrier = pltpu.get_barrier_semaphore()
    for k in range(1, n):
        peer = lax.rem(me + k, n)
        pl.semaphore_signal(barrier, inc=1, device_id={axis: peer}, device_id_type=MESH)
    pl.semaphore_wait(barrier, n - 1)
    sends = []
    for k in range(1, n):
        peer = lax.rem(me + k, n)
        copy = pltpu.make_async_remote_copy(
            src_ref=x_ref.at[peer],
            dst_ref=gathered.at[me],
            send_sem=send_sems.at[peer],
            recv_sem=recv_sems.at[me],
            device_id={axis: peer},
            device_id_type=MESH,
        )
        copy.start()
        sends.append(copy)
    gathered[me] = x_ref[me]
    for k in range(1, n):
        peer = lax.rem(me + k, n)
        pltpu.make_async_remote_copy(
            src_ref=x_ref.at[peer],
            dst_ref=gathered.at[peer],
            send_sem=send_sems.at[peer],
            recv_sem=recv_sems.at[peer],
            device_id={axis: peer},
            device_id_type=MESH,
        ).wait_recv()
    for copy in sends:
        copy.wait_send()
    total = gathered[0]
    for k in range(1, n):
        total = total + gathered[k]
    summed[...] = total
    out_ref[me] = total
    shares = []
    for k in range(1, n):
        peer = lax.rem(me + k, n)
        copy = pltpu.make_async_remote_copy(
            src_ref=summed,
            dst_ref=out_ref.at[me],
            send_sem=out_send.at[peer],
            recv_sem=out_recv.at[me],
            device_id={axis: peer},
            device_id_type=MESH,
        )
        copy.start()
        shares.append(copy)
    for k in range(1, n):
        peer = lax.rem(me + k, n)
        pltpu.make_async_remote_copy(
            src_ref=summed,
            dst_ref=out_ref.at[peer],
            send_sem=out_send.at[peer],
            recv_sem=out_recv.at[peer],
            device_id={axis: peer},
            device_id_type=MESH,
        ).wait_recv()
    for copy in shares:
        copy.wait_send()


def all_reduce(x, axis):
    n = lax.axis_size(axis)
    shape = x.shape
    blocks = x.reshape(n, -1, 128)
    block_shape = blocks.shape[1:]
    out = pl.pallas_call(
        functools.partial(all_reduce_kernel, axis, n),
        out_shape=jax.ShapeDtypeStruct(blocks.shape, x.dtype),
        in_specs=[pl.BlockSpec(memory_space=pltpu.VMEM)],
        out_specs=pl.BlockSpec(memory_space=pltpu.VMEM),
        scratch_shapes=[
            pltpu.VMEM(blocks.shape, x.dtype),
            pltpu.VMEM(block_shape, x.dtype),
            pltpu.SemaphoreType.DMA((n,)),
            pltpu.SemaphoreType.DMA((n,)),
            pltpu.SemaphoreType.DMA((n,)),
            pltpu.SemaphoreType.DMA((n,)),
        ],
        compiler_params=pltpu.CompilerParams(collective_id=0, has_side_effects=True),
    )(blocks)
    return out.reshape(shape)


def grad_reduce_kernel(z_hi, scale, p_ref, out_ref, recv_c, s1b, recv_x, s2, recv_z, s3, recv_y, g16,
                       core_sems, x_send, x_recv, z_send, z_recv, y_send, y_recv, g_send, g_recv, pair_sems):
    n_x = recv_x.shape[0]
    n_z = 2 * z_hi
    n_y = recv_y.shape[0]
    band = recv_c.shape[1]
    half = s2.shape[1]
    width = recv_y.shape[2]
    f = lax.axis_index("fsdp")
    d = lax.axis_index("dp")
    c = lax.rem(f, 2)
    zh = lax.rem(f // 2, z_hi)
    x = f // (2 * z_hi)
    zl = lax.rem(d, 2)
    y = d // 2
    z = zh * 2 + zl

    def device(x_, zh_, c_, y_, zl_):
        return {"dp": y_ * 2 + zl_, "fsdp": (x_ * z_hi + zh_) * 2 + c_}

    partner = device(x, zh, 1 - c, y, zl)
    x_peers = [lax.rem(x + k, n_x) for k in range(1, n_x)]
    z_peers = [lax.rem(z + k, n_z) for k in range(1, n_z)]
    y_peers = [lax.rem(y + k, n_y) for k in range(1, n_y)]
    everyone = [partner]
    everyone += [device(xp, zh, c, y, zl) for xp in x_peers]
    everyone += [device(x, zp // 2, c, y, lax.rem(zp, 2)) for zp in z_peers]
    everyone += [device(x, zh, c, yp, zl) for yp in y_peers]
    barrier = pltpu.get_barrier_semaphore()
    for peer in everyone:
        pl.semaphore_signal(barrier, inc=1, device_id=peer, device_id_type=MESH)
    pl.semaphore_wait(barrier, len(everyone))

    def exchange(src_of, dst_of, send_sems, recv_sems, peers, mine, device_of):
        sends = []
        for p in peers:
            copy = pltpu.make_async_remote_copy(
                src_ref=src_of(p), dst_ref=dst_of(mine), send_sem=send_sems.at[p],
                recv_sem=recv_sems.at[mine], device_id=device_of(p), device_id_type=MESH)
            copy.start()
            sends.append(copy)
        for p in peers:
            pltpu.make_async_remote_copy(
                src_ref=src_of(p), dst_ref=dst_of(p), send_sem=send_sems.at[p],
                recv_sem=recv_sems.at[p], device_id=device_of(p), device_id_type=MESH).wait_recv()
        for copy in sends:
            copy.wait_send()

    core_copy = pltpu.make_async_remote_copy(
        src_ref=p_ref.at[1 - c], dst_ref=recv_c, send_sem=core_sems.at[0],
        recv_sem=core_sems.at[1], device_id=partner, device_id_type=MESH)
    core_copy.start()
    core_copy.wait()

    rows = 32
    chunks = band // rows

    def round_two_sums(i, carry):
        xi, r = i // chunks, lax.rem(i, chunks)
        at = pl.ds(pl.multiple_of(r * rows, rows), rows)
        both = p_ref[c, xi, at, :].astype(jnp.float32) + recv_c[xi, at, :].astype(jnp.float32)
        s1b[xi, at, :] = both.astype(s1b.dtype)
        return carry

    lax.fori_loop(0, n_x * chunks, round_two_sums, 0)
    exchange(lambda p: s1b.at[p], lambda p: recv_x.at[p], x_send, x_recv, x_peers, x,
             lambda p: device(p, zh, c, y, zl))

    def sum_x(j, carry):
        at = pl.ds(pl.multiple_of(j * half, half), half)
        total = p_ref[c, x, at, :].astype(jnp.float32) + recv_c[x, at, :].astype(jnp.float32)
        for p in x_peers:
            total = total + recv_x[p, at, :].astype(jnp.float32)
        s2[j] = total
        return carry

    lax.fori_loop(0, n_z, sum_x, 0)
    exchange(lambda p: s2.at[p], lambda p: recv_z.at[p], z_send, z_recv, z_peers, z,
             lambda p: device(x, p // 2, c, y, lax.rem(p, 2)))
    total = s2[z]
    for p in z_peers:
        total = total + recv_z[p]
    s3[...] = total

    def cols(p):
        return pl.ds(pl.multiple_of(p * width, 128), width)

    exchange(lambda p: s3.at[:, cols(p)], lambda p: recv_y.at[p], y_send, y_recv, y_peers, y,
             lambda p: device(x, zh, c, p, zl))
    total = s3[:, cols(y)]
    for p in y_peers:
        total = total + recv_y[p]
    g16[:, cols(y)] = total * scale
    exchange(lambda p: g16.at[:, cols(y)], lambda p: g16.at[:, cols(p)], g_send, g_recv, y_peers, y,
             lambda p: device(x, zh, c, p, zl))
    out_ref[zl] = g16[...]
    pair_copy = pltpu.make_async_remote_copy(
        src_ref=g16, dst_ref=out_ref.at[zl], send_sem=pair_sems.at[0], recv_sem=pair_sems.at[1],
        device_id=device(x, zh, c, y, 1 - zl), device_id_type=MESH)
    pair_copy.start()
    pltpu.make_async_remote_copy(
        src_ref=g16, dst_ref=out_ref.at[1 - zl], send_sem=pair_sems.at[0], recv_sem=pair_sems.at[1],
        device_id=device(x, zh, c, y, 1 - zl), device_id_type=MESH).wait_recv()
    pair_copy.wait_send()


def grad_reduce(partial_rows, z_hi, scale):
    n_x = partial_rows.shape[1]
    n_y = lax.axis_size("dp") // 2
    cols = partial_rows.shape[3]
    shard = partial_rows.shape[2] // z_hi
    half = shard // 2
    band = partial_rows.shape[2]
    f32 = jnp.float32
    return pl.pallas_call(
        functools.partial(grad_reduce_kernel, z_hi, scale),
        out_shape=jax.ShapeDtypeStruct((2, half, cols), f32),
        in_specs=[pl.BlockSpec(memory_space=pltpu.VMEM)],
        out_specs=pl.BlockSpec(memory_space=pltpu.VMEM),
        scratch_shapes=[
            pltpu.VMEM((n_x, band, cols), partial_rows.dtype),
            pltpu.VMEM((n_x, band, cols), partial_rows.dtype),
            pltpu.VMEM((n_x, band, cols), partial_rows.dtype),
            pltpu.VMEM((2 * z_hi, half, cols), f32),
            pltpu.VMEM((2 * z_hi, half, cols), f32),
            pltpu.VMEM((half, cols), f32),
            pltpu.VMEM((n_y, half, cols // n_y), f32),
            pltpu.VMEM((half, cols), f32),
            pltpu.SemaphoreType.DMA((2,)),
            pltpu.SemaphoreType.DMA((n_x,)),
            pltpu.SemaphoreType.DMA((n_x,)),
            pltpu.SemaphoreType.DMA((2 * z_hi,)),
            pltpu.SemaphoreType.DMA((2 * z_hi,)),
            pltpu.SemaphoreType.DMA((n_y,)),
            pltpu.SemaphoreType.DMA((n_y,)),
            pltpu.SemaphoreType.DMA((n_y,)),
            pltpu.SemaphoreType.DMA((n_y,)),
            pltpu.SemaphoreType.DMA((2,)),
        ],
        compiler_params=pltpu.CompilerParams(
            collective_id=1, has_side_effects=True, vmem_limit_bytes=48 * 1024 * 1024),
    )(partial_rows)


def tap_starts(context_row_block):
    return [context_row_block - (2 - selected_index) * DILATION_SIZE for selected_index in range(3)]


def per_device(signal, grad_gated, conv_weight, source_seg):
    peer_count = lax.axis_size("fsdp")
    seg_count = source_seg.shape[1]
    row_count = signal.shape[0]
    seg_rows = row_count // seg_count
    context_row_block = 2 * DILATION_SIZE
    starts = tap_starts(context_row_block)
    segments = signal.reshape(seg_count, seg_rows, C)
    sources = source_seg[0]
    source_dev = jnp.where(sources >= 0, sources // seg_count, -1)
    peers = jnp.arange(peer_count, dtype=jnp.int32)
    request_mask = (source_dev[None, :] == peers[:, None]).astype(jnp.int32)
    asked = lax.all_to_all(request_mask, "fsdp", split_axis=0, concat_axis=0, tiled=True)
    send_table = asked.astype(jnp.bfloat16)
    recv_table = (source_dev[:, None] == peers[None, :]).astype(jnp.bfloat16)
    outgoing = jnp.einsum(
        "ns,slc->nlc", send_table, segments, preferred_element_type=jnp.float32
    ).astype(jnp.bfloat16)
    incoming = lax.all_to_all(outgoing, "fsdp", split_axis=0, concat_axis=0, tiled=True)
    carries = jnp.einsum(
        "sn,nlc->slc", recv_table, incoming, preferred_element_type=jnp.float32
    ).astype(jnp.bfloat16)
    extended = jnp.concatenate([carries, segments], axis=1)
    full_weight = lax.all_gather(conv_weight, "fsdp", axis=0, tiled=True)
    contract_final_axis = (((1,), (1,)), ((), ()))
    contract_first = (((0,), (0,)), ((), ()))
    windows = [extended[:, start : start + seg_rows, :].reshape(row_count, C) for start in starts]
    preact = sum(
        (
            lax.dot_general(
                windows[selected_index],
                full_weight[:, selected_index * C : (selected_index + 1) * C],
                contract_final_axis,
                preferred_element_type=jnp.float32,
            )
            for selected_index in range(3)
        )
    )
    filter_act = jnp.tanh(preact[:, :H])
    gate_act = jax.nn.sigmoid(preact[:, H:])
    gated_out = (filter_act * gate_act).astype(jnp.bfloat16)
    upstream_wide = grad_gated.astype(jnp.float32)
    grad_pre = jnp.concatenate(
        [
            upstream_wide * gate_act * (1.0 - filter_act * filter_act),
            upstream_wide * filter_act * gate_act * (1.0 - gate_act),
        ],
        axis=1,
    ).astype(jnp.bfloat16)
    z_hi = Z_HI
    n_x = peer_count // (2 * z_hi)
    shard = conv_weight.shape[0]
    routed = (
        grad_pre.reshape(row_count, n_x, z_hi, 2, shard)
        .transpose(0, 3, 1, 2, 4)
        .reshape(row_count, 2 * H)
    )
    partial_value = jnp.concatenate(
        [
            lax.dot_general(
                routed,
                windows[selected_index],
                contract_first,
                preferred_element_type=jnp.float32,
            ).astype(jnp.bfloat16)
            for selected_index in range(3)
        ],
        axis=1,
    )
    total_token_count = row_count * peer_count * lax.axis_size("dp")
    reduced = grad_reduce(
        partial_value.reshape(2, n_x, z_hi * shard, 3 * C), z_hi, 1.0 / math.sqrt(total_token_count)
    )
    grad_weight = reduced.reshape(shard, 3 * C)
    back_proj = jnp.dot(grad_pre, full_weight, preferred_element_type=jnp.float32)
    back_proj = back_proj.reshape(seg_count, seg_rows, 3 * C)
    grad_ext = jnp.zeros((seg_count, context_row_block + seg_rows, C), jnp.float32)
    for selected_index, start in enumerate(starts):
        grad_ext = grad_ext.at[:, start : start + seg_rows, :].add(
            back_proj[:, :, selected_index * C : (selected_index + 1) * C]
        )
    outgoing_grad = jnp.einsum(
        "sn,slc->nlc",
        recv_table.astype(jnp.float32),
        grad_ext[:, :context_row_block, :],
        precision=lax.Precision.HIGHEST,
    )
    incoming_grad = lax.all_to_all(outgoing_grad, "fsdp", split_axis=0, concat_axis=0, tiled=True)
    tail_grad = jnp.einsum(
        "ns,nlc->slc",
        send_table.astype(jnp.float32),
        incoming_grad,
        precision=lax.Precision.HIGHEST,
    )
    grad_in = (
        grad_ext[:, context_row_block:, :].at[:, seg_rows - context_row_block :, :].add(tail_grad)
    )
    grad_in = grad_in.reshape(row_count, C).astype(jnp.bfloat16)
    return (gated_out, grad_in, grad_weight)


def solution(mesh):
    placed = (
        P(("dp", "fsdp"), None),
        P(("dp", "fsdp"), None),
        P("fsdp", None),
        P(("dp", "fsdp"), None),
    )
    return jax.shard_map(
        per_device,
        mesh=mesh,
        in_specs=placed,
        out_specs=(P(("dp", "fsdp"), None), P(("dp", "fsdp"), None), P("fsdp", None)),
        check_vma=False,
    )
```

```python
import functools
import math

import jax
import jax.numpy as jnp
from jax import lax
from jax.experimental import pallas as pl
from jax.experimental.pallas import tpu as pltpu
from jax.sharding import PartitionSpec as P

MESH = pl.DeviceIdType.MESH

C = 1024
H = 512
DILATION_SIZE = 4
Z_HI = 4


def all_reduce_kernel(axis, n, x_ref, out_ref, gathered, summed, send_sems, recv_sems, out_send, out_recv):
    me = lax.axis_index(axis)
    barrier = pltpu.get_barrier_semaphore()
    for k in range(1, n):
        peer = lax.rem(me + k, n)
        pl.semaphore_signal(barrier, inc=1, device_id={axis: peer}, device_id_type=MESH)
    pl.semaphore_wait(barrier, n - 1)
    sends = []
    for k in range(1, n):
        peer = lax.rem(me + k, n)
        copy = pltpu.make_async_remote_copy(
            src_ref=x_ref.at[peer],
            dst_ref=gathered.at[me],
            send_sem=send_sems.at[peer],
            recv_sem=recv_sems.at[me],
            device_id={axis: peer},
            device_id_type=MESH,
        )
        copy.start()
        sends.append(copy)
    gathered[me] = x_ref[me]
    for k in range(1, n):
        peer = lax.rem(me + k, n)
        pltpu.make_async_remote_copy(
            src_ref=x_ref.at[peer],
            dst_ref=gathered.at[peer],
            send_sem=send_sems.at[peer],
            recv_sem=recv_sems.at[peer],
            device_id={axis: peer},
            device_id_type=MESH,
        ).wait_recv()
    for copy in sends:
        copy.wait_send()
    total = gathered[0]
    for k in range(1, n):
        total = total + gathered[k]
    summed[...] = total
    out_ref[me] = total
    shares = []
    for k in range(1, n):
        peer = lax.rem(me + k, n)
        copy = pltpu.make_async_remote_copy(
            src_ref=summed,
            dst_ref=out_ref.at[me],
            send_sem=out_send.at[peer],
            recv_sem=out_recv.at[me],
            device_id={axis: peer},
            device_id_type=MESH,
        )
        copy.start()
        shares.append(copy)
    for k in range(1, n):
        peer = lax.rem(me + k, n)
        pltpu.make_async_remote_copy(
            src_ref=summed,
            dst_ref=out_ref.at[peer],
            send_sem=out_send.at[peer],
            recv_sem=out_recv.at[peer],
            device_id={axis: peer},
            device_id_type=MESH,
        ).wait_recv()
    for copy in shares:
        copy.wait_send()


def all_reduce(x, axis):
    n = lax.axis_size(axis)
    shape = x.shape
    blocks = x.reshape(n, -1, 128)
    block_shape = blocks.shape[1:]
    out = pl.pallas_call(
        functools.partial(all_reduce_kernel, axis, n),
        out_shape=jax.ShapeDtypeStruct(blocks.shape, x.dtype),
        in_specs=[pl.BlockSpec(memory_space=pltpu.VMEM)],
        out_specs=pl.BlockSpec(memory_space=pltpu.VMEM),
        scratch_shapes=[
            pltpu.VMEM(blocks.shape, x.dtype),
            pltpu.VMEM(block_shape, x.dtype),
            pltpu.SemaphoreType.DMA((n,)),
            pltpu.SemaphoreType.DMA((n,)),
            pltpu.SemaphoreType.DMA((n,)),
            pltpu.SemaphoreType.DMA((n,)),
        ],
        compiler_params=pltpu.CompilerParams(collective_id=0, has_side_effects=True),
    )(blocks)
    return out.reshape(shape)


def grad_reduce_kernel(z_hi, scale, p_ref, out_ref, recv_c, s1b, recv_x, s2, own, recv_z, s3, recv_y, g16,
                       core_sems, x_send, x_recv, z_send, z_recv, y_send, y_recv, g_send, g_recv, pair_sems):
    n_x = recv_x.shape[0]
    n_z = 2 * z_hi
    n_y = recv_y.shape[0]
    band = recv_c.shape[1]
    half = s2.shape[1]
    width = recv_y.shape[2]
    f = lax.axis_index("fsdp")
    d = lax.axis_index("dp")
    c = lax.rem(f, 2)
    zh = lax.rem(f // 2, z_hi)
    x = f // (2 * z_hi)
    zl = lax.rem(d, 2)
    y = d // 2
    z = zh * 2 + zl

    def device(x_, zh_, c_, y_, zl_):
        return {"dp": y_ * 2 + zl_, "fsdp": (x_ * z_hi + zh_) * 2 + c_}

    partner = device(x, zh, 1 - c, y, zl)
    x_peers = [lax.rem(x + k, n_x) for k in range(1, n_x)]
    z_peers = [lax.rem(z + k, n_z) for k in range(1, n_z)]
    y_peers = [lax.rem(y + k, n_y) for k in range(1, n_y)]
    everyone = [partner]
    everyone += [device(xp, zh, c, y, zl) for xp in x_peers]
    everyone += [device(x, zp // 2, c, y, lax.rem(zp, 2)) for zp in z_peers]
    everyone += [device(x, zh, c, yp, zl) for yp in y_peers]
    barrier = pltpu.get_barrier_semaphore()
    for peer in everyone:
        pl.semaphore_signal(barrier, inc=1, device_id=peer, device_id_type=MESH)
    pl.semaphore_wait(barrier, len(everyone))

    def exchange(src_of, dst_of, send_sems, recv_sems, peers, mine, device_of):
        sends = []
        for p in peers:
            copy = pltpu.make_async_remote_copy(
                src_ref=src_of(p), dst_ref=dst_of(mine), send_sem=send_sems.at[p],
                recv_sem=recv_sems.at[mine], device_id=device_of(p), device_id_type=MESH)
            copy.start()
            sends.append(copy)
        for p in peers:
            pltpu.make_async_remote_copy(
                src_ref=src_of(p), dst_ref=dst_of(p), send_sem=send_sems.at[p],
                recv_sem=recv_sems.at[p], device_id=device_of(p), device_id_type=MESH).wait_recv()
        for copy in sends:
            copy.wait_send()

    core_copy = pltpu.make_async_remote_copy(
        src_ref=p_ref.at[1 - c], dst_ref=recv_c, send_sem=core_sems.at[0],
        recv_sem=core_sems.at[1], device_id=partner, device_id_type=MESH)
    core_copy.start()
    core_copy.wait()

    rows = 32
    chunks = band // rows

    def round_two_sums(i, carry):
        xi, r = i // chunks, lax.rem(i, chunks)
        at = pl.ds(pl.multiple_of(r * rows, rows), rows)
        both = p_ref[c, xi, at, :].astype(jnp.float32) + recv_c[xi, at, :].astype(jnp.float32)
        s1b[xi, at, :] = both.astype(s1b.dtype)
        return carry

    lax.fori_loop(0, n_x * chunks, round_two_sums, 0)
    exchange(lambda p: s1b.at[p], lambda p: recv_x.at[p], x_send, x_recv, x_peers, x,
             lambda p: device(p, zh, c, y, zl))

    def sum_x(j, carry):
        at = pl.ds(pl.multiple_of(j * half, half), half)
        total = p_ref[c, x, at, :].astype(jnp.float32) + recv_c[x, at, :].astype(jnp.float32)
        for p in x_peers:
            total = total + recv_x[p, at, :].astype(jnp.float32)
        s2[j] = total.astype(s2.dtype)
        own[j] = total
        return carry

    lax.fori_loop(0, n_z, sum_x, 0)
    exchange(lambda p: s2.at[p], lambda p: recv_z.at[p], z_send, z_recv, z_peers, z,
             lambda p: device(x, p // 2, c, y, lax.rem(p, 2)))
    total = own[z]
    for p in z_peers:
        total = total + recv_z[p].astype(jnp.float32)
    s3[...] = total

    def cols(p):
        return pl.ds(pl.multiple_of(p * width, 128), width)

    exchange(lambda p: s3.at[:, cols(p)], lambda p: recv_y.at[p], y_send, y_recv, y_peers, y,
             lambda p: device(x, zh, c, p, zl))
    total = s3[:, cols(y)]
    for p in y_peers:
        total = total + recv_y[p]
    g16[:, cols(y)] = total * scale
    exchange(lambda p: g16.at[:, cols(y)], lambda p: g16.at[:, cols(p)], g_send, g_recv, y_peers, y,
             lambda p: device(x, zh, c, p, zl))
    out_ref[zl] = g16[...]
    pair_copy = pltpu.make_async_remote_copy(
        src_ref=g16, dst_ref=out_ref.at[zl], send_sem=pair_sems.at[0], recv_sem=pair_sems.at[1],
        device_id=device(x, zh, c, y, 1 - zl), device_id_type=MESH)
    pair_copy.start()
    pltpu.make_async_remote_copy(
        src_ref=g16, dst_ref=out_ref.at[1 - zl], send_sem=pair_sems.at[0], recv_sem=pair_sems.at[1],
        device_id=device(x, zh, c, y, 1 - zl), device_id_type=MESH).wait_recv()
    pair_copy.wait_send()


def grad_reduce(partial_rows, z_hi, scale):
    n_x = partial_rows.shape[1]
    n_y = lax.axis_size("dp") // 2
    cols = partial_rows.shape[3]
    shard = partial_rows.shape[2] // z_hi
    half = shard // 2
    band = partial_rows.shape[2]
    f32 = jnp.float32
    return pl.pallas_call(
        functools.partial(grad_reduce_kernel, z_hi, scale),
        out_shape=jax.ShapeDtypeStruct((2, half, cols), f32),
        in_specs=[pl.BlockSpec(memory_space=pltpu.VMEM)],
        out_specs=pl.BlockSpec(memory_space=pltpu.VMEM),
        scratch_shapes=[
            pltpu.VMEM((n_x, band, cols), partial_rows.dtype),
            pltpu.VMEM((n_x, band, cols), partial_rows.dtype),
            pltpu.VMEM((n_x, band, cols), partial_rows.dtype),
            pltpu.VMEM((2 * z_hi, half, cols), partial_rows.dtype),
            pltpu.VMEM((2 * z_hi, half, cols), f32),
            pltpu.VMEM((2 * z_hi, half, cols), partial_rows.dtype),
            pltpu.VMEM((half, cols), f32),
            pltpu.VMEM((n_y, half, cols // n_y), f32),
            pltpu.VMEM((half, cols), f32),
            pltpu.SemaphoreType.DMA((2,)),
            pltpu.SemaphoreType.DMA((n_x,)),
            pltpu.SemaphoreType.DMA((n_x,)),
            pltpu.SemaphoreType.DMA((2 * z_hi,)),
            pltpu.SemaphoreType.DMA((2 * z_hi,)),
            pltpu.SemaphoreType.DMA((n_y,)),
            pltpu.SemaphoreType.DMA((n_y,)),
            pltpu.SemaphoreType.DMA((n_y,)),
            pltpu.SemaphoreType.DMA((n_y,)),
            pltpu.SemaphoreType.DMA((2,)),
        ],
        compiler_params=pltpu.CompilerParams(
            collective_id=1, has_side_effects=True, vmem_limit_bytes=48 * 1024 * 1024),
    )(partial_rows)


def tap_starts(context_row_block):
    return [context_row_block - (2 - selected_index) * DILATION_SIZE for selected_index in range(3)]


def per_device(signal, grad_gated, conv_weight, source_seg):
    peer_count = lax.axis_size("fsdp")
    seg_count = source_seg.shape[1]
    row_count = signal.shape[0]
    seg_rows = row_count // seg_count
    context_row_block = 2 * DILATION_SIZE
    starts = tap_starts(context_row_block)
    segments = signal.reshape(seg_count, seg_rows, C)
    sources = source_seg[0]
    source_dev = jnp.where(sources >= 0, sources // seg_count, -1)
    peers = jnp.arange(peer_count, dtype=jnp.int32)
    request_mask = (source_dev[None, :] == peers[:, None]).astype(jnp.int32)
    asked = lax.all_to_all(request_mask, "fsdp", split_axis=0, concat_axis=0, tiled=True)
    send_table = asked.astype(jnp.bfloat16)
    recv_table = (source_dev[:, None] == peers[None, :]).astype(jnp.bfloat16)
    outgoing = jnp.einsum(
        "ns,slc->nlc", send_table, segments, preferred_element_type=jnp.float32
    ).astype(jnp.bfloat16)
    incoming = lax.all_to_all(outgoing, "fsdp", split_axis=0, concat_axis=0, tiled=True)
    carries = jnp.einsum(
        "sn,nlc->slc", recv_table, incoming, preferred_element_type=jnp.float32
    ).astype(jnp.bfloat16)
    extended = jnp.concatenate([carries, segments], axis=1)
    full_weight = lax.all_gather(conv_weight, "fsdp", axis=0, tiled=True)
    contract_final_axis = (((1,), (1,)), ((), ()))
    contract_first = (((0,), (0,)), ((), ()))
    windows = [extended[:, start : start + seg_rows, :].reshape(row_count, C) for start in starts]
    preact = sum(
        (
            lax.dot_general(
                windows[selected_index],
                full_weight[:, selected_index * C : (selected_index + 1) * C],
                contract_final_axis,
                preferred_element_type=jnp.float32,
            )
            for selected_index in range(3)
        )
    )
    filter_act = jnp.tanh(preact[:, :H])
    gate_act = jax.nn.sigmoid(preact[:, H:])
    gated_out = (filter_act * gate_act).astype(jnp.bfloat16)
    upstream_wide = grad_gated.astype(jnp.float32)
    grad_pre = jnp.concatenate(
        [
            upstream_wide * gate_act * (1.0 - filter_act * filter_act),
            upstream_wide * filter_act * gate_act * (1.0 - gate_act),
        ],
        axis=1,
    ).astype(jnp.bfloat16)
    z_hi = Z_HI
    n_x = peer_count // (2 * z_hi)
    shard = conv_weight.shape[0]
    routed = (
        grad_pre.reshape(row_count, n_x, z_hi, 2, shard)
        .transpose(0, 3, 1, 2, 4)
        .reshape(row_count, 2 * H)
    )
    stacked = jnp.concatenate(windows, axis=1)
    partial_value = lax.dot_general(
        routed, stacked, contract_first, preferred_element_type=jnp.float32
    ).astype(jnp.bfloat16)
    total_token_count = row_count * peer_count * lax.axis_size("dp")
    reduced = grad_reduce(
        partial_value.reshape(2, n_x, z_hi * shard, 3 * C), z_hi, 1.0 / math.sqrt(total_token_count)
    )
    grad_weight = reduced.reshape(shard, 3 * C)
    back_proj = jnp.dot(grad_pre, full_weight, preferred_element_type=jnp.float32)
    back_proj = back_proj.reshape(seg_count, seg_rows, 3 * C)
    grad_ext = jnp.zeros((seg_count, context_row_block + seg_rows, C), jnp.float32)
    for selected_index, start in enumerate(starts):
        grad_ext = grad_ext.at[:, start : start + seg_rows, :].add(
            back_proj[:, :, selected_index * C : (selected_index + 1) * C]
        )
    outgoing_grad = jnp.einsum(
        "sn,slc->nlc",
        recv_table.astype(jnp.float32),
        grad_ext[:, :context_row_block, :],
        precision=lax.Precision.HIGHEST,
    )
    incoming_grad = lax.all_to_all(outgoing_grad, "fsdp", split_axis=0, concat_axis=0, tiled=True)
    tail_grad = jnp.einsum(
        "ns,nlc->slc",
        send_table.astype(jnp.float32),
        incoming_grad,
        precision=lax.Precision.HIGHEST,
    )
    grad_in = (
        grad_ext[:, context_row_block:, :].at[:, seg_rows - context_row_block :, :].add(tail_grad)
    )
    grad_in = grad_in.reshape(row_count, C).astype(jnp.bfloat16)
    return (gated_out, grad_in, grad_weight)


def solution(mesh):
    placed = (
        P(("dp", "fsdp"), None),
        P(("dp", "fsdp"), None),
        P("fsdp", None),
        P(("dp", "fsdp"), None),
    )
    return jax.shard_map(
        per_device,
        mesh=mesh,
        in_specs=placed,
        out_specs=(P(("dp", "fsdp"), None), P(("dp", "fsdp"), None), P("fsdp", None)),
        check_vma=False,
    )
```

```python
import functools
import math

import jax
import jax.numpy as jnp
from jax import lax
from jax.experimental import pallas as pl
from jax.experimental.pallas import tpu as pltpu
from jax.sharding import PartitionSpec as P

MESH = pl.DeviceIdType.MESH

C = 1024
H = 512
DILATION_SIZE = 4
Z_HI = 4


def all_reduce_kernel(axis, n, x_ref, out_ref, gathered, summed, send_sems, recv_sems, out_send, out_recv):
    me = lax.axis_index(axis)
    barrier = pltpu.get_barrier_semaphore()
    for k in range(1, n):
        peer = lax.rem(me + k, n)
        pl.semaphore_signal(barrier, inc=1, device_id={axis: peer}, device_id_type=MESH)
    pl.semaphore_wait(barrier, n - 1)
    sends = []
    for k in range(1, n):
        peer = lax.rem(me + k, n)
        copy = pltpu.make_async_remote_copy(
            src_ref=x_ref.at[peer],
            dst_ref=gathered.at[me],
            send_sem=send_sems.at[peer],
            recv_sem=recv_sems.at[me],
            device_id={axis: peer},
            device_id_type=MESH,
        )
        copy.start()
        sends.append(copy)
    gathered[me] = x_ref[me]
    for k in range(1, n):
        peer = lax.rem(me + k, n)
        pltpu.make_async_remote_copy(
            src_ref=x_ref.at[peer],
            dst_ref=gathered.at[peer],
            send_sem=send_sems.at[peer],
            recv_sem=recv_sems.at[peer],
            device_id={axis: peer},
            device_id_type=MESH,
        ).wait_recv()
    for copy in sends:
        copy.wait_send()
    total = gathered[0]
    for k in range(1, n):
        total = total + gathered[k]
    summed[...] = total
    out_ref[me] = total
    shares = []
    for k in range(1, n):
        peer = lax.rem(me + k, n)
        copy = pltpu.make_async_remote_copy(
            src_ref=summed,
            dst_ref=out_ref.at[me],
            send_sem=out_send.at[peer],
            recv_sem=out_recv.at[me],
            device_id={axis: peer},
            device_id_type=MESH,
        )
        copy.start()
        shares.append(copy)
    for k in range(1, n):
        peer = lax.rem(me + k, n)
        pltpu.make_async_remote_copy(
            src_ref=summed,
            dst_ref=out_ref.at[peer],
            send_sem=out_send.at[peer],
            recv_sem=out_recv.at[peer],
            device_id={axis: peer},
            device_id_type=MESH,
        ).wait_recv()
    for copy in shares:
        copy.wait_send()


def all_reduce(x, axis):
    n = lax.axis_size(axis)
    shape = x.shape
    blocks = x.reshape(n, -1, 128)
    block_shape = blocks.shape[1:]
    out = pl.pallas_call(
        functools.partial(all_reduce_kernel, axis, n),
        out_shape=jax.ShapeDtypeStruct(blocks.shape, x.dtype),
        in_specs=[pl.BlockSpec(memory_space=pltpu.VMEM)],
        out_specs=pl.BlockSpec(memory_space=pltpu.VMEM),
        scratch_shapes=[
            pltpu.VMEM(blocks.shape, x.dtype),
            pltpu.VMEM(block_shape, x.dtype),
            pltpu.SemaphoreType.DMA((n,)),
            pltpu.SemaphoreType.DMA((n,)),
            pltpu.SemaphoreType.DMA((n,)),
            pltpu.SemaphoreType.DMA((n,)),
        ],
        compiler_params=pltpu.CompilerParams(collective_id=0, has_side_effects=True),
    )(blocks)
    return out.reshape(shape)


def grad_reduce_kernel(z_hi, scale, p_ref, out_ref, recv_c, s1b, recv_x, s2, own, recv_z, s3, recv_y, g16,
                       core_sems, x_send, x_recv, z_send, z_recv, y_send, y_recv, g_send, g_recv, pair_sems,
                       relay, relay_sems):
    n_x = recv_x.shape[0]
    n_z = 2 * z_hi
    n_y = recv_y.shape[0]
    band = recv_c.shape[1]
    half = s2.shape[1]
    width = recv_y.shape[2]
    f = lax.axis_index("fsdp")
    d = lax.axis_index("dp")
    c = lax.rem(f, 2)
    zh = lax.rem(f // 2, z_hi)
    x = f // (2 * z_hi)
    zl = lax.rem(d, 2)
    y = d // 2
    z = zh * 2 + zl

    def device(x_, zh_, c_, y_, zl_):
        return {"dp": y_ * 2 + zl_, "fsdp": (x_ * z_hi + zh_) * 2 + c_}

    partner = device(x, zh, 1 - c, y, zl)
    x_peers = [lax.rem(x + k, n_x) for k in range(1, n_x)]
    z_peers = [lax.rem(z + k, n_z) for k in range(1, n_z)]
    y_peers = [lax.rem(y + k, n_y) for k in range(1, n_y)]
    everyone = [partner]
    everyone += [device(xp, zh, c, y, zl) for xp in x_peers]
    everyone += [device(x, zp // 2, c, y, lax.rem(zp, 2)) for zp in z_peers]
    everyone += [device(x, zh, c, yp, zl) for yp in y_peers]
    barrier = pltpu.get_barrier_semaphore()
    for peer in everyone:
        pl.semaphore_signal(barrier, inc=1, device_id=peer, device_id_type=MESH)
    pl.semaphore_wait(barrier, len(everyone))

    def exchange(src_of, dst_of, send_sems, recv_sems, peers, mine, device_of):
        sends = []
        for p in peers:
            copy = pltpu.make_async_remote_copy(
                src_ref=src_of(p), dst_ref=dst_of(mine), send_sem=send_sems.at[p],
                recv_sem=recv_sems.at[mine], device_id=device_of(p), device_id_type=MESH)
            copy.start()
            sends.append(copy)
        for p in peers:
            pltpu.make_async_remote_copy(
                src_ref=src_of(p), dst_ref=dst_of(p), send_sem=send_sems.at[p],
                recv_sem=recv_sems.at[p], device_id=device_of(p), device_id_type=MESH).wait_recv()
        for copy in sends:
            copy.wait_send()

    core_copy = pltpu.make_async_remote_copy(
        src_ref=p_ref.at[1 - c], dst_ref=recv_c, send_sem=core_sems.at[0],
        recv_sem=core_sems.at[1], device_id=partner, device_id_type=MESH)
    core_copy.start()
    core_copy.wait()

    rows = 32
    chunks = band // rows

    def round_two_sums(i, carry):
        xi, r = i // chunks, lax.rem(i, chunks)
        at = pl.ds(pl.multiple_of(r * rows, rows), rows)
        both = p_ref[c, xi, at, :].astype(jnp.float32) + recv_c[xi, at, :].astype(jnp.float32)
        s1b[xi, at, :] = both.astype(s1b.dtype)
        return carry

    lax.fori_loop(0, n_x * chunks, round_two_sums, 0)
    if n_x == 4:
        right, across, left = x_peers
        split = band // 2
        head, tail = pl.ds(0, split), pl.ds(split, split)
        sends = []
        for p in (right, left):
            copy = pltpu.make_async_remote_copy(
                src_ref=s1b.at[p], dst_ref=recv_x.at[x], send_sem=x_send.at[p],
                recv_sem=x_recv.at[x], device_id=device(p, zh, c, y, zl), device_id_type=MESH)
            copy.start()
            sends.append(copy)
        for slot, (p, rows_) in enumerate(((right, head), (left, tail))):
            copy = pltpu.make_async_remote_copy(
                src_ref=s1b.at[across, rows_], dst_ref=relay.at[slot], send_sem=relay_sems.at[0, slot],
                recv_sem=relay_sems.at[1, slot], device_id=device(p, zh, c, y, zl), device_id_type=MESH)
            copy.start()
            sends.append(copy)
        for slot, (p, q, rows_) in enumerate(((right, left, head), (left, right, tail))):
            pltpu.make_async_remote_copy(
                src_ref=s1b.at[across, rows_], dst_ref=relay.at[slot], send_sem=relay_sems.at[0, slot],
                recv_sem=relay_sems.at[1, slot], device_id=device(p, zh, c, y, zl),
                device_id_type=MESH).wait_recv()
            copy = pltpu.make_async_remote_copy(
                src_ref=relay.at[slot], dst_ref=recv_x.at[q, rows_], send_sem=relay_sems.at[2, slot],
                recv_sem=relay_sems.at[3, slot], device_id=device(p, zh, c, y, zl), device_id_type=MESH)
            copy.start()
            sends.append(copy)
        for p in (right, left):
            pltpu.make_async_remote_copy(
                src_ref=s1b.at[p], dst_ref=recv_x.at[p], send_sem=x_send.at[p],
                recv_sem=x_recv.at[p], device_id=device(p, zh, c, y, zl), device_id_type=MESH).wait_recv()
        for slot, rows_ in enumerate((head, tail)):
            pltpu.make_async_remote_copy(
                src_ref=relay.at[slot], dst_ref=recv_x.at[across, rows_], send_sem=relay_sems.at[2, slot],
                recv_sem=relay_sems.at[3, slot], device_id=device(across, zh, c, y, zl),
                device_id_type=MESH).wait_recv()
        for copy in sends:
            copy.wait_send()
    else:
        exchange(lambda p: s1b.at[p], lambda p: recv_x.at[p], x_send, x_recv, x_peers, x,
                 lambda p: device(p, zh, c, y, zl))

    def sum_x(j, carry):
        at = pl.ds(pl.multiple_of(j * half, half), half)
        total = p_ref[c, x, at, :].astype(jnp.float32) + recv_c[x, at, :].astype(jnp.float32)
        for p in x_peers:
            total = total + recv_x[p, at, :].astype(jnp.float32)
        s2[j] = total.astype(s2.dtype)
        own[j] = total
        return carry

    lax.fori_loop(0, n_z, sum_x, 0)
    exchange(lambda p: s2.at[p], lambda p: recv_z.at[p], z_send, z_recv, z_peers, z,
             lambda p: device(x, p // 2, c, y, lax.rem(p, 2)))
    total = own[z]
    for p in z_peers:
        total = total + recv_z[p].astype(jnp.float32)
    s3[...] = total

    def cols(p):
        return pl.ds(pl.multiple_of(p * width, 128), width)

    exchange(lambda p: s3.at[:, cols(p)], lambda p: recv_y.at[p], y_send, y_recv, y_peers, y,
             lambda p: device(x, zh, c, p, zl))
    total = s3[:, cols(y)]
    for p in y_peers:
        total = total + recv_y[p]
    g16[:, cols(y)] = total * scale
    exchange(lambda p: g16.at[:, cols(y)], lambda p: g16.at[:, cols(p)], g_send, g_recv, y_peers, y,
             lambda p: device(x, zh, c, p, zl))
    out_ref[zl] = g16[...]
    pair_copy = pltpu.make_async_remote_copy(
        src_ref=g16, dst_ref=out_ref.at[zl], send_sem=pair_sems.at[0], recv_sem=pair_sems.at[1],
        device_id=device(x, zh, c, y, 1 - zl), device_id_type=MESH)
    pair_copy.start()
    pltpu.make_async_remote_copy(
        src_ref=g16, dst_ref=out_ref.at[1 - zl], send_sem=pair_sems.at[0], recv_sem=pair_sems.at[1],
        device_id=device(x, zh, c, y, 1 - zl), device_id_type=MESH).wait_recv()
    pair_copy.wait_send()


def grad_reduce(partial_rows, z_hi, scale):
    n_x = partial_rows.shape[1]
    n_y = lax.axis_size("dp") // 2
    cols = partial_rows.shape[3]
    shard = partial_rows.shape[2] // z_hi
    half = shard // 2
    band = partial_rows.shape[2]
    f32 = jnp.float32
    return pl.pallas_call(
        functools.partial(grad_reduce_kernel, z_hi, scale),
        out_shape=jax.ShapeDtypeStruct((2, half, cols), f32),
        in_specs=[pl.BlockSpec(memory_space=pltpu.VMEM)],
        out_specs=pl.BlockSpec(memory_space=pltpu.VMEM),
        scratch_shapes=[
            pltpu.VMEM((n_x, band, cols), partial_rows.dtype),
            pltpu.VMEM((n_x, band, cols), partial_rows.dtype),
            pltpu.VMEM((n_x, band, cols), partial_rows.dtype),
            pltpu.VMEM((2 * z_hi, half, cols), partial_rows.dtype),
            pltpu.VMEM((2 * z_hi, half, cols), f32),
            pltpu.VMEM((2 * z_hi, half, cols), partial_rows.dtype),
            pltpu.VMEM((half, cols), f32),
            pltpu.VMEM((n_y, half, cols // n_y), f32),
            pltpu.VMEM((half, cols), f32),
            pltpu.SemaphoreType.DMA((2,)),
            pltpu.SemaphoreType.DMA((n_x,)),
            pltpu.SemaphoreType.DMA((n_x,)),
            pltpu.SemaphoreType.DMA((2 * z_hi,)),
            pltpu.SemaphoreType.DMA((2 * z_hi,)),
            pltpu.SemaphoreType.DMA((n_y,)),
            pltpu.SemaphoreType.DMA((n_y,)),
            pltpu.SemaphoreType.DMA((n_y,)),
            pltpu.SemaphoreType.DMA((n_y,)),
            pltpu.SemaphoreType.DMA((2,)),
            pltpu.VMEM((2, band // 2, cols), partial_rows.dtype),
            pltpu.SemaphoreType.DMA((4, 2)),
        ],
        compiler_params=pltpu.CompilerParams(
            collective_id=1, has_side_effects=True, vmem_limit_bytes=48 * 1024 * 1024),
    )(partial_rows)


def tap_starts(context_row_block):
    return [context_row_block - (2 - selected_index) * DILATION_SIZE for selected_index in range(3)]


def per_device(signal, grad_gated, conv_weight, source_seg):
    peer_count = lax.axis_size("fsdp")
    seg_count = source_seg.shape[1]
    row_count = signal.shape[0]
    seg_rows = row_count // seg_count
    context_row_block = 2 * DILATION_SIZE
    starts = tap_starts(context_row_block)
    segments = signal.reshape(seg_count, seg_rows, C)
    sources = source_seg[0]
    source_dev = jnp.where(sources >= 0, sources // seg_count, -1)
    peers = jnp.arange(peer_count, dtype=jnp.int32)
    request_mask = (source_dev[None, :] == peers[:, None]).astype(jnp.int32)
    asked = lax.all_to_all(request_mask, "fsdp", split_axis=0, concat_axis=0, tiled=True)
    send_table = asked.astype(jnp.bfloat16)
    recv_table = (source_dev[:, None] == peers[None, :]).astype(jnp.bfloat16)
    outgoing = jnp.einsum(
        "ns,slc->nlc", send_table, segments, preferred_element_type=jnp.float32
    ).astype(jnp.bfloat16)
    incoming = lax.all_to_all(outgoing, "fsdp", split_axis=0, concat_axis=0, tiled=True)
    carries = jnp.einsum(
        "sn,nlc->slc", recv_table, incoming, preferred_element_type=jnp.float32
    ).astype(jnp.bfloat16)
    extended = jnp.concatenate([carries, segments], axis=1)
    full_weight = lax.all_gather(conv_weight, "fsdp", axis=0, tiled=True)
    contract_final_axis = (((1,), (1,)), ((), ()))
    contract_first = (((0,), (0,)), ((), ()))
    windows = [extended[:, start : start + seg_rows, :].reshape(row_count, C) for start in starts]
    preact = sum(
        (
            lax.dot_general(
                windows[selected_index],
                full_weight[:, selected_index * C : (selected_index + 1) * C],
                contract_final_axis,
                preferred_element_type=jnp.float32,
            )
            for selected_index in range(3)
        )
    )
    filter_act = jnp.tanh(preact[:, :H])
    gate_act = jax.nn.sigmoid(preact[:, H:])
    gated_out = (filter_act * gate_act).astype(jnp.bfloat16)
    upstream_wide = grad_gated.astype(jnp.float32)
    grad_pre = jnp.concatenate(
        [
            upstream_wide * gate_act * (1.0 - filter_act * filter_act),
            upstream_wide * filter_act * gate_act * (1.0 - gate_act),
        ],
        axis=1,
    ).astype(jnp.bfloat16)
    z_hi = Z_HI
    n_x = peer_count // (2 * z_hi)
    shard = conv_weight.shape[0]
    routed = (
        grad_pre.reshape(row_count, n_x, z_hi, 2, shard)
        .transpose(0, 3, 1, 2, 4)
        .reshape(row_count, 2 * H)
    )
    stacked = jnp.concatenate(windows, axis=1)
    partial_value = lax.dot_general(
        routed, stacked, contract_first, preferred_element_type=jnp.float32
    ).astype(jnp.bfloat16)
    total_token_count = row_count * peer_count * lax.axis_size("dp")
    reduced = grad_reduce(
        partial_value.reshape(2, n_x, z_hi * shard, 3 * C), z_hi, 1.0 / math.sqrt(total_token_count)
    )
    grad_weight = reduced.reshape(shard, 3 * C)
    back_proj = jnp.dot(grad_pre, full_weight, preferred_element_type=jnp.float32)
    back_proj = back_proj.reshape(seg_count, seg_rows, 3 * C)
    grad_ext = jnp.zeros((seg_count, context_row_block + seg_rows, C), jnp.float32)
    for selected_index, start in enumerate(starts):
        grad_ext = grad_ext.at[:, start : start + seg_rows, :].add(
            back_proj[:, :, selected_index * C : (selected_index + 1) * C]
        )
    outgoing_grad = jnp.einsum(
        "sn,slc->nlc",
        recv_table.astype(jnp.float32),
        grad_ext[:, :context_row_block, :],
        precision=lax.Precision.HIGHEST,
    )
    incoming_grad = lax.all_to_all(outgoing_grad, "fsdp", split_axis=0, concat_axis=0, tiled=True)
    tail_grad = jnp.einsum(
        "ns,nlc->slc",
        send_table.astype(jnp.float32),
        incoming_grad,
        precision=lax.Precision.HIGHEST,
    )
    grad_in = (
        grad_ext[:, context_row_block:, :].at[:, seg_rows - context_row_block :, :].add(tail_grad)
    )
    grad_in = grad_in.reshape(row_count, C).astype(jnp.bfloat16)
    return (gated_out, grad_in, grad_weight)


def solution(mesh):
    placed = (
        P(("dp", "fsdp"), None),
        P(("dp", "fsdp"), None),
        P("fsdp", None),
        P(("dp", "fsdp"), None),
    )
    return jax.shard_map(
        per_device,
        mesh=mesh,
        in_specs=placed,
        out_specs=(P(("dp", "fsdp"), None), P(("dp", "fsdp"), None), P("fsdp", None)),
        check_vma=False,
    )
```

```python
import functools
import math

import jax
import jax.numpy as jnp
from jax import lax
from jax.experimental import pallas as pl
from jax.experimental.pallas import tpu as pltpu
from jax.sharding import PartitionSpec as P

MESH = pl.DeviceIdType.MESH

C = 1024
H = 512
DILATION_SIZE = 4
Z_HI = 4
PIECES = 2


def all_reduce_kernel(axis, n, x_ref, out_ref, gathered, summed, send_sems, recv_sems, out_send, out_recv):
    me = lax.axis_index(axis)
    barrier = pltpu.get_barrier_semaphore()
    for k in range(1, n):
        peer = lax.rem(me + k, n)
        pl.semaphore_signal(barrier, inc=1, device_id={axis: peer}, device_id_type=MESH)
    pl.semaphore_wait(barrier, n - 1)
    sends = []
    for k in range(1, n):
        peer = lax.rem(me + k, n)
        copy = pltpu.make_async_remote_copy(
            src_ref=x_ref.at[peer],
            dst_ref=gathered.at[me],
            send_sem=send_sems.at[peer],
            recv_sem=recv_sems.at[me],
            device_id={axis: peer},
            device_id_type=MESH,
        )
        copy.start()
        sends.append(copy)
    gathered[me] = x_ref[me]
    for k in range(1, n):
        peer = lax.rem(me + k, n)
        pltpu.make_async_remote_copy(
            src_ref=x_ref.at[peer],
            dst_ref=gathered.at[peer],
            send_sem=send_sems.at[peer],
            recv_sem=recv_sems.at[peer],
            device_id={axis: peer},
            device_id_type=MESH,
        ).wait_recv()
    for copy in sends:
        copy.wait_send()
    total = gathered[0]
    for k in range(1, n):
        total = total + gathered[k]
    summed[...] = total
    out_ref[me] = total
    shares = []
    for k in range(1, n):
        peer = lax.rem(me + k, n)
        copy = pltpu.make_async_remote_copy(
            src_ref=summed,
            dst_ref=out_ref.at[me],
            send_sem=out_send.at[peer],
            recv_sem=out_recv.at[me],
            device_id={axis: peer},
            device_id_type=MESH,
        )
        copy.start()
        shares.append(copy)
    for k in range(1, n):
        peer = lax.rem(me + k, n)
        pltpu.make_async_remote_copy(
            src_ref=summed,
            dst_ref=out_ref.at[peer],
            send_sem=out_send.at[peer],
            recv_sem=out_recv.at[peer],
            device_id={axis: peer},
            device_id_type=MESH,
        ).wait_recv()
    for copy in shares:
        copy.wait_send()


def all_reduce(x, axis):
    n = lax.axis_size(axis)
    shape = x.shape
    blocks = x.reshape(n, -1, 128)
    block_shape = blocks.shape[1:]
    out = pl.pallas_call(
        functools.partial(all_reduce_kernel, axis, n),
        out_shape=jax.ShapeDtypeStruct(blocks.shape, x.dtype),
        in_specs=[pl.BlockSpec(memory_space=pltpu.VMEM)],
        out_specs=pl.BlockSpec(memory_space=pltpu.VMEM),
        scratch_shapes=[
            pltpu.VMEM(blocks.shape, x.dtype),
            pltpu.VMEM(block_shape, x.dtype),
            pltpu.SemaphoreType.DMA((n,)),
            pltpu.SemaphoreType.DMA((n,)),
            pltpu.SemaphoreType.DMA((n,)),
            pltpu.SemaphoreType.DMA((n,)),
        ],
        compiler_params=pltpu.CompilerParams(collective_id=0, has_side_effects=True),
    )(blocks)
    return out.reshape(shape)


def grad_reduce_kernel(z_hi, scale, p_ref, out_ref, recv_c, s1b, recv_x, s2, own, recv_z, s3, recv_y, g16,
                       core_sems, x_send, x_recv, z_send, z_recv, y_send, y_recv, g_send, g_recv, pair_sems):
    n_x = recv_x.shape[0]
    n_z = 2 * z_hi
    n_y = recv_y.shape[0]
    band = recv_c.shape[1]
    half = s2.shape[1]
    width = recv_y.shape[2]
    f = lax.axis_index("fsdp")
    d = lax.axis_index("dp")
    c = lax.rem(f, 2)
    zh = lax.rem(f // 2, z_hi)
    x = f // (2 * z_hi)
    zl = lax.rem(d, 2)
    y = d // 2
    z = zh * 2 + zl

    def device(x_, zh_, c_, y_, zl_):
        return {"dp": y_ * 2 + zl_, "fsdp": (x_ * z_hi + zh_) * 2 + c_}

    partner = device(x, zh, 1 - c, y, zl)
    x_peers = [lax.rem(x + k, n_x) for k in range(1, n_x)]
    z_peers = [lax.rem(z + k, n_z) for k in range(1, n_z)]
    y_peers = [lax.rem(y + k, n_y) for k in range(1, n_y)]
    everyone = [partner]
    everyone += [device(xp, zh, c, y, zl) for xp in x_peers]
    everyone += [device(x, zp // 2, c, y, lax.rem(zp, 2)) for zp in z_peers]
    everyone += [device(x, zh, c, yp, zl) for yp in y_peers]
    barrier = pltpu.get_barrier_semaphore()
    for peer in everyone:
        pl.semaphore_signal(barrier, inc=1, device_id=peer, device_id_type=MESH)
    pl.semaphore_wait(barrier, len(everyone))

    def start_exchange(src_of, dst_of, send_sems, recv_sems, peers, mine, device_of):
        sends, arrivals = [], []
        for p in peers:
            copy = pltpu.make_async_remote_copy(
                src_ref=src_of(p), dst_ref=dst_of(mine), send_sem=send_sems.at[p],
                recv_sem=recv_sems.at[mine], device_id=device_of(p), device_id_type=MESH)
            copy.start()
            sends.append(copy)
            arrivals.append(pltpu.make_async_remote_copy(
                src_ref=src_of(p), dst_ref=dst_of(p), send_sem=send_sems.at[p],
                recv_sem=recv_sems.at[p], device_id=device_of(p), device_id_type=MESH))
        return sends, arrivals

    def finish_exchange(pending):
        sends, arrivals = pending
        for copy in arrivals:
            copy.wait_recv()
        for copy in sends:
            copy.wait_send()

    def exchange(*args):
        finish_exchange(start_exchange(*args))

    core_copy = pltpu.make_async_remote_copy(
        src_ref=p_ref.at[1 - c], dst_ref=recv_c, send_sem=core_sems.at[0],
        recv_sem=core_sems.at[1], device_id=partner, device_id_type=MESH)
    core_copy.start()
    core_copy.wait()

    rows = 32
    chunks = band // rows

    def round_two_sums(i, carry):
        xi, r = i // chunks, lax.rem(i, chunks)
        at = pl.ds(pl.multiple_of(r * rows, rows), rows)
        both = p_ref[c, xi, at, :].astype(jnp.float32) + recv_c[xi, at, :].astype(jnp.float32)
        s1b[xi, at, :] = both.astype(s1b.dtype)
        return carry

    lax.fori_loop(0, n_x * chunks, round_two_sums, 0)
    pieces = x_send.shape[0]
    span = s1b.shape[2] // pieces

    def piece(k):
        return pl.ds(k * span, span)

    def x_stage(k):
        return start_exchange(lambda p: s1b.at[p, :, piece(k)], lambda p: recv_x.at[p, :, piece(k)],
                              x_send.at[k], x_recv.at[k], x_peers, x, lambda p: device(p, zh, c, y, zl))

    def z_stage(k):
        return start_exchange(lambda p: s2.at[p, :, piece(k)], lambda p: recv_z.at[p, :, piece(k)],
                              z_send.at[k], z_recv.at[k], z_peers, z,
                              lambda p: device(x, p // 2, c, y, lax.rem(p, 2)))

    def sum_x(k):
        def body(j, carry):
            at = pl.ds(pl.multiple_of(j * half, half), half)
            total = (p_ref[c, x, at, piece(k)].astype(jnp.float32)
                     + recv_c[x, at, piece(k)].astype(jnp.float32))
            for p in x_peers:
                total = total + recv_x[p, at, piece(k)].astype(jnp.float32)
            s2[j, :, piece(k)] = total.astype(s2.dtype)
            own[j, :, piece(k)] = total
            return carry
        lax.fori_loop(0, n_z, body, 0)

    x_pending = x_stage(0)
    z_pending = []
    for k in range(pieces):
        finish_exchange(x_pending)
        sum_x(k)
        z_pending.append(z_stage(k))
        if k + 1 < pieces:
            x_pending = x_stage(k + 1)
    for pending in z_pending:
        finish_exchange(pending)
    total = own[z]
    for p in z_peers:
        total = total + recv_z[p].astype(jnp.float32)
    s3[...] = total

    def cols(p):
        return pl.ds(pl.multiple_of(p * width, 128), width)

    exchange(lambda p: s3.at[:, cols(p)], lambda p: recv_y.at[p], y_send, y_recv, y_peers, y,
             lambda p: device(x, zh, c, p, zl))
    total = s3[:, cols(y)]
    for p in y_peers:
        total = total + recv_y[p]
    g16[:, cols(y)] = total * scale
    exchange(lambda p: g16.at[:, cols(y)], lambda p: g16.at[:, cols(p)], g_send, g_recv, y_peers, y,
             lambda p: device(x, zh, c, p, zl))
    out_ref[zl] = g16[...]
    pair_copy = pltpu.make_async_remote_copy(
        src_ref=g16, dst_ref=out_ref.at[zl], send_sem=pair_sems.at[0], recv_sem=pair_sems.at[1],
        device_id=device(x, zh, c, y, 1 - zl), device_id_type=MESH)
    pair_copy.start()
    pltpu.make_async_remote_copy(
        src_ref=g16, dst_ref=out_ref.at[1 - zl], send_sem=pair_sems.at[0], recv_sem=pair_sems.at[1],
        device_id=device(x, zh, c, y, 1 - zl), device_id_type=MESH).wait_recv()
    pair_copy.wait_send()


def grad_reduce(partial_rows, z_hi, scale):
    n_x = partial_rows.shape[1]
    n_y = lax.axis_size("dp") // 2
    cols = partial_rows.shape[3]
    shard = partial_rows.shape[2] // z_hi
    half = shard // 2
    band = partial_rows.shape[2]
    f32 = jnp.float32
    return pl.pallas_call(
        functools.partial(grad_reduce_kernel, z_hi, scale),
        out_shape=jax.ShapeDtypeStruct((2, half, cols), f32),
        in_specs=[pl.BlockSpec(memory_space=pltpu.VMEM)],
        out_specs=pl.BlockSpec(memory_space=pltpu.VMEM),
        scratch_shapes=[
            pltpu.VMEM((n_x, band, cols), partial_rows.dtype),
            pltpu.VMEM((n_x, band, cols), partial_rows.dtype),
            pltpu.VMEM((n_x, band, cols), partial_rows.dtype),
            pltpu.VMEM((2 * z_hi, half, cols), partial_rows.dtype),
            pltpu.VMEM((2 * z_hi, half, cols), f32),
            pltpu.VMEM((2 * z_hi, half, cols), partial_rows.dtype),
            pltpu.VMEM((half, cols), f32),
            pltpu.VMEM((n_y, half, cols // n_y), f32),
            pltpu.VMEM((half, cols), f32),
            pltpu.SemaphoreType.DMA((2,)),
            pltpu.SemaphoreType.DMA((PIECES, n_x)),
            pltpu.SemaphoreType.DMA((PIECES, n_x)),
            pltpu.SemaphoreType.DMA((PIECES, 2 * z_hi)),
            pltpu.SemaphoreType.DMA((PIECES, 2 * z_hi)),
            pltpu.SemaphoreType.DMA((n_y,)),
            pltpu.SemaphoreType.DMA((n_y,)),
            pltpu.SemaphoreType.DMA((n_y,)),
            pltpu.SemaphoreType.DMA((n_y,)),
            pltpu.SemaphoreType.DMA((2,)),
        ],
        compiler_params=pltpu.CompilerParams(
            collective_id=1, has_side_effects=True, vmem_limit_bytes=48 * 1024 * 1024),
    )(partial_rows)


def tap_starts(context_row_block):
    return [context_row_block - (2 - selected_index) * DILATION_SIZE for selected_index in range(3)]


def per_device(signal, grad_gated, conv_weight, source_seg):
    peer_count = lax.axis_size("fsdp")
    seg_count = source_seg.shape[1]
    row_count = signal.shape[0]
    seg_rows = row_count // seg_count
    context_row_block = 2 * DILATION_SIZE
    starts = tap_starts(context_row_block)
    segments = signal.reshape(seg_count, seg_rows, C)
    sources = source_seg[0]
    source_dev = jnp.where(sources >= 0, sources // seg_count, -1)
    peers = jnp.arange(peer_count, dtype=jnp.int32)
    request_mask = (source_dev[None, :] == peers[:, None]).astype(jnp.int32)
    asked = lax.all_to_all(request_mask, "fsdp", split_axis=0, concat_axis=0, tiled=True)
    send_table = asked.astype(jnp.bfloat16)
    recv_table = (source_dev[:, None] == peers[None, :]).astype(jnp.bfloat16)
    outgoing = jnp.einsum(
        "ns,slc->nlc", send_table, segments, preferred_element_type=jnp.float32
    ).astype(jnp.bfloat16)
    incoming = lax.all_to_all(outgoing, "fsdp", split_axis=0, concat_axis=0, tiled=True)
    carries = jnp.einsum(
        "sn,nlc->slc", recv_table, incoming, preferred_element_type=jnp.float32
    ).astype(jnp.bfloat16)
    extended = jnp.concatenate([carries, segments], axis=1)
    full_weight = lax.all_gather(conv_weight, "fsdp", axis=0, tiled=True)
    contract_final_axis = (((1,), (1,)), ((), ()))
    contract_first = (((0,), (0,)), ((), ()))
    windows = [extended[:, start : start + seg_rows, :].reshape(row_count, C) for start in starts]
    preact = sum(
        (
            lax.dot_general(
                windows[selected_index],
                full_weight[:, selected_index * C : (selected_index + 1) * C],
                contract_final_axis,
                preferred_element_type=jnp.float32,
            )
            for selected_index in range(3)
        )
    )
    filter_act = jnp.tanh(preact[:, :H])
    gate_act = jax.nn.sigmoid(preact[:, H:])
    gated_out = (filter_act * gate_act).astype(jnp.bfloat16)
    upstream_wide = grad_gated.astype(jnp.float32)
    grad_pre = jnp.concatenate(
        [
            upstream_wide * gate_act * (1.0 - filter_act * filter_act),
            upstream_wide * filter_act * gate_act * (1.0 - gate_act),
        ],
        axis=1,
    ).astype(jnp.bfloat16)
    z_hi = Z_HI
    n_x = peer_count // (2 * z_hi)
    shard = conv_weight.shape[0]
    routed = (
        grad_pre.reshape(row_count, n_x, z_hi, 2, shard)
        .transpose(0, 3, 1, 2, 4)
        .reshape(row_count, 2 * H)
    )
    stacked = jnp.concatenate(windows, axis=1)
    partial_value = lax.dot_general(
        routed, stacked, contract_first, preferred_element_type=jnp.float32
    ).astype(jnp.bfloat16)
    total_token_count = row_count * peer_count * lax.axis_size("dp")
    reduced = grad_reduce(
        partial_value.reshape(2, n_x, z_hi * shard, 3 * C), z_hi, 1.0 / math.sqrt(total_token_count)
    )
    grad_weight = reduced.reshape(shard, 3 * C)
    back_proj = jnp.dot(grad_pre, full_weight, preferred_element_type=jnp.float32)
    back_proj = back_proj.reshape(seg_count, seg_rows, 3 * C)
    grad_ext = jnp.zeros((seg_count, context_row_block + seg_rows, C), jnp.float32)
    for selected_index, start in enumerate(starts):
        grad_ext = grad_ext.at[:, start : start + seg_rows, :].add(
            back_proj[:, :, selected_index * C : (selected_index + 1) * C]
        )
    outgoing_grad = jnp.einsum(
        "sn,slc->nlc",
        recv_table.astype(jnp.float32),
        grad_ext[:, :context_row_block, :],
        precision=lax.Precision.HIGHEST,
    )
    incoming_grad = lax.all_to_all(outgoing_grad, "fsdp", split_axis=0, concat_axis=0, tiled=True)
    tail_grad = jnp.einsum(
        "ns,nlc->slc",
        send_table.astype(jnp.float32),
        incoming_grad,
        precision=lax.Precision.HIGHEST,
    )
    grad_in = (
        grad_ext[:, context_row_block:, :].at[:, seg_rows - context_row_block :, :].add(tail_grad)
    )
    grad_in = grad_in.reshape(row_count, C).astype(jnp.bfloat16)
    return (gated_out, grad_in, grad_weight)


def solution(mesh):
    placed = (
        P(("dp", "fsdp"), None),
        P(("dp", "fsdp"), None),
        P("fsdp", None),
        P(("dp", "fsdp"), None),
    )
    return jax.shard_map(
        per_device,
        mesh=mesh,
        in_specs=placed,
        out_specs=(P(("dp", "fsdp"), None), P(("dp", "fsdp"), None), P("fsdp", None)),
        check_vma=False,
    )
```

```python
import functools
import math

import jax
import jax.numpy as jnp
from jax import lax
from jax.experimental import pallas as pl
from jax.experimental.pallas import tpu as pltpu
from jax.sharding import PartitionSpec as P

MESH = pl.DeviceIdType.MESH

C = 1024
H = 512
DILATION_SIZE = 4
Z_HI = 4
PIECES = 4


def all_reduce_kernel(axis, n, x_ref, out_ref, gathered, summed, send_sems, recv_sems, out_send, out_recv):
    me = lax.axis_index(axis)
    barrier = pltpu.get_barrier_semaphore()
    for k in range(1, n):
        peer = lax.rem(me + k, n)
        pl.semaphore_signal(barrier, inc=1, device_id={axis: peer}, device_id_type=MESH)
    pl.semaphore_wait(barrier, n - 1)
    sends = []
    for k in range(1, n):
        peer = lax.rem(me + k, n)
        copy = pltpu.make_async_remote_copy(
            src_ref=x_ref.at[peer],
            dst_ref=gathered.at[me],
            send_sem=send_sems.at[peer],
            recv_sem=recv_sems.at[me],
            device_id={axis: peer},
            device_id_type=MESH,
        )
        copy.start()
        sends.append(copy)
    gathered[me] = x_ref[me]
    for k in range(1, n):
        peer = lax.rem(me + k, n)
        pltpu.make_async_remote_copy(
            src_ref=x_ref.at[peer],
            dst_ref=gathered.at[peer],
            send_sem=send_sems.at[peer],
            recv_sem=recv_sems.at[peer],
            device_id={axis: peer},
            device_id_type=MESH,
        ).wait_recv()
    for copy in sends:
        copy.wait_send()
    total = gathered[0]
    for k in range(1, n):
        total = total + gathered[k]
    summed[...] = total
    out_ref[me] = total
    shares = []
    for k in range(1, n):
        peer = lax.rem(me + k, n)
        copy = pltpu.make_async_remote_copy(
            src_ref=summed,
            dst_ref=out_ref.at[me],
            send_sem=out_send.at[peer],
            recv_sem=out_recv.at[me],
            device_id={axis: peer},
            device_id_type=MESH,
        )
        copy.start()
        shares.append(copy)
    for k in range(1, n):
        peer = lax.rem(me + k, n)
        pltpu.make_async_remote_copy(
            src_ref=summed,
            dst_ref=out_ref.at[peer],
            send_sem=out_send.at[peer],
            recv_sem=out_recv.at[peer],
            device_id={axis: peer},
            device_id_type=MESH,
        ).wait_recv()
    for copy in shares:
        copy.wait_send()


def all_reduce(x, axis):
    n = lax.axis_size(axis)
    shape = x.shape
    blocks = x.reshape(n, -1, 128)
    block_shape = blocks.shape[1:]
    out = pl.pallas_call(
        functools.partial(all_reduce_kernel, axis, n),
        out_shape=jax.ShapeDtypeStruct(blocks.shape, x.dtype),
        in_specs=[pl.BlockSpec(memory_space=pltpu.VMEM)],
        out_specs=pl.BlockSpec(memory_space=pltpu.VMEM),
        scratch_shapes=[
            pltpu.VMEM(blocks.shape, x.dtype),
            pltpu.VMEM(block_shape, x.dtype),
            pltpu.SemaphoreType.DMA((n,)),
            pltpu.SemaphoreType.DMA((n,)),
            pltpu.SemaphoreType.DMA((n,)),
            pltpu.SemaphoreType.DMA((n,)),
        ],
        compiler_params=pltpu.CompilerParams(collective_id=0, has_side_effects=True),
    )(blocks)
    return out.reshape(shape)


def grad_reduce_kernel(z_hi, scale, p_ref, out_ref, recv_c, s1b, recv_x, s2, own, recv_z, s3, recv_y, g16,
                       core_sems, x_send, x_recv, z_send, z_recv, y_send, y_recv, g_send, g_recv, pair_sems):
    n_x = recv_x.shape[0]
    n_z = 2 * z_hi
    n_y = recv_y.shape[0]
    band = recv_c.shape[1]
    half = s2.shape[1]
    width = recv_y.shape[2]
    f = lax.axis_index("fsdp")
    d = lax.axis_index("dp")
    c = lax.rem(f, 2)
    zh = lax.rem(f // 2, z_hi)
    x = f // (2 * z_hi)
    zl = lax.rem(d, 2)
    y = d // 2
    z = zh * 2 + zl

    def device(x_, zh_, c_, y_, zl_):
        return {"dp": y_ * 2 + zl_, "fsdp": (x_ * z_hi + zh_) * 2 + c_}

    partner = device(x, zh, 1 - c, y, zl)
    x_peers = [lax.rem(x + k, n_x) for k in range(1, n_x)]
    z_peers = [lax.rem(z + k, n_z) for k in range(1, n_z)]
    y_peers = [lax.rem(y + k, n_y) for k in range(1, n_y)]
    everyone = [partner]
    everyone += [device(xp, zh, c, y, zl) for xp in x_peers]
    everyone += [device(x, zp // 2, c, y, lax.rem(zp, 2)) for zp in z_peers]
    everyone += [device(x, zh, c, yp, zl) for yp in y_peers]
    barrier = pltpu.get_barrier_semaphore()
    for peer in everyone:
        pl.semaphore_signal(barrier, inc=1, device_id=peer, device_id_type=MESH)
    pl.semaphore_wait(barrier, len(everyone))

    def start_exchange(src_of, dst_of, send_sems, recv_sems, peers, mine, device_of):
        sends, arrivals = [], []
        for p in peers:
            copy = pltpu.make_async_remote_copy(
                src_ref=src_of(p), dst_ref=dst_of(mine), send_sem=send_sems.at[p],
                recv_sem=recv_sems.at[mine], device_id=device_of(p), device_id_type=MESH)
            copy.start()
            sends.append(copy)
            arrivals.append(pltpu.make_async_remote_copy(
                src_ref=src_of(p), dst_ref=dst_of(p), send_sem=send_sems.at[p],
                recv_sem=recv_sems.at[p], device_id=device_of(p), device_id_type=MESH))
        return sends, arrivals

    def finish_exchange(pending):
        sends, arrivals = pending
        for copy in arrivals:
            copy.wait_recv()
        for copy in sends:
            copy.wait_send()

    def exchange(*args):
        finish_exchange(start_exchange(*args))

    core_copy = pltpu.make_async_remote_copy(
        src_ref=p_ref.at[1 - c], dst_ref=recv_c, send_sem=core_sems.at[0],
        recv_sem=core_sems.at[1], device_id=partner, device_id_type=MESH)
    core_copy.start()
    core_copy.wait()

    rows = 32
    chunks = band // rows

    def round_two_sums(i, carry):
        xi, r = i // chunks, lax.rem(i, chunks)
        at = pl.ds(pl.multiple_of(r * rows, rows), rows)
        both = p_ref[c, xi, at, :].astype(jnp.float32) + recv_c[xi, at, :].astype(jnp.float32)
        s1b[xi, at, :] = both.astype(s1b.dtype)
        return carry

    lax.fori_loop(0, n_x * chunks, round_two_sums, 0)
    pieces = x_send.shape[0]
    span = s1b.shape[2] // pieces

    def piece(k):
        return pl.ds(k * span, span)

    def x_stage(k):
        return start_exchange(lambda p: s1b.at[p, :, piece(k)], lambda p: recv_x.at[p, :, piece(k)],
                              x_send.at[k], x_recv.at[k], x_peers, x, lambda p: device(p, zh, c, y, zl))

    def z_stage(k):
        return start_exchange(lambda p: s2.at[p, :, piece(k)], lambda p: recv_z.at[p, :, piece(k)],
                              z_send.at[k], z_recv.at[k], z_peers, z,
                              lambda p: device(x, p // 2, c, y, lax.rem(p, 2)))

    def sum_x(k):
        def body(j, carry):
            at = pl.ds(pl.multiple_of(j * half, half), half)
            total = (p_ref[c, x, at, piece(k)].astype(jnp.float32)
                     + recv_c[x, at, piece(k)].astype(jnp.float32))
            for p in x_peers:
                total = total + recv_x[p, at, piece(k)].astype(jnp.float32)
            s2[j, :, piece(k)] = total.astype(s2.dtype)
            own[j, :, piece(k)] = total
            return carry
        lax.fori_loop(0, n_z, body, 0)

    x_pending = x_stage(0)
    z_pending = []
    for k in range(pieces):
        finish_exchange(x_pending)
        sum_x(k)
        z_pending.append(z_stage(k))
        if k + 1 < pieces:
            x_pending = x_stage(k + 1)
    for pending in z_pending:
        finish_exchange(pending)
    total = own[z]
    for p in z_peers:
        total = total + recv_z[p].astype(jnp.float32)
    s3[...] = total

    def cols(p):
        return pl.ds(pl.multiple_of(p * width, 128), width)

    exchange(lambda p: s3.at[:, cols(p)], lambda p: recv_y.at[p], y_send, y_recv, y_peers, y,
             lambda p: device(x, zh, c, p, zl))
    total = s3[:, cols(y)]
    for p in y_peers:
        total = total + recv_y[p]
    g16[:, cols(y)] = total * scale
    exchange(lambda p: g16.at[:, cols(y)], lambda p: g16.at[:, cols(p)], g_send, g_recv, y_peers, y,
             lambda p: device(x, zh, c, p, zl))
    out_ref[zl] = g16[...]
    pair_copy = pltpu.make_async_remote_copy(
        src_ref=g16, dst_ref=out_ref.at[zl], send_sem=pair_sems.at[0], recv_sem=pair_sems.at[1],
        device_id=device(x, zh, c, y, 1 - zl), device_id_type=MESH)
    pair_copy.start()
    pltpu.make_async_remote_copy(
        src_ref=g16, dst_ref=out_ref.at[1 - zl], send_sem=pair_sems.at[0], recv_sem=pair_sems.at[1],
        device_id=device(x, zh, c, y, 1 - zl), device_id_type=MESH).wait_recv()
    pair_copy.wait_send()


def grad_reduce(partial_rows, z_hi, scale):
    n_x = partial_rows.shape[1]
    n_y = lax.axis_size("dp") // 2
    cols = partial_rows.shape[3]
    shard = partial_rows.shape[2] // z_hi
    half = shard // 2
    band = partial_rows.shape[2]
    f32 = jnp.float32
    return pl.pallas_call(
        functools.partial(grad_reduce_kernel, z_hi, scale),
        out_shape=jax.ShapeDtypeStruct((2, half, cols), f32),
        in_specs=[pl.BlockSpec(memory_space=pltpu.VMEM)],
        out_specs=pl.BlockSpec(memory_space=pltpu.VMEM),
        scratch_shapes=[
            pltpu.VMEM((n_x, band, cols), partial_rows.dtype),
            pltpu.VMEM((n_x, band, cols), partial_rows.dtype),
            pltpu.VMEM((n_x, band, cols), partial_rows.dtype),
            pltpu.VMEM((2 * z_hi, half, cols), partial_rows.dtype),
            pltpu.VMEM((2 * z_hi, half, cols), f32),
            pltpu.VMEM((2 * z_hi, half, cols), partial_rows.dtype),
            pltpu.VMEM((half, cols), f32),
            pltpu.VMEM((n_y, half, cols // n_y), f32),
            pltpu.VMEM((half, cols), f32),
            pltpu.SemaphoreType.DMA((2,)),
            pltpu.SemaphoreType.DMA((PIECES, n_x)),
            pltpu.SemaphoreType.DMA((PIECES, n_x)),
            pltpu.SemaphoreType.DMA((PIECES, 2 * z_hi)),
            pltpu.SemaphoreType.DMA((PIECES, 2 * z_hi)),
            pltpu.SemaphoreType.DMA((n_y,)),
            pltpu.SemaphoreType.DMA((n_y,)),
            pltpu.SemaphoreType.DMA((n_y,)),
            pltpu.SemaphoreType.DMA((n_y,)),
            pltpu.SemaphoreType.DMA((2,)),
        ],
        compiler_params=pltpu.CompilerParams(
            collective_id=1, has_side_effects=True, vmem_limit_bytes=48 * 1024 * 1024),
    )(partial_rows)


def tap_starts(context_row_block):
    return [context_row_block - (2 - selected_index) * DILATION_SIZE for selected_index in range(3)]


def per_device(signal, grad_gated, conv_weight, source_seg):
    peer_count = lax.axis_size("fsdp")
    seg_count = source_seg.shape[1]
    row_count = signal.shape[0]
    seg_rows = row_count // seg_count
    context_row_block = 2 * DILATION_SIZE
    starts = tap_starts(context_row_block)
    segments = signal.reshape(seg_count, seg_rows, C)
    sources = source_seg[0]
    source_dev = jnp.where(sources >= 0, sources // seg_count, -1)
    peers = jnp.arange(peer_count, dtype=jnp.int32)
    request_mask = (source_dev[None, :] == peers[:, None]).astype(jnp.int32)
    asked = lax.all_to_all(request_mask, "fsdp", split_axis=0, concat_axis=0, tiled=True)
    send_table = asked.astype(jnp.bfloat16)
    recv_table = (source_dev[:, None] == peers[None, :]).astype(jnp.bfloat16)
    outgoing = jnp.einsum(
        "ns,slc->nlc", send_table, segments, preferred_element_type=jnp.float32
    ).astype(jnp.bfloat16)
    incoming = lax.all_to_all(outgoing, "fsdp", split_axis=0, concat_axis=0, tiled=True)
    carries = jnp.einsum(
        "sn,nlc->slc", recv_table, incoming, preferred_element_type=jnp.float32
    ).astype(jnp.bfloat16)
    extended = jnp.concatenate([carries, segments], axis=1)
    full_weight = lax.all_gather(conv_weight, "fsdp", axis=0, tiled=True)
    contract_final_axis = (((1,), (1,)), ((), ()))
    contract_first = (((0,), (0,)), ((), ()))
    windows = [extended[:, start : start + seg_rows, :].reshape(row_count, C) for start in starts]
    preact = sum(
        (
            lax.dot_general(
                windows[selected_index],
                full_weight[:, selected_index * C : (selected_index + 1) * C],
                contract_final_axis,
                preferred_element_type=jnp.float32,
            )
            for selected_index in range(3)
        )
    )
    filter_act = jnp.tanh(preact[:, :H])
    gate_act = jax.nn.sigmoid(preact[:, H:])
    gated_out = (filter_act * gate_act).astype(jnp.bfloat16)
    upstream_wide = grad_gated.astype(jnp.float32)
    grad_pre = jnp.concatenate(
        [
            upstream_wide * gate_act * (1.0 - filter_act * filter_act),
            upstream_wide * filter_act * gate_act * (1.0 - gate_act),
        ],
        axis=1,
    ).astype(jnp.bfloat16)
    z_hi = Z_HI
    n_x = peer_count // (2 * z_hi)
    shard = conv_weight.shape[0]
    routed = (
        grad_pre.reshape(row_count, n_x, z_hi, 2, shard)
        .transpose(0, 3, 1, 2, 4)
        .reshape(row_count, 2 * H)
    )
    stacked = jnp.concatenate(windows, axis=1)
    partial_value = lax.dot_general(
        routed, stacked, contract_first, preferred_element_type=jnp.float32
    ).astype(jnp.bfloat16)
    total_token_count = row_count * peer_count * lax.axis_size("dp")
    reduced = grad_reduce(
        partial_value.reshape(2, n_x, z_hi * shard, 3 * C), z_hi, 1.0 / math.sqrt(total_token_count)
    )
    grad_weight = reduced.reshape(shard, 3 * C)
    back_proj = jnp.dot(grad_pre, full_weight, preferred_element_type=jnp.float32)
    back_proj = back_proj.reshape(seg_count, seg_rows, 3 * C)
    grad_ext = jnp.zeros((seg_count, context_row_block + seg_rows, C), jnp.float32)
    for selected_index, start in enumerate(starts):
        grad_ext = grad_ext.at[:, start : start + seg_rows, :].add(
            back_proj[:, :, selected_index * C : (selected_index + 1) * C]
        )
    outgoing_grad = jnp.einsum(
        "sn,slc->nlc",
        recv_table.astype(jnp.float32),
        grad_ext[:, :context_row_block, :],
        precision=lax.Precision.HIGHEST,
    )
    incoming_grad = lax.all_to_all(outgoing_grad, "fsdp", split_axis=0, concat_axis=0, tiled=True)
    tail_grad = jnp.einsum(
        "ns,nlc->slc",
        send_table.astype(jnp.float32),
        incoming_grad,
        precision=lax.Precision.HIGHEST,
    )
    grad_in = (
        grad_ext[:, context_row_block:, :].at[:, seg_rows - context_row_block :, :].add(tail_grad)
    )
    grad_in = grad_in.reshape(row_count, C).astype(jnp.bfloat16)
    return (gated_out, grad_in, grad_weight)


def solution(mesh):
    placed = (
        P(("dp", "fsdp"), None),
        P(("dp", "fsdp"), None),
        P("fsdp", None),
        P(("dp", "fsdp"), None),
    )
    return jax.shard_map(
        per_device,
        mesh=mesh,
        in_specs=placed,
        out_specs=(P(("dp", "fsdp"), None), P(("dp", "fsdp"), None), P("fsdp", None)),
        check_vma=False,
    )
```

```python
import functools
import math

import jax
import jax.numpy as jnp
from jax import lax
from jax.experimental import pallas as pl
from jax.experimental.pallas import tpu as pltpu
from jax.sharding import PartitionSpec as P

MESH = pl.DeviceIdType.MESH

C = 1024
H = 512
DILATION_SIZE = 4
Z_HI = 4
PIECES = 2


def all_reduce_kernel(axis, n, x_ref, out_ref, gathered, summed, send_sems, recv_sems, out_send, out_recv):
    me = lax.axis_index(axis)
    barrier = pltpu.get_barrier_semaphore()
    for k in range(1, n):
        peer = lax.rem(me + k, n)
        pl.semaphore_signal(barrier, inc=1, device_id={axis: peer}, device_id_type=MESH)
    pl.semaphore_wait(barrier, n - 1)
    sends = []
    for k in range(1, n):
        peer = lax.rem(me + k, n)
        copy = pltpu.make_async_remote_copy(
            src_ref=x_ref.at[peer],
            dst_ref=gathered.at[me],
            send_sem=send_sems.at[peer],
            recv_sem=recv_sems.at[me],
            device_id={axis: peer},
            device_id_type=MESH,
        )
        copy.start()
        sends.append(copy)
    gathered[me] = x_ref[me]
    for k in range(1, n):
        peer = lax.rem(me + k, n)
        pltpu.make_async_remote_copy(
            src_ref=x_ref.at[peer],
            dst_ref=gathered.at[peer],
            send_sem=send_sems.at[peer],
            recv_sem=recv_sems.at[peer],
            device_id={axis: peer},
            device_id_type=MESH,
        ).wait_recv()
    for copy in sends:
        copy.wait_send()
    total = gathered[0]
    for k in range(1, n):
        total = total + gathered[k]
    summed[...] = total
    out_ref[me] = total
    shares = []
    for k in range(1, n):
        peer = lax.rem(me + k, n)
        copy = pltpu.make_async_remote_copy(
            src_ref=summed,
            dst_ref=out_ref.at[me],
            send_sem=out_send.at[peer],
            recv_sem=out_recv.at[me],
            device_id={axis: peer},
            device_id_type=MESH,
        )
        copy.start()
        shares.append(copy)
    for k in range(1, n):
        peer = lax.rem(me + k, n)
        pltpu.make_async_remote_copy(
            src_ref=summed,
            dst_ref=out_ref.at[peer],
            send_sem=out_send.at[peer],
            recv_sem=out_recv.at[peer],
            device_id={axis: peer},
            device_id_type=MESH,
        ).wait_recv()
    for copy in shares:
        copy.wait_send()


def all_reduce(x, axis):
    n = lax.axis_size(axis)
    shape = x.shape
    blocks = x.reshape(n, -1, 128)
    block_shape = blocks.shape[1:]
    out = pl.pallas_call(
        functools.partial(all_reduce_kernel, axis, n),
        out_shape=jax.ShapeDtypeStruct(blocks.shape, x.dtype),
        in_specs=[pl.BlockSpec(memory_space=pltpu.VMEM)],
        out_specs=pl.BlockSpec(memory_space=pltpu.VMEM),
        scratch_shapes=[
            pltpu.VMEM(blocks.shape, x.dtype),
            pltpu.VMEM(block_shape, x.dtype),
            pltpu.SemaphoreType.DMA((n,)),
            pltpu.SemaphoreType.DMA((n,)),
            pltpu.SemaphoreType.DMA((n,)),
            pltpu.SemaphoreType.DMA((n,)),
        ],
        compiler_params=pltpu.CompilerParams(collective_id=0, has_side_effects=True),
    )(blocks)
    return out.reshape(shape)


def grad_reduce_kernel(z_hi, scale, p_ref, out_ref, recv_c, s1b, recv_x, s2, own, recv_z, s3, recv_y, g16,
                       core_sems, x_send, x_recv, z_send, z_recv, y_send, y_recv, g_send, g_recv, pair_sems):
    n_x = recv_x.shape[0]
    n_z = 2 * z_hi
    n_y = recv_y.shape[0]
    band = recv_c.shape[1]
    half = s2.shape[1]
    width = recv_y.shape[2]
    f = lax.axis_index("fsdp")
    d = lax.axis_index("dp")
    c = lax.rem(f, 2)
    zh = lax.rem(f // 2, z_hi)
    x = f // (2 * z_hi)
    zl = lax.rem(d, 2)
    y = d // 2
    z = zh * 2 + zl

    def device(x_, zh_, c_, y_, zl_):
        return {"dp": y_ * 2 + zl_, "fsdp": (x_ * z_hi + zh_) * 2 + c_}

    partner = device(x, zh, 1 - c, y, zl)
    x_peers = [lax.rem(x + k, n_x) for k in range(1, n_x)]
    z_peers = [lax.rem(z + k, n_z) for k in range(1, n_z)]
    y_peers = [lax.rem(y + k, n_y) for k in range(1, n_y)]
    everyone = [partner]
    everyone += [device(xp, zh, c, y, zl) for xp in x_peers]
    everyone += [device(x, zp // 2, c, y, lax.rem(zp, 2)) for zp in z_peers]
    everyone += [device(x, zh, c, yp, zl) for yp in y_peers]
    barrier = pltpu.get_barrier_semaphore()
    for peer in everyone:
        pl.semaphore_signal(barrier, inc=1, device_id=peer, device_id_type=MESH)
    pl.semaphore_wait(barrier, len(everyone))

    def start_exchange(src_of, dst_of, send_sems, recv_sems, peers, mine, device_of):
        sends, arrivals = [], []
        for p in peers:
            copy = pltpu.make_async_remote_copy(
                src_ref=src_of(p), dst_ref=dst_of(mine), send_sem=send_sems.at[p],
                recv_sem=recv_sems.at[mine], device_id=device_of(p), device_id_type=MESH)
            copy.start()
            sends.append(copy)
            arrivals.append(pltpu.make_async_remote_copy(
                src_ref=src_of(p), dst_ref=dst_of(p), send_sem=send_sems.at[p],
                recv_sem=recv_sems.at[p], device_id=device_of(p), device_id_type=MESH))
        return sends, arrivals

    def finish_exchange(pending):
        sends, arrivals = pending
        for copy in arrivals:
            copy.wait_recv()
        for copy in sends:
            copy.wait_send()

    def exchange(*args):
        finish_exchange(start_exchange(*args))

    core_copy = pltpu.make_async_remote_copy(
        src_ref=p_ref.at[1 - c], dst_ref=recv_c, send_sem=core_sems.at[0],
        recv_sem=core_sems.at[1], device_id=partner, device_id_type=MESH)
    core_copy.start()
    core_copy.wait()

    rows = 32
    chunks = band // rows

    def round_two_sums(i, carry):
        xi, r = i // chunks, lax.rem(i, chunks)
        at = pl.ds(pl.multiple_of(r * rows, rows), rows)
        both = p_ref[c, xi, at, :].astype(jnp.float32) + recv_c[xi, at, :].astype(jnp.float32)
        s1b[xi, at, :] = both.astype(s1b.dtype)
        return carry

    lax.fori_loop(0, n_x * chunks, round_two_sums, 0)
    pieces = x_send.shape[0]
    span = s1b.shape[2] // pieces

    def piece(k):
        return pl.ds(k * span, span)

    def x_stage(k):
        return start_exchange(lambda p: s1b.at[p, :, piece(k)], lambda p: recv_x.at[p, :, piece(k)],
                              x_send.at[k], x_recv.at[k], x_peers, x, lambda p: device(p, zh, c, y, zl))

    def z_stage(k):
        return start_exchange(lambda p: s2.at[p, :, piece(k)], lambda p: recv_z.at[p, :, piece(k)],
                              z_send.at[k], z_recv.at[k], z_peers, z,
                              lambda p: device(x, p // 2, c, y, lax.rem(p, 2)))

    def sum_x(k):
        def body(j, carry):
            at = pl.ds(pl.multiple_of(j * half, half), half)
            total = (p_ref[c, x, at, piece(k)].astype(jnp.float32)
                     + recv_c[x, at, piece(k)].astype(jnp.float32))
            for p in x_peers:
                total = total + recv_x[p, at, piece(k)].astype(jnp.float32)
            s2[j, :, piece(k)] = total.astype(s2.dtype)
            own[j, :, piece(k)] = total
            return carry
        lax.fori_loop(0, n_z, body, 0)

    x_pending = x_stage(0)
    z_pending = []
    for k in range(pieces):
        finish_exchange(x_pending)
        sum_x(k)
        z_pending.append(z_stage(k))
        if k + 1 < pieces:
            x_pending = x_stage(k + 1)
    for pending in z_pending:
        finish_exchange(pending)
    total = own[z]
    for p in z_peers:
        total = total + recv_z[p].astype(jnp.float32)
    s3[...] = total

    def cols(p):
        return pl.ds(pl.multiple_of(p * width, 128), width)

    exchange(lambda p: s3.at[:, cols(p)], lambda p: recv_y.at[p], y_send, y_recv, y_peers, y,
             lambda p: device(x, zh, c, p, zl))
    total = s3[:, cols(y)]
    for p in y_peers:
        total = total + recv_y[p]
    g16[:, cols(y)] = total * scale
    exchange(lambda p: g16.at[:, cols(y)], lambda p: g16.at[:, cols(p)], g_send, g_recv, y_peers, y,
             lambda p: device(x, zh, c, p, zl))
    out_ref[zl] = g16[...]
    pair_copy = pltpu.make_async_remote_copy(
        src_ref=g16, dst_ref=out_ref.at[zl], send_sem=pair_sems.at[0], recv_sem=pair_sems.at[1],
        device_id=device(x, zh, c, y, 1 - zl), device_id_type=MESH)
    pair_copy.start()
    pltpu.make_async_remote_copy(
        src_ref=g16, dst_ref=out_ref.at[1 - zl], send_sem=pair_sems.at[0], recv_sem=pair_sems.at[1],
        device_id=device(x, zh, c, y, 1 - zl), device_id_type=MESH).wait_recv()
    pair_copy.wait_send()


def grad_reduce(partial_rows, z_hi, scale):
    n_x = partial_rows.shape[1]
    n_y = lax.axis_size("dp") // 2
    cols = partial_rows.shape[3]
    shard = partial_rows.shape[2] // z_hi
    half = shard // 2
    band = partial_rows.shape[2]
    f32 = jnp.float32
    return pl.pallas_call(
        functools.partial(grad_reduce_kernel, z_hi, scale),
        out_shape=jax.ShapeDtypeStruct((2, half, cols), f32),
        in_specs=[pl.BlockSpec(memory_space=pltpu.VMEM)],
        out_specs=pl.BlockSpec(memory_space=pltpu.VMEM),
        scratch_shapes=[
            pltpu.VMEM((n_x, band, cols), partial_rows.dtype),
            pltpu.VMEM((n_x, band, cols), partial_rows.dtype),
            pltpu.VMEM((n_x, band, cols), partial_rows.dtype),
            pltpu.VMEM((2 * z_hi, half, cols), partial_rows.dtype),
            pltpu.VMEM((2 * z_hi, half, cols), f32),
            pltpu.VMEM((2 * z_hi, half, cols), partial_rows.dtype),
            pltpu.VMEM((half, cols), f32),
            pltpu.VMEM((n_y, half, cols // n_y), f32),
            pltpu.VMEM((half, cols), f32),
            pltpu.SemaphoreType.DMA((2,)),
            pltpu.SemaphoreType.DMA((PIECES, n_x)),
            pltpu.SemaphoreType.DMA((PIECES, n_x)),
            pltpu.SemaphoreType.DMA((PIECES, 2 * z_hi)),
            pltpu.SemaphoreType.DMA((PIECES, 2 * z_hi)),
            pltpu.SemaphoreType.DMA((n_y,)),
            pltpu.SemaphoreType.DMA((n_y,)),
            pltpu.SemaphoreType.DMA((n_y,)),
            pltpu.SemaphoreType.DMA((n_y,)),
            pltpu.SemaphoreType.DMA((2,)),
        ],
        compiler_params=pltpu.CompilerParams(
            collective_id=1, has_side_effects=True, vmem_limit_bytes=48 * 1024 * 1024),
    )(partial_rows)


def tap_starts(context_row_block):
    return [context_row_block - (2 - selected_index) * DILATION_SIZE for selected_index in range(3)]


def per_device(signal, grad_gated, conv_weight, source_seg):
    peer_count = lax.axis_size("fsdp")
    seg_count = source_seg.shape[1]
    row_count = signal.shape[0]
    seg_rows = row_count // seg_count
    context_row_block = 2 * DILATION_SIZE
    starts = tap_starts(context_row_block)
    segments = signal.reshape(seg_count, seg_rows, C)
    sources = source_seg[0]
    source_dev = jnp.where(sources >= 0, sources // seg_count, -1)
    peers = jnp.arange(peer_count, dtype=jnp.int32)
    request_mask = (source_dev[None, :] == peers[:, None]).astype(jnp.int32)
    asked = lax.all_to_all(request_mask, "fsdp", split_axis=0, concat_axis=0, tiled=True)
    send_table = asked.astype(jnp.bfloat16)
    recv_table = (source_dev[:, None] == peers[None, :]).astype(jnp.bfloat16)
    outgoing = jnp.einsum(
        "ns,slc->nlc", send_table, segments, preferred_element_type=jnp.float32
    ).astype(jnp.bfloat16)
    incoming = lax.all_to_all(outgoing, "fsdp", split_axis=0, concat_axis=0, tiled=True)
    carries = jnp.einsum(
        "sn,nlc->slc", recv_table, incoming, preferred_element_type=jnp.float32
    ).astype(jnp.bfloat16)
    extended = jnp.concatenate([carries, segments], axis=1)
    full_weight = lax.all_gather(conv_weight, "fsdp", axis=0, tiled=True)
    contract_final_axis = (((1,), (1,)), ((), ()))
    contract_first = (((0,), (0,)), ((), ()))
    windows = [extended[:, start : start + seg_rows, :].reshape(row_count, C) for start in starts]
    preact = sum(
        (
            lax.dot_general(
                windows[selected_index],
                full_weight[:, selected_index * C : (selected_index + 1) * C],
                contract_final_axis,
                preferred_element_type=jnp.float32,
            )
            for selected_index in range(3)
        )
    )
    filter_act = jnp.tanh(preact[:, :H])
    gate_act = jax.nn.sigmoid(preact[:, H:])
    gated_out = (filter_act * gate_act).astype(jnp.bfloat16)
    upstream_wide = grad_gated.astype(jnp.float32)
    grad_pre = jnp.concatenate(
        [
            upstream_wide * gate_act * (1.0 - filter_act * filter_act),
            upstream_wide * filter_act * gate_act * (1.0 - gate_act),
        ],
        axis=1,
    ).astype(jnp.bfloat16)
    z_hi = Z_HI
    n_x = peer_count // (2 * z_hi)
    shard = conv_weight.shape[0]
    routed = (
        grad_pre.reshape(row_count, n_x, z_hi, 2, shard)
        .transpose(0, 3, 1, 2, 4)
        .reshape(row_count, 2 * H)
    )
    stacked = jnp.concatenate(windows, axis=1)
    partial_value = lax.dot_general(
        routed, stacked, contract_first, preferred_element_type=jnp.float32
    ).astype(jnp.bfloat16)
    total_token_count = row_count * peer_count * lax.axis_size("dp")
    reduced = grad_reduce(
        partial_value.reshape(2, n_x, z_hi * shard, 3 * C), z_hi, 1.0 / math.sqrt(total_token_count)
    )
    grad_weight = reduced.reshape(shard, 3 * C)
    back_proj = jnp.dot(grad_pre, full_weight, preferred_element_type=jnp.float32)
    back_proj = back_proj.reshape(seg_count, seg_rows, 3 * C)
    grad_ext = jnp.zeros((seg_count, context_row_block + seg_rows, C), jnp.float32)
    for selected_index, start in enumerate(starts):
        grad_ext = grad_ext.at[:, start : start + seg_rows, :].add(
            back_proj[:, :, selected_index * C : (selected_index + 1) * C]
        )
    outgoing_grad = jnp.einsum(
        "sn,slc->nlc",
        recv_table,
        grad_ext[:, :context_row_block, :].astype(jnp.bfloat16),
        preferred_element_type=jnp.float32,
    ).astype(jnp.bfloat16)
    incoming_grad = lax.all_to_all(outgoing_grad, "fsdp", split_axis=0, concat_axis=0, tiled=True)
    tail_grad = jnp.einsum(
        "ns,nlc->slc",
        send_table,
        incoming_grad,
        preferred_element_type=jnp.float32,
    )
    grad_in = (
        grad_ext[:, context_row_block:, :].at[:, seg_rows - context_row_block :, :].add(tail_grad)
    )
    grad_in = grad_in.reshape(row_count, C).astype(jnp.bfloat16)
    return (gated_out, grad_in, grad_weight)


def solution(mesh):
    placed = (
        P(("dp", "fsdp"), None),
        P(("dp", "fsdp"), None),
        P("fsdp", None),
        P(("dp", "fsdp"), None),
    )
    return jax.shard_map(
        per_device,
        mesh=mesh,
        in_specs=placed,
        out_specs=(P(("dp", "fsdp"), None), P(("dp", "fsdp"), None), P("fsdp", None)),
        check_vma=False,
    )
```

```python
import functools
import math

import jax
import jax.numpy as jnp
from jax import lax
from jax.experimental import pallas as pl
from jax.experimental.pallas import tpu as pltpu
from jax.sharding import PartitionSpec as P

MESH = pl.DeviceIdType.MESH

C = 1024
H = 512
DILATION_SIZE = 4
Z_HI = 4
PIECES = 2


def all_reduce_kernel(axis, n, x_ref, out_ref, gathered, summed, send_sems, recv_sems, out_send, out_recv):
    me = lax.axis_index(axis)
    barrier = pltpu.get_barrier_semaphore()
    for k in range(1, n):
        peer = lax.rem(me + k, n)
        pl.semaphore_signal(barrier, inc=1, device_id={axis: peer}, device_id_type=MESH)
    pl.semaphore_wait(barrier, n - 1)
    sends = []
    for k in range(1, n):
        peer = lax.rem(me + k, n)
        copy = pltpu.make_async_remote_copy(
            src_ref=x_ref.at[peer],
            dst_ref=gathered.at[me],
            send_sem=send_sems.at[peer],
            recv_sem=recv_sems.at[me],
            device_id={axis: peer},
            device_id_type=MESH,
        )
        copy.start()
        sends.append(copy)
    gathered[me] = x_ref[me]
    for k in range(1, n):
        peer = lax.rem(me + k, n)
        pltpu.make_async_remote_copy(
            src_ref=x_ref.at[peer],
            dst_ref=gathered.at[peer],
            send_sem=send_sems.at[peer],
            recv_sem=recv_sems.at[peer],
            device_id={axis: peer},
            device_id_type=MESH,
        ).wait_recv()
    for copy in sends:
        copy.wait_send()
    total = gathered[0]
    for k in range(1, n):
        total = total + gathered[k]
    summed[...] = total
    out_ref[me] = total
    shares = []
    for k in range(1, n):
        peer = lax.rem(me + k, n)
        copy = pltpu.make_async_remote_copy(
            src_ref=summed,
            dst_ref=out_ref.at[me],
            send_sem=out_send.at[peer],
            recv_sem=out_recv.at[me],
            device_id={axis: peer},
            device_id_type=MESH,
        )
        copy.start()
        shares.append(copy)
    for k in range(1, n):
        peer = lax.rem(me + k, n)
        pltpu.make_async_remote_copy(
            src_ref=summed,
            dst_ref=out_ref.at[peer],
            send_sem=out_send.at[peer],
            recv_sem=out_recv.at[peer],
            device_id={axis: peer},
            device_id_type=MESH,
        ).wait_recv()
    for copy in shares:
        copy.wait_send()


def all_reduce(x, axis):
    n = lax.axis_size(axis)
    shape = x.shape
    blocks = x.reshape(n, -1, 128)
    block_shape = blocks.shape[1:]
    out = pl.pallas_call(
        functools.partial(all_reduce_kernel, axis, n),
        out_shape=jax.ShapeDtypeStruct(blocks.shape, x.dtype),
        in_specs=[pl.BlockSpec(memory_space=pltpu.VMEM)],
        out_specs=pl.BlockSpec(memory_space=pltpu.VMEM),
        scratch_shapes=[
            pltpu.VMEM(blocks.shape, x.dtype),
            pltpu.VMEM(block_shape, x.dtype),
            pltpu.SemaphoreType.DMA((n,)),
            pltpu.SemaphoreType.DMA((n,)),
            pltpu.SemaphoreType.DMA((n,)),
            pltpu.SemaphoreType.DMA((n,)),
        ],
        compiler_params=pltpu.CompilerParams(collective_id=0, has_side_effects=True),
    )(blocks)
    return out.reshape(shape)


def grad_reduce_kernel(z_hi, scale, p_ref, back_ref, out_ref, back_out, recv_c, s1b, recv_x, s2, own, recv_z, s3, recv_y, g16,
                       core_sems, x_send, x_recv, z_send, z_recv, y_send, y_recv, g_send, g_recv, pair_sems,
                       back_sems):
    n_x = recv_x.shape[0]
    n_z = 2 * z_hi
    n_y = recv_y.shape[0]
    band = recv_c.shape[1]
    half = s2.shape[1]
    width = recv_y.shape[2]
    f = lax.axis_index("fsdp")
    d = lax.axis_index("dp")
    c = lax.rem(f, 2)
    zh = lax.rem(f // 2, z_hi)
    x = f // (2 * z_hi)
    zl = lax.rem(d, 2)
    y = d // 2
    z = zh * 2 + zl

    def device(x_, zh_, c_, y_, zl_):
        return {"dp": y_ * 2 + zl_, "fsdp": (x_ * z_hi + zh_) * 2 + c_}

    partner = device(x, zh, 1 - c, y, zl)
    x_peers = [lax.rem(x + k, n_x) for k in range(1, n_x)]
    z_peers = [lax.rem(z + k, n_z) for k in range(1, n_z)]
    y_peers = [lax.rem(y + k, n_y) for k in range(1, n_y)]
    n_f = back_ref.shape[0]
    f_peers = [lax.rem(f + k, n_f) for k in range(1, n_f)]
    everyone = [{"dp": d, "fsdp": fp} for fp in f_peers]
    everyone += [device(x, zp // 2, c, y, lax.rem(zp, 2)) for k, zp in enumerate(z_peers, 1) if k % 2]
    everyone += [device(x, zh, c, yp, zl) for yp in y_peers]
    barrier = pltpu.get_barrier_semaphore()
    for peer in everyone:
        pl.semaphore_signal(barrier, inc=1, device_id=peer, device_id_type=MESH)
    pl.semaphore_wait(barrier, len(everyone))

    def start_exchange(src_of, dst_of, send_sems, recv_sems, peers, mine, device_of):
        sends, arrivals = [], []
        for p in peers:
            copy = pltpu.make_async_remote_copy(
                src_ref=src_of(p), dst_ref=dst_of(mine), send_sem=send_sems.at[p],
                recv_sem=recv_sems.at[mine], device_id=device_of(p), device_id_type=MESH)
            copy.start()
            sends.append(copy)
            arrivals.append(pltpu.make_async_remote_copy(
                src_ref=src_of(p), dst_ref=dst_of(p), send_sem=send_sems.at[p],
                recv_sem=recv_sems.at[p], device_id=device_of(p), device_id_type=MESH))
        return sends, arrivals

    def finish_exchange(pending):
        sends, arrivals = pending
        for copy in arrivals:
            copy.wait_recv()
        for copy in sends:
            copy.wait_send()

    def exchange(*args):
        finish_exchange(start_exchange(*args))

    back_pending = start_exchange(lambda p: back_ref.at[p], lambda p: back_out.at[p], back_sems.at[0],
                                  back_sems.at[1], f_peers, f, lambda p: {"dp": d, "fsdp": p})
    back_out[f] = back_ref[f]
    core_copy = pltpu.make_async_remote_copy(
        src_ref=p_ref.at[1 - c], dst_ref=recv_c, send_sem=core_sems.at[0],
        recv_sem=core_sems.at[1], device_id=partner, device_id_type=MESH)
    core_copy.start()
    core_copy.wait()

    rows = 32
    chunks = band // rows

    def round_two_sums(i, carry):
        xi, r = i // chunks, lax.rem(i, chunks)
        at = pl.ds(pl.multiple_of(r * rows, rows), rows)
        both = p_ref[c, xi, at, :].astype(jnp.float32) + recv_c[xi, at, :].astype(jnp.float32)
        s1b[xi, at, :] = both.astype(s1b.dtype)
        return carry

    lax.fori_loop(0, n_x * chunks, round_two_sums, 0)
    pieces = x_send.shape[0]
    span = s1b.shape[2] // pieces

    def piece(k):
        return pl.ds(k * span, span)

    def x_stage(k):
        return start_exchange(lambda p: s1b.at[p, :, piece(k)], lambda p: recv_x.at[p, :, piece(k)],
                              x_send.at[k], x_recv.at[k], x_peers, x, lambda p: device(p, zh, c, y, zl))

    def z_stage(k):
        return start_exchange(lambda p: s2.at[p, :, piece(k)], lambda p: recv_z.at[p, :, piece(k)],
                              z_send.at[k], z_recv.at[k], z_peers, z,
                              lambda p: device(x, p // 2, c, y, lax.rem(p, 2)))

    def sum_x(k):
        def body(j, carry):
            at = pl.ds(pl.multiple_of(j * half, half), half)
            total = (p_ref[c, x, at, piece(k)].astype(jnp.float32)
                     + recv_c[x, at, piece(k)].astype(jnp.float32))
            for p in x_peers:
                total = total + recv_x[p, at, piece(k)].astype(jnp.float32)
            s2[j, :, piece(k)] = total.astype(s2.dtype)
            own[j, :, piece(k)] = total
            return carry
        lax.fori_loop(0, n_z, body, 0)

    x_pending = x_stage(0)
    z_pending = []
    for k in range(pieces):
        finish_exchange(x_pending)
        sum_x(k)
        z_pending.append(z_stage(k))
        if k + 1 < pieces:
            x_pending = x_stage(k + 1)
    for pending in z_pending:
        finish_exchange(pending)
    total = own[z]
    for p in z_peers:
        total = total + recv_z[p].astype(jnp.float32)
    s3[...] = total

    def cols(p):
        return pl.ds(pl.multiple_of(p * width, 128), width)

    exchange(lambda p: s3.at[:, cols(p)], lambda p: recv_y.at[p], y_send, y_recv, y_peers, y,
             lambda p: device(x, zh, c, p, zl))
    total = s3[:, cols(y)]
    for p in y_peers:
        total = total + recv_y[p]
    g16[:, cols(y)] = total * scale
    exchange(lambda p: g16.at[:, cols(y)], lambda p: g16.at[:, cols(p)], g_send, g_recv, y_peers, y,
             lambda p: device(x, zh, c, p, zl))
    out_ref[zl] = g16[...]
    pair_copy = pltpu.make_async_remote_copy(
        src_ref=g16, dst_ref=out_ref.at[zl], send_sem=pair_sems.at[0], recv_sem=pair_sems.at[1],
        device_id=device(x, zh, c, y, 1 - zl), device_id_type=MESH)
    pair_copy.start()
    pltpu.make_async_remote_copy(
        src_ref=g16, dst_ref=out_ref.at[1 - zl], send_sem=pair_sems.at[0], recv_sem=pair_sems.at[1],
        device_id=device(x, zh, c, y, 1 - zl), device_id_type=MESH).wait_recv()
    pair_copy.wait_send()
    finish_exchange(back_pending)


def grad_reduce(partial_rows, back, z_hi, scale):
    n_x = partial_rows.shape[1]
    n_y = lax.axis_size("dp") // 2
    cols = partial_rows.shape[3]
    shard = partial_rows.shape[2] // z_hi
    half = shard // 2
    band = partial_rows.shape[2]
    f32 = jnp.float32
    return pl.pallas_call(
        functools.partial(grad_reduce_kernel, z_hi, scale),
        out_shape=(jax.ShapeDtypeStruct((2, half, cols), f32), jax.ShapeDtypeStruct(back.shape, back.dtype)),
        in_specs=[pl.BlockSpec(memory_space=pltpu.VMEM)] * 2,
        out_specs=(pl.BlockSpec(memory_space=pltpu.VMEM),) * 2,
        scratch_shapes=[
            pltpu.VMEM((n_x, band, cols), partial_rows.dtype),
            pltpu.VMEM((n_x, band, cols), partial_rows.dtype),
            pltpu.VMEM((n_x, band, cols), partial_rows.dtype),
            pltpu.VMEM((2 * z_hi, half, cols), partial_rows.dtype),
            pltpu.VMEM((2 * z_hi, half, cols), f32),
            pltpu.VMEM((2 * z_hi, half, cols), partial_rows.dtype),
            pltpu.VMEM((half, cols), f32),
            pltpu.VMEM((n_y, half, cols // n_y), f32),
            pltpu.VMEM((half, cols), f32),
            pltpu.SemaphoreType.DMA((2,)),
            pltpu.SemaphoreType.DMA((PIECES, n_x)),
            pltpu.SemaphoreType.DMA((PIECES, n_x)),
            pltpu.SemaphoreType.DMA((PIECES, 2 * z_hi)),
            pltpu.SemaphoreType.DMA((PIECES, 2 * z_hi)),
            pltpu.SemaphoreType.DMA((n_y,)),
            pltpu.SemaphoreType.DMA((n_y,)),
            pltpu.SemaphoreType.DMA((n_y,)),
            pltpu.SemaphoreType.DMA((n_y,)),
            pltpu.SemaphoreType.DMA((2,)),
            pltpu.SemaphoreType.DMA((2, back.shape[0])),
        ],
        compiler_params=pltpu.CompilerParams(
            collective_id=1, has_side_effects=True, vmem_limit_bytes=48 * 1024 * 1024),
    )(partial_rows, back)


def tap_starts(context_row_block):
    return [context_row_block - (2 - selected_index) * DILATION_SIZE for selected_index in range(3)]


def per_device(signal, grad_gated, conv_weight, source_seg):
    peer_count = lax.axis_size("fsdp")
    seg_count = source_seg.shape[1]
    row_count = signal.shape[0]
    seg_rows = row_count // seg_count
    context_row_block = 2 * DILATION_SIZE
    starts = tap_starts(context_row_block)
    segments = signal.reshape(seg_count, seg_rows, C)
    sources = source_seg[0]
    source_dev = jnp.where(sources >= 0, sources // seg_count, -1)
    peers = jnp.arange(peer_count, dtype=jnp.int32)
    request_mask = (source_dev[None, :] == peers[:, None]).astype(jnp.int32)
    asked = lax.all_to_all(request_mask, "fsdp", split_axis=0, concat_axis=0, tiled=True)
    send_table = asked.astype(jnp.bfloat16)
    recv_table = (source_dev[:, None] == peers[None, :]).astype(jnp.bfloat16)
    outgoing = jnp.einsum(
        "ns,slc->nlc", send_table, segments, preferred_element_type=jnp.float32
    ).astype(jnp.bfloat16)
    incoming = lax.all_to_all(outgoing, "fsdp", split_axis=0, concat_axis=0, tiled=True)
    carries = jnp.einsum(
        "sn,nlc->slc", recv_table, incoming, preferred_element_type=jnp.float32
    ).astype(jnp.bfloat16)
    extended = jnp.concatenate([carries, segments], axis=1)
    full_weight = lax.all_gather(conv_weight, "fsdp", axis=0, tiled=True)
    contract_final_axis = (((1,), (1,)), ((), ()))
    contract_first = (((0,), (0,)), ((), ()))
    windows = [extended[:, start : start + seg_rows, :].reshape(row_count, C) for start in starts]
    preact = sum(
        (
            lax.dot_general(
                windows[selected_index],
                full_weight[:, selected_index * C : (selected_index + 1) * C],
                contract_final_axis,
                preferred_element_type=jnp.float32,
            )
            for selected_index in range(3)
        )
    )
    filter_act = jnp.tanh(preact[:, :H])
    gate_act = jax.nn.sigmoid(preact[:, H:])
    gated_out = (filter_act * gate_act).astype(jnp.bfloat16)
    upstream_wide = grad_gated.astype(jnp.float32)
    grad_pre = jnp.concatenate(
        [
            upstream_wide * gate_act * (1.0 - filter_act * filter_act),
            upstream_wide * filter_act * gate_act * (1.0 - gate_act),
        ],
        axis=1,
    ).astype(jnp.bfloat16)
    z_hi = Z_HI
    n_x = peer_count // (2 * z_hi)
    shard = conv_weight.shape[0]
    routed = (
        grad_pre.reshape(row_count, n_x, z_hi, 2, shard)
        .transpose(0, 3, 1, 2, 4)
        .reshape(row_count, 2 * H)
    )
    stacked = jnp.concatenate(windows, axis=1)
    partial_value = lax.dot_general(
        routed, stacked, contract_first, preferred_element_type=jnp.float32
    ).astype(jnp.bfloat16)
    back_proj = jnp.dot(grad_pre, full_weight, preferred_element_type=jnp.float32)
    back_proj = back_proj.reshape(seg_count, seg_rows, 3 * C)
    grad_ext = jnp.zeros((seg_count, context_row_block + seg_rows, C), jnp.float32)
    for selected_index, start in enumerate(starts):
        grad_ext = grad_ext.at[:, start : start + seg_rows, :].add(
            back_proj[:, :, selected_index * C : (selected_index + 1) * C]
        )
    outgoing_grad = jnp.einsum(
        "sn,slc->nlc",
        recv_table,
        grad_ext[:, :context_row_block, :].astype(jnp.bfloat16),
        preferred_element_type=jnp.float32,
    ).astype(jnp.bfloat16)
    total_token_count = row_count * peer_count * lax.axis_size("dp")
    reduced, incoming_grad = grad_reduce(
        partial_value.reshape(2, n_x, z_hi * shard, 3 * C),
        outgoing_grad,
        z_hi,
        1.0 / math.sqrt(total_token_count),
    )
    grad_weight = reduced.reshape(shard, 3 * C)
    tail_grad = jnp.einsum(
        "ns,nlc->slc",
        send_table,
        incoming_grad,
        preferred_element_type=jnp.float32,
    )
    grad_in = (
        grad_ext[:, context_row_block:, :].at[:, seg_rows - context_row_block :, :].add(tail_grad)
    )
    grad_in = grad_in.reshape(row_count, C).astype(jnp.bfloat16)
    return (gated_out, grad_in, grad_weight)


def solution(mesh):
    placed = (
        P(("dp", "fsdp"), None),
        P(("dp", "fsdp"), None),
        P("fsdp", None),
        P(("dp", "fsdp"), None),
    )
    return jax.shard_map(
        per_device,
        mesh=mesh,
        in_specs=placed,
        out_specs=(P(("dp", "fsdp"), None), P(("dp", "fsdp"), None), P("fsdp", None)),
        check_vma=False,
    )
```

```python
import functools
import math

import jax
import jax.numpy as jnp
from jax import lax
from jax.experimental import pallas as pl
from jax.experimental.pallas import tpu as pltpu
from jax.sharding import PartitionSpec as P

MESH = pl.DeviceIdType.MESH

C = 1024
H = 512
DILATION_SIZE = 4
Z_HI = 4
PIECES = 2


def all_reduce_kernel(axis, n, x_ref, out_ref, gathered, summed, send_sems, recv_sems, out_send, out_recv):
    me = lax.axis_index(axis)
    barrier = pltpu.get_barrier_semaphore()
    for k in range(1, n):
        peer = lax.rem(me + k, n)
        pl.semaphore_signal(barrier, inc=1, device_id={axis: peer}, device_id_type=MESH)
    pl.semaphore_wait(barrier, n - 1)
    sends = []
    for k in range(1, n):
        peer = lax.rem(me + k, n)
        copy = pltpu.make_async_remote_copy(
            src_ref=x_ref.at[peer],
            dst_ref=gathered.at[me],
            send_sem=send_sems.at[peer],
            recv_sem=recv_sems.at[me],
            device_id={axis: peer},
            device_id_type=MESH,
        )
        copy.start()
        sends.append(copy)
    gathered[me] = x_ref[me]
    for k in range(1, n):
        peer = lax.rem(me + k, n)
        pltpu.make_async_remote_copy(
            src_ref=x_ref.at[peer],
            dst_ref=gathered.at[peer],
            send_sem=send_sems.at[peer],
            recv_sem=recv_sems.at[peer],
            device_id={axis: peer},
            device_id_type=MESH,
        ).wait_recv()
    for copy in sends:
        copy.wait_send()
    total = gathered[0]
    for k in range(1, n):
        total = total + gathered[k]
    summed[...] = total
    out_ref[me] = total
    shares = []
    for k in range(1, n):
        peer = lax.rem(me + k, n)
        copy = pltpu.make_async_remote_copy(
            src_ref=summed,
            dst_ref=out_ref.at[me],
            send_sem=out_send.at[peer],
            recv_sem=out_recv.at[me],
            device_id={axis: peer},
            device_id_type=MESH,
        )
        copy.start()
        shares.append(copy)
    for k in range(1, n):
        peer = lax.rem(me + k, n)
        pltpu.make_async_remote_copy(
            src_ref=summed,
            dst_ref=out_ref.at[peer],
            send_sem=out_send.at[peer],
            recv_sem=out_recv.at[peer],
            device_id={axis: peer},
            device_id_type=MESH,
        ).wait_recv()
    for copy in shares:
        copy.wait_send()


def all_reduce(x, axis):
    n = lax.axis_size(axis)
    shape = x.shape
    blocks = x.reshape(n, -1, 128)
    block_shape = blocks.shape[1:]
    out = pl.pallas_call(
        functools.partial(all_reduce_kernel, axis, n),
        out_shape=jax.ShapeDtypeStruct(blocks.shape, x.dtype),
        in_specs=[pl.BlockSpec(memory_space=pltpu.VMEM)],
        out_specs=pl.BlockSpec(memory_space=pltpu.VMEM),
        scratch_shapes=[
            pltpu.VMEM(blocks.shape, x.dtype),
            pltpu.VMEM(block_shape, x.dtype),
            pltpu.SemaphoreType.DMA((n,)),
            pltpu.SemaphoreType.DMA((n,)),
            pltpu.SemaphoreType.DMA((n,)),
            pltpu.SemaphoreType.DMA((n,)),
        ],
        compiler_params=pltpu.CompilerParams(collective_id=0, has_side_effects=True),
    )(blocks)
    return out.reshape(shape)


def grad_reduce_kernel(z_hi, scale, p_ref, back_ref, out_ref, back_out, recv_c, s1b, recv_x, s2, own, recv_z, s3, recv_y, g16,
                       core_sems, x_send, x_recv, z_send, z_recv, y_send, y_recv, g_send, g_recv, pair_sems,
                       back_sems):
    n_x = recv_x.shape[0]
    n_z = 2 * z_hi
    n_y = recv_y.shape[0]
    band = recv_c.shape[1]
    half = s2.shape[1]
    width = recv_y.shape[2]
    f = lax.axis_index("fsdp")
    d = lax.axis_index("dp")
    c = lax.rem(f, 2)
    zh = lax.rem(f // 2, z_hi)
    x = f // (2 * z_hi)
    zl = lax.rem(d, 2)
    y = d // 2
    z = zh * 2 + zl

    def device(x_, zh_, c_, y_, zl_):
        return {"dp": y_ * 2 + zl_, "fsdp": (x_ * z_hi + zh_) * 2 + c_}

    partner = device(x, zh, 1 - c, y, zl)
    x_peers = [lax.rem(x + k, n_x) for k in range(1, n_x)]
    z_peers = [lax.rem(z + k, n_z) for k in range(1, n_z)]
    y_peers = [lax.rem(y + k, n_y) for k in range(1, n_y)]
    n_f = back_ref.shape[0]
    f_peers = [lax.rem(f + k, n_f) for k in range(1, n_f)]
    everyone = [{"dp": d, "fsdp": fp} for fp in f_peers]
    everyone += [device(x, zp // 2, c, y, lax.rem(zp, 2)) for k, zp in enumerate(z_peers, 1) if k % 2]
    everyone += [device(x, zh, c, yp, zl) for yp in y_peers]
    everyone += [device(x, zh, c, yp, 1 - zl) for yp in y_peers]
    barrier = pltpu.get_barrier_semaphore()
    for peer in everyone:
        pl.semaphore_signal(barrier, inc=1, device_id=peer, device_id_type=MESH)
    pl.semaphore_wait(barrier, len(everyone))

    def start_exchange(src_of, dst_of, send_sems, recv_sems, peers, mine, device_of):
        sends, arrivals = [], []
        for p in peers:
            copy = pltpu.make_async_remote_copy(
                src_ref=src_of(p), dst_ref=dst_of(mine), send_sem=send_sems.at[p],
                recv_sem=recv_sems.at[mine], device_id=device_of(p), device_id_type=MESH)
            copy.start()
            sends.append(copy)
            arrivals.append(pltpu.make_async_remote_copy(
                src_ref=src_of(p), dst_ref=dst_of(p), send_sem=send_sems.at[p],
                recv_sem=recv_sems.at[p], device_id=device_of(p), device_id_type=MESH))
        return sends, arrivals

    def finish_exchange(pending):
        sends, arrivals = pending
        for copy in arrivals:
            copy.wait_recv()
        for copy in sends:
            copy.wait_send()

    def exchange(*args):
        finish_exchange(start_exchange(*args))

    back_pending = start_exchange(lambda p: back_ref.at[p], lambda p: back_out.at[p], back_sems.at[0],
                                  back_sems.at[1], f_peers, f, lambda p: {"dp": d, "fsdp": p})
    back_out[f] = back_ref[f]
    core_copy = pltpu.make_async_remote_copy(
        src_ref=p_ref.at[1 - c], dst_ref=recv_c, send_sem=core_sems.at[0],
        recv_sem=core_sems.at[1], device_id=partner, device_id_type=MESH)
    core_copy.start()
    core_copy.wait()

    rows = 32
    chunks = band // rows

    def round_two_sums(i, carry):
        xi, r = i // chunks, lax.rem(i, chunks)
        at = pl.ds(pl.multiple_of(r * rows, rows), rows)
        both = p_ref[c, xi, at, :].astype(jnp.float32) + recv_c[xi, at, :].astype(jnp.float32)
        s1b[xi, at, :] = both.astype(s1b.dtype)
        return carry

    lax.fori_loop(0, n_x * chunks, round_two_sums, 0)
    pieces = x_send.shape[0]
    span = s1b.shape[2] // pieces

    def piece(k):
        return pl.ds(k * span, span)

    def x_stage(k):
        return start_exchange(lambda p: s1b.at[p, :, piece(k)], lambda p: recv_x.at[p, :, piece(k)],
                              x_send.at[k], x_recv.at[k], x_peers, x, lambda p: device(p, zh, c, y, zl))

    def z_stage(k):
        return start_exchange(lambda p: s2.at[p, :, piece(k)], lambda p: recv_z.at[p, :, piece(k)],
                              z_send.at[k], z_recv.at[k], z_peers, z,
                              lambda p: device(x, p // 2, c, y, lax.rem(p, 2)))

    def sum_x(k):
        def body(j, carry):
            at = pl.ds(pl.multiple_of(j * half, half), half)
            total = (p_ref[c, x, at, piece(k)].astype(jnp.float32)
                     + recv_c[x, at, piece(k)].astype(jnp.float32))
            for p in x_peers:
                total = total + recv_x[p, at, piece(k)].astype(jnp.float32)
            s2[j, :, piece(k)] = total.astype(s2.dtype)
            own[j, :, piece(k)] = total
            return carry
        lax.fori_loop(0, n_z, body, 0)

    x_pending = x_stage(0)
    z_pending = []
    for k in range(pieces):
        finish_exchange(x_pending)
        sum_x(k)
        z_pending.append(z_stage(k))
        if k + 1 < pieces:
            x_pending = x_stage(k + 1)
    for pending in z_pending:
        finish_exchange(pending)
    total = own[z]
    for p in z_peers:
        total = total + recv_z[p].astype(jnp.float32)
    s3[...] = total

    def cols(p):
        return pl.ds(pl.multiple_of(p * width, 128), width)

    exchange(lambda p: s3.at[:, cols(p)], lambda p: recv_y.at[p], y_send, y_recv, y_peers, y,
             lambda p: device(x, zh, c, p, zl))
    total = s3[:, cols(y)]
    for p in y_peers:
        total = total + recv_y[p]
    n_dp = g_send.shape[0]
    out_ref[zl, :, cols(y)] = total * scale
    g16[...] = total * scale
    dp_peers = [lax.rem(d + k, n_dp) for k in range(1, n_dp)]
    exchange(lambda q: g16, lambda q: out_ref.at[lax.rem(q, 2), :, cols(q // 2)], g_send, g_recv, dp_peers, d,
             lambda q: {"dp": q, "fsdp": f})
    finish_exchange(back_pending)


def grad_reduce(partial_rows, back, z_hi, scale):
    n_x = partial_rows.shape[1]
    n_y = lax.axis_size("dp") // 2
    cols = partial_rows.shape[3]
    shard = partial_rows.shape[2] // z_hi
    half = shard // 2
    band = partial_rows.shape[2]
    f32 = jnp.float32
    return pl.pallas_call(
        functools.partial(grad_reduce_kernel, z_hi, scale),
        out_shape=(jax.ShapeDtypeStruct((2, half, cols), f32), jax.ShapeDtypeStruct(back.shape, back.dtype)),
        in_specs=[pl.BlockSpec(memory_space=pltpu.VMEM)] * 2,
        out_specs=(pl.BlockSpec(memory_space=pltpu.VMEM),) * 2,
        scratch_shapes=[
            pltpu.VMEM((n_x, band, cols), partial_rows.dtype),
            pltpu.VMEM((n_x, band, cols), partial_rows.dtype),
            pltpu.VMEM((n_x, band, cols), partial_rows.dtype),
            pltpu.VMEM((2 * z_hi, half, cols), partial_rows.dtype),
            pltpu.VMEM((2 * z_hi, half, cols), f32),
            pltpu.VMEM((2 * z_hi, half, cols), partial_rows.dtype),
            pltpu.VMEM((half, cols), f32),
            pltpu.VMEM((n_y, half, cols // n_y), f32),
            pltpu.VMEM((half, cols // n_y), f32),
            pltpu.SemaphoreType.DMA((2,)),
            pltpu.SemaphoreType.DMA((PIECES, n_x)),
            pltpu.SemaphoreType.DMA((PIECES, n_x)),
            pltpu.SemaphoreType.DMA((PIECES, 2 * z_hi)),
            pltpu.SemaphoreType.DMA((PIECES, 2 * z_hi)),
            pltpu.SemaphoreType.DMA((n_y,)),
            pltpu.SemaphoreType.DMA((n_y,)),
            pltpu.SemaphoreType.DMA((2 * n_y,)),
            pltpu.SemaphoreType.DMA((2 * n_y,)),
            pltpu.SemaphoreType.DMA((2,)),
            pltpu.SemaphoreType.DMA((2, back.shape[0])),
        ],
        compiler_params=pltpu.CompilerParams(
            collective_id=1, has_side_effects=True, vmem_limit_bytes=48 * 1024 * 1024),
    )(partial_rows, back)


def tap_starts(context_row_block):
    return [context_row_block - (2 - selected_index) * DILATION_SIZE for selected_index in range(3)]


def per_device(signal, grad_gated, conv_weight, source_seg):
    peer_count = lax.axis_size("fsdp")
    seg_count = source_seg.shape[1]
    row_count = signal.shape[0]
    seg_rows = row_count // seg_count
    context_row_block = 2 * DILATION_SIZE
    starts = tap_starts(context_row_block)
    segments = signal.reshape(seg_count, seg_rows, C)
    sources = source_seg[0]
    source_dev = jnp.where(sources >= 0, sources // seg_count, -1)
    peers = jnp.arange(peer_count, dtype=jnp.int32)
    request_mask = (source_dev[None, :] == peers[:, None]).astype(jnp.int32)
    asked = lax.all_to_all(request_mask, "fsdp", split_axis=0, concat_axis=0, tiled=True)
    send_table = asked.astype(jnp.bfloat16)
    recv_table = (source_dev[:, None] == peers[None, :]).astype(jnp.bfloat16)
    outgoing = jnp.einsum(
        "ns,slc->nlc", send_table, segments, preferred_element_type=jnp.float32
    ).astype(jnp.bfloat16)
    incoming = lax.all_to_all(outgoing, "fsdp", split_axis=0, concat_axis=0, tiled=True)
    carries = jnp.einsum(
        "sn,nlc->slc", recv_table, incoming, preferred_element_type=jnp.float32
    ).astype(jnp.bfloat16)
    extended = jnp.concatenate([carries, segments], axis=1)
    full_weight = lax.all_gather(conv_weight, "fsdp", axis=0, tiled=True)
    contract_final_axis = (((1,), (1,)), ((), ()))
    contract_first = (((0,), (0,)), ((), ()))
    windows = [extended[:, start : start + seg_rows, :].reshape(row_count, C) for start in starts]
    preact = sum(
        (
            lax.dot_general(
                windows[selected_index],
                full_weight[:, selected_index * C : (selected_index + 1) * C],
                contract_final_axis,
                preferred_element_type=jnp.float32,
            )
            for selected_index in range(3)
        )
    )
    filter_act = jnp.tanh(preact[:, :H])
    gate_act = jax.nn.sigmoid(preact[:, H:])
    gated_out = (filter_act * gate_act).astype(jnp.bfloat16)
    upstream_wide = grad_gated.astype(jnp.float32)
    grad_pre = jnp.concatenate(
        [
            upstream_wide * gate_act * (1.0 - filter_act * filter_act),
            upstream_wide * filter_act * gate_act * (1.0 - gate_act),
        ],
        axis=1,
    ).astype(jnp.bfloat16)
    z_hi = Z_HI
    n_x = peer_count // (2 * z_hi)
    shard = conv_weight.shape[0]
    routed = (
        grad_pre.reshape(row_count, n_x, z_hi, 2, shard)
        .transpose(0, 3, 1, 2, 4)
        .reshape(row_count, 2 * H)
    )
    stacked = jnp.concatenate(windows, axis=1)
    partial_value = lax.dot_general(
        routed, stacked, contract_first, preferred_element_type=jnp.float32
    ).astype(jnp.bfloat16)
    back_proj = jnp.dot(grad_pre, full_weight, preferred_element_type=jnp.float32)
    back_proj = back_proj.reshape(seg_count, seg_rows, 3 * C)
    grad_ext = jnp.zeros((seg_count, context_row_block + seg_rows, C), jnp.float32)
    for selected_index, start in enumerate(starts):
        grad_ext = grad_ext.at[:, start : start + seg_rows, :].add(
            back_proj[:, :, selected_index * C : (selected_index + 1) * C]
        )
    outgoing_grad = jnp.einsum(
        "sn,slc->nlc",
        recv_table,
        grad_ext[:, :context_row_block, :].astype(jnp.bfloat16),
        preferred_element_type=jnp.float32,
    ).astype(jnp.bfloat16)
    total_token_count = row_count * peer_count * lax.axis_size("dp")
    reduced, incoming_grad = grad_reduce(
        partial_value.reshape(2, n_x, z_hi * shard, 3 * C),
        outgoing_grad,
        z_hi,
        1.0 / math.sqrt(total_token_count),
    )
    grad_weight = reduced.reshape(shard, 3 * C)
    tail_grad = jnp.einsum(
        "ns,nlc->slc",
        send_table,
        incoming_grad,
        preferred_element_type=jnp.float32,
    )
    grad_in = (
        grad_ext[:, context_row_block:, :].at[:, seg_rows - context_row_block :, :].add(tail_grad)
    )
    grad_in = grad_in.reshape(row_count, C).astype(jnp.bfloat16)
    return (gated_out, grad_in, grad_weight)


def solution(mesh):
    placed = (
        P(("dp", "fsdp"), None),
        P(("dp", "fsdp"), None),
        P("fsdp", None),
        P(("dp", "fsdp"), None),
    )
    return jax.shard_map(
        per_device,
        mesh=mesh,
        in_specs=placed,
        out_specs=(P(("dp", "fsdp"), None), P(("dp", "fsdp"), None), P("fsdp", None)),
        check_vma=False,
    )
```

```python
import functools
import math

import jax
import jax.numpy as jnp
from jax import lax
from jax.experimental import pallas as pl
from jax.experimental.pallas import tpu as pltpu
from jax.sharding import PartitionSpec as P

MESH = pl.DeviceIdType.MESH

C = 1024
H = 512
DILATION_SIZE = 4
Z_HI = 4
PIECES = 2


def all_reduce_kernel(axis, n, x_ref, out_ref, gathered, summed, send_sems, recv_sems, out_send, out_recv):
    me = lax.axis_index(axis)
    barrier = pltpu.get_barrier_semaphore()
    for k in range(1, n):
        peer = lax.rem(me + k, n)
        pl.semaphore_signal(barrier, inc=1, device_id={axis: peer}, device_id_type=MESH)
    pl.semaphore_wait(barrier, n - 1)
    sends = []
    for k in range(1, n):
        peer = lax.rem(me + k, n)
        copy = pltpu.make_async_remote_copy(
            src_ref=x_ref.at[peer],
            dst_ref=gathered.at[me],
            send_sem=send_sems.at[peer],
            recv_sem=recv_sems.at[me],
            device_id={axis: peer},
            device_id_type=MESH,
        )
        copy.start()
        sends.append(copy)
    gathered[me] = x_ref[me]
    for k in range(1, n):
        peer = lax.rem(me + k, n)
        pltpu.make_async_remote_copy(
            src_ref=x_ref.at[peer],
            dst_ref=gathered.at[peer],
            send_sem=send_sems.at[peer],
            recv_sem=recv_sems.at[peer],
            device_id={axis: peer},
            device_id_type=MESH,
        ).wait_recv()
    for copy in sends:
        copy.wait_send()
    total = gathered[0]
    for k in range(1, n):
        total = total + gathered[k]
    summed[...] = total
    out_ref[me] = total
    shares = []
    for k in range(1, n):
        peer = lax.rem(me + k, n)
        copy = pltpu.make_async_remote_copy(
            src_ref=summed,
            dst_ref=out_ref.at[me],
            send_sem=out_send.at[peer],
            recv_sem=out_recv.at[me],
            device_id={axis: peer},
            device_id_type=MESH,
        )
        copy.start()
        shares.append(copy)
    for k in range(1, n):
        peer = lax.rem(me + k, n)
        pltpu.make_async_remote_copy(
            src_ref=summed,
            dst_ref=out_ref.at[peer],
            send_sem=out_send.at[peer],
            recv_sem=out_recv.at[peer],
            device_id={axis: peer},
            device_id_type=MESH,
        ).wait_recv()
    for copy in shares:
        copy.wait_send()


def all_reduce(x, axis):
    n = lax.axis_size(axis)
    shape = x.shape
    blocks = x.reshape(n, -1, 128)
    block_shape = blocks.shape[1:]
    out = pl.pallas_call(
        functools.partial(all_reduce_kernel, axis, n),
        out_shape=jax.ShapeDtypeStruct(blocks.shape, x.dtype),
        in_specs=[pl.BlockSpec(memory_space=pltpu.VMEM)],
        out_specs=pl.BlockSpec(memory_space=pltpu.VMEM),
        scratch_shapes=[
            pltpu.VMEM(blocks.shape, x.dtype),
            pltpu.VMEM(block_shape, x.dtype),
            pltpu.SemaphoreType.DMA((n,)),
            pltpu.SemaphoreType.DMA((n,)),
            pltpu.SemaphoreType.DMA((n,)),
            pltpu.SemaphoreType.DMA((n,)),
        ],
        compiler_params=pltpu.CompilerParams(collective_id=0, has_side_effects=True),
    )(blocks)
    return out.reshape(shape)


def grad_reduce_kernel(z_hi, scale, p_ref, back_ref, out_ref, back_out, recv_c, s1b, recv_x, s2, own, recv_z, s3, recv_y, g16,
                       core_sems, x_send, x_recv, z_send, z_recv, y_send, y_recv, g_send, g_recv, pair_sems,
                       back_sems):
    n_x = recv_x.shape[0]
    n_z = 2 * z_hi
    n_y = recv_y.shape[0]
    band = recv_c.shape[1]
    half = s2.shape[1]
    width = recv_y.shape[2]
    f = lax.axis_index("fsdp")
    d = lax.axis_index("dp")
    c = lax.rem(f, 2)
    zh = lax.rem(f // 2, z_hi)
    x = f // (2 * z_hi)
    zl = lax.rem(d, 2)
    y = d // 2
    z = zh * 2 + zl

    def device(x_, zh_, c_, y_, zl_):
        return {"dp": y_ * 2 + zl_, "fsdp": (x_ * z_hi + zh_) * 2 + c_}

    partner = device(x, zh, 1 - c, y, zl)
    x_peers = [lax.rem(x + k, n_x) for k in range(1, n_x)]
    z_peers = [lax.rem(z + k, n_z) for k in range(1, n_z)]
    y_peers = [lax.rem(y + k, n_y) for k in range(1, n_y)]
    n_f = back_ref.shape[0]
    f_peers = [lax.rem(f + k, n_f) for k in range(1, n_f)]
    everyone = [{"dp": d, "fsdp": fp} for fp in f_peers]
    everyone += [device(x, zp // 2, c, y, lax.rem(zp, 2)) for k, zp in enumerate(z_peers, 1) if k % 2]
    everyone += [device(x, zh, c, yp, zl) for yp in y_peers]
    barrier = pltpu.get_barrier_semaphore()
    for peer in everyone:
        pl.semaphore_signal(barrier, inc=1, device_id=peer, device_id_type=MESH)
    pl.semaphore_wait(barrier, len(everyone))

    def start_exchange(src_of, dst_of, send_sems, recv_sems, peers, mine, device_of):
        sends, arrivals = [], []
        for p in peers:
            copy = pltpu.make_async_remote_copy(
                src_ref=src_of(p), dst_ref=dst_of(mine), send_sem=send_sems.at[p],
                recv_sem=recv_sems.at[mine], device_id=device_of(p), device_id_type=MESH)
            copy.start()
            sends.append(copy)
            arrivals.append(pltpu.make_async_remote_copy(
                src_ref=src_of(p), dst_ref=dst_of(p), send_sem=send_sems.at[p],
                recv_sem=recv_sems.at[p], device_id=device_of(p), device_id_type=MESH))
        return sends, arrivals

    def finish_exchange(pending):
        sends, arrivals = pending
        for copy in arrivals:
            copy.wait_recv()
        for copy in sends:
            copy.wait_send()

    def exchange(*args):
        finish_exchange(start_exchange(*args))

    back_pending = start_exchange(lambda p: back_ref.at[p], lambda p: back_out.at[p], back_sems.at[0],
                                  back_sems.at[1], f_peers, f, lambda p: {"dp": d, "fsdp": p})
    back_out[f] = back_ref[f]
    core_copy = pltpu.make_async_remote_copy(
        src_ref=p_ref.at[1 - c], dst_ref=recv_c, send_sem=core_sems.at[0],
        recv_sem=core_sems.at[1], device_id=partner, device_id_type=MESH)
    core_copy.start()
    core_copy.wait()

    rows = 32
    chunks = band // rows

    def round_two_sums(i, carry):
        xi, r = i // chunks, lax.rem(i, chunks)
        at = pl.ds(pl.multiple_of(r * rows, rows), rows)
        both = p_ref[c, xi, at, :].astype(jnp.float32) + recv_c[xi, at, :].astype(jnp.float32)
        s1b[xi, at, :] = both.astype(s1b.dtype)
        return carry

    lax.fori_loop(0, n_x * chunks, round_two_sums, 0)
    pieces = x_send.shape[0]
    span = s1b.shape[2] // pieces

    def piece(k):
        return pl.ds(k * span, span)

    def x_stage(k):
        return start_exchange(lambda p: s1b.at[p, :, piece(k)], lambda p: recv_x.at[p, :, piece(k)],
                              x_send.at[k], x_recv.at[k], x_peers, x, lambda p: device(p, zh, c, y, zl))

    def z_stage(k):
        return start_exchange(lambda p: s2.at[p, :, piece(k)], lambda p: recv_z.at[p, :, piece(k)],
                              z_send.at[k], z_recv.at[k], z_peers, z,
                              lambda p: device(x, p // 2, c, y, lax.rem(p, 2)))

    def sum_x(k):
        def body(j, carry):
            at = pl.ds(pl.multiple_of(j * half, half), half)
            total = (p_ref[c, x, at, piece(k)].astype(jnp.float32)
                     + recv_c[x, at, piece(k)].astype(jnp.float32))
            for p in x_peers:
                total = total + recv_x[p, at, piece(k)].astype(jnp.float32)
            s2[j, :, piece(k)] = total.astype(s2.dtype)
            own[j, :, piece(k)] = total
            return carry
        lax.fori_loop(0, n_z, body, 0)

    x_pending = x_stage(0)
    z_pending = []
    for k in range(pieces):
        finish_exchange(x_pending)
        sum_x(k)
        z_pending.append(z_stage(k))
        if k + 1 < pieces:
            x_pending = x_stage(k + 1)
    for pending in z_pending:
        finish_exchange(pending)
    total = own[z]
    for p in z_peers:
        total = total + recv_z[p].astype(jnp.float32)
    s3[...] = total

    def cols(p):
        return pl.ds(pl.multiple_of(p * width, 128), width)

    exchange(lambda p: s3.at[:, cols(p)], lambda p: recv_y.at[p], y_send, y_recv, y_peers, y,
             lambda p: device(x, zh, c, p, zl))
    total = s3[:, cols(y)]
    for p in y_peers:
        total = total + recv_y[p]
    g16[:, cols(y)] = total * scale
    exchange(lambda p: g16.at[:, cols(y)], lambda p: g16.at[:, cols(p)], g_send, g_recv, y_peers, y,
             lambda p: device(x, zh, c, p, zl))
    out_ref[zl] = g16[...]
    pair_copy = pltpu.make_async_remote_copy(
        src_ref=g16, dst_ref=out_ref.at[zl], send_sem=pair_sems.at[0], recv_sem=pair_sems.at[1],
        device_id=device(x, zh, c, y, 1 - zl), device_id_type=MESH)
    pair_copy.start()
    pltpu.make_async_remote_copy(
        src_ref=g16, dst_ref=out_ref.at[1 - zl], send_sem=pair_sems.at[0], recv_sem=pair_sems.at[1],
        device_id=device(x, zh, c, y, 1 - zl), device_id_type=MESH).wait_recv()
    pair_copy.wait_send()
    finish_exchange(back_pending)


def grad_reduce(partial_rows, back, z_hi, scale):
    n_x = partial_rows.shape[1]
    n_y = lax.axis_size("dp") // 2
    cols = partial_rows.shape[3]
    shard = partial_rows.shape[2] // z_hi
    half = shard // 2
    band = partial_rows.shape[2]
    f32 = jnp.float32
    return pl.pallas_call(
        functools.partial(grad_reduce_kernel, z_hi, scale),
        out_shape=(jax.ShapeDtypeStruct((2, half, cols), f32), jax.ShapeDtypeStruct(back.shape, back.dtype)),
        in_specs=[pl.BlockSpec(memory_space=pltpu.VMEM)] * 2,
        out_specs=(pl.BlockSpec(memory_space=pltpu.VMEM),) * 2,
        scratch_shapes=[
            pltpu.VMEM((n_x, band, cols), partial_rows.dtype),
            pltpu.VMEM((n_x, band, cols), partial_rows.dtype),
            pltpu.VMEM((n_x, band, cols), partial_rows.dtype),
            pltpu.VMEM((2 * z_hi, half, cols), partial_rows.dtype),
            pltpu.VMEM((2 * z_hi, half, cols), f32),
            pltpu.VMEM((2 * z_hi, half, cols), partial_rows.dtype),
            pltpu.VMEM((half, cols), f32),
            pltpu.VMEM((n_y, half, cols // n_y), f32),
            pltpu.VMEM((half, cols), f32),
            pltpu.SemaphoreType.DMA((2,)),
            pltpu.SemaphoreType.DMA((PIECES, n_x)),
            pltpu.SemaphoreType.DMA((PIECES, n_x)),
            pltpu.SemaphoreType.DMA((PIECES, 2 * z_hi)),
            pltpu.SemaphoreType.DMA((PIECES, 2 * z_hi)),
            pltpu.SemaphoreType.DMA((n_y,)),
            pltpu.SemaphoreType.DMA((n_y,)),
            pltpu.SemaphoreType.DMA((n_y,)),
            pltpu.SemaphoreType.DMA((n_y,)),
            pltpu.SemaphoreType.DMA((2,)),
            pltpu.SemaphoreType.DMA((2, back.shape[0])),
        ],
        compiler_params=pltpu.CompilerParams(
            collective_id=1, has_side_effects=True, vmem_limit_bytes=48 * 1024 * 1024),
    )(partial_rows, back)


def tap_starts(context_row_block):
    return [context_row_block - (2 - selected_index) * DILATION_SIZE for selected_index in range(3)]


def per_device(signal, grad_gated, conv_weight, source_seg):
    peer_count = lax.axis_size("fsdp")
    seg_count = source_seg.shape[1]
    row_count = signal.shape[0]
    seg_rows = row_count // seg_count
    context_row_block = 2 * DILATION_SIZE
    starts = tap_starts(context_row_block)
    segments = signal.reshape(seg_count, seg_rows, C)
    sources = source_seg[0]
    source_dev = jnp.where(sources >= 0, sources // seg_count, -1)
    peers = jnp.arange(peer_count, dtype=jnp.int32)
    request_mask = (source_dev[None, :] == peers[:, None]).astype(jnp.int32)
    asked = lax.all_to_all(request_mask, "fsdp", split_axis=0, concat_axis=0, tiled=True)
    send_table = asked.astype(jnp.bfloat16)
    recv_table = (source_dev[:, None] == peers[None, :]).astype(jnp.bfloat16)
    outgoing = jnp.einsum(
        "ns,slc->nlc", send_table, segments, preferred_element_type=jnp.float32
    ).astype(jnp.bfloat16)
    incoming = lax.all_to_all(outgoing, "fsdp", split_axis=0, concat_axis=0, tiled=True)
    carries = jnp.einsum(
        "sn,nlc->slc", recv_table, incoming, preferred_element_type=jnp.float32
    ).astype(jnp.bfloat16)
    extended = jnp.concatenate([carries, segments], axis=1)
    full_weight = lax.all_gather(conv_weight, "fsdp", axis=0, tiled=True)
    contract_final_axis = (((1,), (1,)), ((), ()))
    contract_first = (((0,), (0,)), ((), ()))
    windows = [extended[:, start : start + seg_rows, :].reshape(row_count, C) for start in starts]
    stacked = jnp.concatenate(windows, axis=1)
    preact = lax.dot_general(
        stacked, full_weight, contract_final_axis, preferred_element_type=jnp.float32
    )
    filter_act = jnp.tanh(preact[:, :H])
    gate_act = jax.nn.sigmoid(preact[:, H:])
    gated_out = (filter_act * gate_act).astype(jnp.bfloat16)
    upstream_wide = grad_gated.astype(jnp.float32)
    grad_pre = jnp.concatenate(
        [
            upstream_wide * gate_act * (1.0 - filter_act * filter_act),
            upstream_wide * filter_act * gate_act * (1.0 - gate_act),
        ],
        axis=1,
    ).astype(jnp.bfloat16)
    z_hi = Z_HI
    n_x = peer_count // (2 * z_hi)
    shard = conv_weight.shape[0]
    routed = (
        grad_pre.reshape(row_count, n_x, z_hi, 2, shard)
        .transpose(0, 3, 1, 2, 4)
        .reshape(row_count, 2 * H)
    )
    partial_value = lax.dot_general(
        routed, stacked, contract_first, preferred_element_type=jnp.float32
    ).astype(jnp.bfloat16)
    back_proj = jnp.dot(grad_pre, full_weight, preferred_element_type=jnp.float32)
    back_proj = back_proj.reshape(seg_count, seg_rows, 3 * C)
    grad_ext = jnp.zeros((seg_count, context_row_block + seg_rows, C), jnp.float32)
    for selected_index, start in enumerate(starts):
        grad_ext = grad_ext.at[:, start : start + seg_rows, :].add(
            back_proj[:, :, selected_index * C : (selected_index + 1) * C]
        )
    outgoing_grad = jnp.einsum(
        "sn,slc->nlc",
        recv_table,
        grad_ext[:, :context_row_block, :].astype(jnp.bfloat16),
        preferred_element_type=jnp.float32,
    ).astype(jnp.bfloat16)
    total_token_count = row_count * peer_count * lax.axis_size("dp")
    reduced, incoming_grad = grad_reduce(
        partial_value.reshape(2, n_x, z_hi * shard, 3 * C),
        outgoing_grad,
        z_hi,
        1.0 / math.sqrt(total_token_count),
    )
    grad_weight = reduced.reshape(shard, 3 * C)
    tail_grad = jnp.einsum(
        "ns,nlc->slc",
        send_table,
        incoming_grad,
        preferred_element_type=jnp.float32,
    )
    grad_in = (
        grad_ext[:, context_row_block:, :].at[:, seg_rows - context_row_block :, :].add(tail_grad)
    )
    grad_in = grad_in.reshape(row_count, C).astype(jnp.bfloat16)
    return (gated_out, grad_in, grad_weight)


def solution(mesh):
    placed = (
        P(("dp", "fsdp"), None),
        P(("dp", "fsdp"), None),
        P("fsdp", None),
        P(("dp", "fsdp"), None),
    )
    return jax.shard_map(
        per_device,
        mesh=mesh,
        in_specs=placed,
        out_specs=(P(("dp", "fsdp"), None), P(("dp", "fsdp"), None), P("fsdp", None)),
        check_vma=False,
    )
```

```python
import functools
import math

import jax
import jax.numpy as jnp
from jax import lax
from jax.experimental import pallas as pl
from jax.experimental.pallas import tpu as pltpu
from jax.sharding import PartitionSpec as P

MESH = pl.DeviceIdType.MESH

C = 1024
H = 512
DILATION_SIZE = 4
Z_HI = 4
PIECES = 2


def all_reduce_kernel(axis, n, x_ref, out_ref, gathered, summed, send_sems, recv_sems, out_send, out_recv):
    me = lax.axis_index(axis)
    barrier = pltpu.get_barrier_semaphore()
    for k in range(1, n):
        peer = lax.rem(me + k, n)
        pl.semaphore_signal(barrier, inc=1, device_id={axis: peer}, device_id_type=MESH)
    pl.semaphore_wait(barrier, n - 1)
    sends = []
    for k in range(1, n):
        peer = lax.rem(me + k, n)
        copy = pltpu.make_async_remote_copy(
            src_ref=x_ref.at[peer],
            dst_ref=gathered.at[me],
            send_sem=send_sems.at[peer],
            recv_sem=recv_sems.at[me],
            device_id={axis: peer},
            device_id_type=MESH,
        )
        copy.start()
        sends.append(copy)
    gathered[me] = x_ref[me]
    for k in range(1, n):
        peer = lax.rem(me + k, n)
        pltpu.make_async_remote_copy(
            src_ref=x_ref.at[peer],
            dst_ref=gathered.at[peer],
            send_sem=send_sems.at[peer],
            recv_sem=recv_sems.at[peer],
            device_id={axis: peer},
            device_id_type=MESH,
        ).wait_recv()
    for copy in sends:
        copy.wait_send()
    total = gathered[0]
    for k in range(1, n):
        total = total + gathered[k]
    summed[...] = total
    out_ref[me] = total
    shares = []
    for k in range(1, n):
        peer = lax.rem(me + k, n)
        copy = pltpu.make_async_remote_copy(
            src_ref=summed,
            dst_ref=out_ref.at[me],
            send_sem=out_send.at[peer],
            recv_sem=out_recv.at[me],
            device_id={axis: peer},
            device_id_type=MESH,
        )
        copy.start()
        shares.append(copy)
    for k in range(1, n):
        peer = lax.rem(me + k, n)
        pltpu.make_async_remote_copy(
            src_ref=summed,
            dst_ref=out_ref.at[peer],
            send_sem=out_send.at[peer],
            recv_sem=out_recv.at[peer],
            device_id={axis: peer},
            device_id_type=MESH,
        ).wait_recv()
    for copy in shares:
        copy.wait_send()


def all_reduce(x, axis):
    n = lax.axis_size(axis)
    shape = x.shape
    blocks = x.reshape(n, -1, 128)
    block_shape = blocks.shape[1:]
    out = pl.pallas_call(
        functools.partial(all_reduce_kernel, axis, n),
        out_shape=jax.ShapeDtypeStruct(blocks.shape, x.dtype),
        in_specs=[pl.BlockSpec(memory_space=pltpu.VMEM)],
        out_specs=pl.BlockSpec(memory_space=pltpu.VMEM),
        scratch_shapes=[
            pltpu.VMEM(blocks.shape, x.dtype),
            pltpu.VMEM(block_shape, x.dtype),
            pltpu.SemaphoreType.DMA((n,)),
            pltpu.SemaphoreType.DMA((n,)),
            pltpu.SemaphoreType.DMA((n,)),
            pltpu.SemaphoreType.DMA((n,)),
        ],
        compiler_params=pltpu.CompilerParams(collective_id=0, has_side_effects=True),
    )(blocks)
    return out.reshape(shape)


def grad_reduce_kernel(z_hi, scale, p_ref, back_ref, out_ref, back_out, recv_c, s1b, recv_x, s2, own, recv_z, s3, recv_y, g16,
                       core_sems, x_send, x_recv, z_send, z_recv, y_send, y_recv, g_send, g_recv, pair_sems,
                       back_sems):
    n_x = recv_x.shape[0]
    n_z = 2 * z_hi
    n_y = recv_y.shape[0]
    band = recv_c.shape[1]
    half = s2.shape[1]
    width = recv_y.shape[2]
    f = lax.axis_index("fsdp")
    d = lax.axis_index("dp")
    c = lax.rem(f, 2)
    zh = lax.rem(f // 2, z_hi)
    x = f // (2 * z_hi)
    zl = lax.rem(d, 2)
    y = d // 2
    z = zh * 2 + zl

    def device(x_, zh_, c_, y_, zl_):
        return {"dp": y_ * 2 + zl_, "fsdp": (x_ * z_hi + zh_) * 2 + c_}

    partner = device(x, zh, 1 - c, y, zl)
    x_peers = [lax.rem(x + k, n_x) for k in range(1, n_x)]
    z_peers = [lax.rem(z + k, n_z) for k in range(1, n_z)]
    y_peers = [lax.rem(y + k, n_y) for k in range(1, n_y)]
    n_f = back_ref.shape[0]
    f_peers = [lax.rem(f + k, n_f) for k in range(1, n_f)]
    everyone = [{"dp": d, "fsdp": fp} for fp in f_peers]
    everyone += [device(x, zp // 2, c, y, lax.rem(zp, 2)) for k, zp in enumerate(z_peers, 1) if k % 2]
    everyone += [device(x, zh, c, yp, zl) for yp in y_peers]
    barrier = pltpu.get_barrier_semaphore()
    for peer in everyone:
        pl.semaphore_signal(barrier, inc=1, device_id=peer, device_id_type=MESH)
    pl.semaphore_wait(barrier, len(everyone))

    def start_exchange(src_of, dst_of, send_sems, recv_sems, peers, mine, device_of):
        sends, arrivals = [], []
        for p in peers:
            copy = pltpu.make_async_remote_copy(
                src_ref=src_of(p), dst_ref=dst_of(mine), send_sem=send_sems.at[p],
                recv_sem=recv_sems.at[mine], device_id=device_of(p), device_id_type=MESH)
            copy.start()
            sends.append(copy)
            arrivals.append(pltpu.make_async_remote_copy(
                src_ref=src_of(p), dst_ref=dst_of(p), send_sem=send_sems.at[p],
                recv_sem=recv_sems.at[p], device_id=device_of(p), device_id_type=MESH))
        return sends, arrivals

    def finish_exchange(pending):
        sends, arrivals = pending
        for copy in arrivals:
            copy.wait_recv()
        for copy in sends:
            copy.wait_send()

    def exchange(*args):
        finish_exchange(start_exchange(*args))

    back_pending = start_exchange(lambda p: back_ref.at[p], lambda p: back_out.at[p], back_sems.at[0],
                                  back_sems.at[1], f_peers, f, lambda p: {"dp": d, "fsdp": p})
    back_out[f] = back_ref[f]
    rows = 32
    chunks = band // rows

    pieces = x_send.shape[0]
    span = s1b.shape[2] // pieces

    def piece(k):
        return pl.ds(k * span, span)

    def core_stage(k):
        copy = pltpu.make_async_remote_copy(
            src_ref=p_ref.at[1 - c, :, :, piece(k)], dst_ref=recv_c.at[:, :, piece(k)],
            send_sem=core_sems.at[0, k], recv_sem=core_sems.at[1, k], device_id=partner,
            device_id_type=MESH)
        copy.start()
        return copy

    def round_two_sums(k):
        def body(i, carry):
            xi, r = i // chunks, lax.rem(i, chunks)
            at = pl.ds(pl.multiple_of(r * rows, rows), rows)
            both = (p_ref[c, xi, at, piece(k)].astype(jnp.float32)
                    + recv_c[xi, at, piece(k)].astype(jnp.float32))
            s1b[xi, at, piece(k)] = both.astype(s1b.dtype)
            return carry
        lax.fori_loop(0, n_x * chunks, body, 0)

    def x_stage(k):
        return start_exchange(lambda p: s1b.at[p, :, piece(k)], lambda p: recv_x.at[p, :, piece(k)],
                              x_send.at[k], x_recv.at[k], x_peers, x, lambda p: device(p, zh, c, y, zl))

    def z_stage(k):
        return start_exchange(lambda p: s2.at[p, :, piece(k)], lambda p: recv_z.at[p, :, piece(k)],
                              z_send.at[k], z_recv.at[k], z_peers, z,
                              lambda p: device(x, p // 2, c, y, lax.rem(p, 2)))

    def sum_x(k):
        def body(j, carry):
            at = pl.ds(pl.multiple_of(j * half, half), half)
            total = (p_ref[c, x, at, piece(k)].astype(jnp.float32)
                     + recv_c[x, at, piece(k)].astype(jnp.float32))
            for p in x_peers:
                total = total + recv_x[p, at, piece(k)].astype(jnp.float32)
            s2[j, :, piece(k)] = total.astype(s2.dtype)
            own[j, :, piece(k)] = total
            return carry
        lax.fori_loop(0, n_z, body, 0)

    core_copy = core_stage(0)
    core_copy.wait()
    round_two_sums(0)
    x_pending = x_stage(0)
    if pieces > 1:
        core_copy = core_stage(1)
    z_pending = []
    for k in range(pieces):
        if k + 1 < pieces:
            core_copy.wait()
            round_two_sums(k + 1)
        finish_exchange(x_pending)
        sum_x(k)
        z_pending.append(z_stage(k))
        if k + 1 < pieces:
            x_pending = x_stage(k + 1)
            if k + 2 < pieces:
                core_copy = core_stage(k + 2)
    for pending in z_pending:
        finish_exchange(pending)
    total = own[z]
    for p in z_peers:
        total = total + recv_z[p].astype(jnp.float32)
    s3[...] = total

    def cols(p):
        return pl.ds(pl.multiple_of(p * width, 128), width)

    exchange(lambda p: s3.at[:, cols(p)], lambda p: recv_y.at[p], y_send, y_recv, y_peers, y,
             lambda p: device(x, zh, c, p, zl))
    total = s3[:, cols(y)]
    for p in y_peers:
        total = total + recv_y[p]
    g16[:, cols(y)] = total * scale
    exchange(lambda p: g16.at[:, cols(y)], lambda p: g16.at[:, cols(p)], g_send, g_recv, y_peers, y,
             lambda p: device(x, zh, c, p, zl))
    out_ref[zl] = g16[...]
    pair_copy = pltpu.make_async_remote_copy(
        src_ref=g16, dst_ref=out_ref.at[zl], send_sem=pair_sems.at[0], recv_sem=pair_sems.at[1],
        device_id=device(x, zh, c, y, 1 - zl), device_id_type=MESH)
    pair_copy.start()
    pltpu.make_async_remote_copy(
        src_ref=g16, dst_ref=out_ref.at[1 - zl], send_sem=pair_sems.at[0], recv_sem=pair_sems.at[1],
        device_id=device(x, zh, c, y, 1 - zl), device_id_type=MESH).wait_recv()
    pair_copy.wait_send()
    finish_exchange(back_pending)


def grad_reduce(partial_rows, back, z_hi, scale):
    n_x = partial_rows.shape[1]
    n_y = lax.axis_size("dp") // 2
    cols = partial_rows.shape[3]
    shard = partial_rows.shape[2] // z_hi
    half = shard // 2
    band = partial_rows.shape[2]
    f32 = jnp.float32
    return pl.pallas_call(
        functools.partial(grad_reduce_kernel, z_hi, scale),
        out_shape=(jax.ShapeDtypeStruct((2, half, cols), f32), jax.ShapeDtypeStruct(back.shape, back.dtype)),
        in_specs=[pl.BlockSpec(memory_space=pltpu.VMEM)] * 2,
        out_specs=(pl.BlockSpec(memory_space=pltpu.VMEM),) * 2,
        scratch_shapes=[
            pltpu.VMEM((n_x, band, cols), partial_rows.dtype),
            pltpu.VMEM((n_x, band, cols), partial_rows.dtype),
            pltpu.VMEM((n_x, band, cols), partial_rows.dtype),
            pltpu.VMEM((2 * z_hi, half, cols), partial_rows.dtype),
            pltpu.VMEM((2 * z_hi, half, cols), f32),
            pltpu.VMEM((2 * z_hi, half, cols), partial_rows.dtype),
            pltpu.VMEM((half, cols), f32),
            pltpu.VMEM((n_y, half, cols // n_y), f32),
            pltpu.VMEM((half, cols), f32),
            pltpu.SemaphoreType.DMA((2, PIECES)),
            pltpu.SemaphoreType.DMA((PIECES, n_x)),
            pltpu.SemaphoreType.DMA((PIECES, n_x)),
            pltpu.SemaphoreType.DMA((PIECES, 2 * z_hi)),
            pltpu.SemaphoreType.DMA((PIECES, 2 * z_hi)),
            pltpu.SemaphoreType.DMA((n_y,)),
            pltpu.SemaphoreType.DMA((n_y,)),
            pltpu.SemaphoreType.DMA((n_y,)),
            pltpu.SemaphoreType.DMA((n_y,)),
            pltpu.SemaphoreType.DMA((2,)),
            pltpu.SemaphoreType.DMA((2, back.shape[0])),
        ],
        compiler_params=pltpu.CompilerParams(
            collective_id=1, has_side_effects=True, vmem_limit_bytes=48 * 1024 * 1024),
    )(partial_rows, back)


def tap_starts(context_row_block):
    return [context_row_block - (2 - selected_index) * DILATION_SIZE for selected_index in range(3)]


def per_device(signal, grad_gated, conv_weight, source_seg):
    peer_count = lax.axis_size("fsdp")
    seg_count = source_seg.shape[1]
    row_count = signal.shape[0]
    seg_rows = row_count // seg_count
    context_row_block = 2 * DILATION_SIZE
    starts = tap_starts(context_row_block)
    segments = signal.reshape(seg_count, seg_rows, C)
    sources = source_seg[0]
    source_dev = jnp.where(sources >= 0, sources // seg_count, -1)
    peers = jnp.arange(peer_count, dtype=jnp.int32)
    request_mask = (source_dev[None, :] == peers[:, None]).astype(jnp.int32)
    asked = lax.all_to_all(request_mask, "fsdp", split_axis=0, concat_axis=0, tiled=True)
    send_table = asked.astype(jnp.bfloat16)
    recv_table = (source_dev[:, None] == peers[None, :]).astype(jnp.bfloat16)
    outgoing = jnp.einsum(
        "ns,slc->nlc", send_table, segments, preferred_element_type=jnp.float32
    ).astype(jnp.bfloat16)
    incoming = lax.all_to_all(outgoing, "fsdp", split_axis=0, concat_axis=0, tiled=True)
    carries = jnp.einsum(
        "sn,nlc->slc", recv_table, incoming, preferred_element_type=jnp.float32
    ).astype(jnp.bfloat16)
    extended = jnp.concatenate([carries, segments], axis=1)
    full_weight = lax.all_gather(conv_weight, "fsdp", axis=0, tiled=True)
    contract_final_axis = (((1,), (1,)), ((), ()))
    contract_first = (((0,), (0,)), ((), ()))
    windows = [extended[:, start : start + seg_rows, :].reshape(row_count, C) for start in starts]
    stacked = jnp.concatenate(windows, axis=1)
    preact = lax.dot_general(
        stacked, full_weight, contract_final_axis, preferred_element_type=jnp.float32
    )
    filter_act = jnp.tanh(preact[:, :H])
    gate_act = jax.nn.sigmoid(preact[:, H:])
    gated_out = (filter_act * gate_act).astype(jnp.bfloat16)
    upstream_wide = grad_gated.astype(jnp.float32)
    grad_pre = jnp.concatenate(
        [
            upstream_wide * gate_act * (1.0 - filter_act * filter_act),
            upstream_wide * filter_act * gate_act * (1.0 - gate_act),
        ],
        axis=1,
    ).astype(jnp.bfloat16)
    z_hi = Z_HI
    n_x = peer_count // (2 * z_hi)
    shard = conv_weight.shape[0]
    routed = (
        grad_pre.reshape(row_count, n_x, z_hi, 2, shard)
        .transpose(0, 3, 1, 2, 4)
        .reshape(row_count, 2 * H)
    )
    partial_value = lax.dot_general(
        routed, stacked, contract_first, preferred_element_type=jnp.float32
    ).astype(jnp.bfloat16)
    back_proj = jnp.dot(grad_pre, full_weight, preferred_element_type=jnp.float32)
    back_proj = back_proj.reshape(seg_count, seg_rows, 3 * C)
    grad_ext = jnp.zeros((seg_count, context_row_block + seg_rows, C), jnp.float32)
    for selected_index, start in enumerate(starts):
        grad_ext = grad_ext.at[:, start : start + seg_rows, :].add(
            back_proj[:, :, selected_index * C : (selected_index + 1) * C]
        )
    outgoing_grad = jnp.einsum(
        "sn,slc->nlc",
        recv_table,
        grad_ext[:, :context_row_block, :].astype(jnp.bfloat16),
        preferred_element_type=jnp.float32,
    ).astype(jnp.bfloat16)
    total_token_count = row_count * peer_count * lax.axis_size("dp")
    reduced, incoming_grad = grad_reduce(
        partial_value.reshape(2, n_x, z_hi * shard, 3 * C),
        outgoing_grad,
        z_hi,
        1.0 / math.sqrt(total_token_count),
    )
    grad_weight = reduced.reshape(shard, 3 * C)
    tail_grad = jnp.einsum(
        "ns,nlc->slc",
        send_table,
        incoming_grad,
        preferred_element_type=jnp.float32,
    )
    grad_in = (
        grad_ext[:, context_row_block:, :].at[:, seg_rows - context_row_block :, :].add(tail_grad)
    )
    grad_in = grad_in.reshape(row_count, C).astype(jnp.bfloat16)
    return (gated_out, grad_in, grad_weight)


def solution(mesh):
    placed = (
        P(("dp", "fsdp"), None),
        P(("dp", "fsdp"), None),
        P("fsdp", None),
        P(("dp", "fsdp"), None),
    )
    return jax.shard_map(
        per_device,
        mesh=mesh,
        in_specs=placed,
        out_specs=(P(("dp", "fsdp"), None), P(("dp", "fsdp"), None), P("fsdp", None)),
        check_vma=False,
    )
```

```python
import functools
import math

import jax
import jax.numpy as jnp
from jax import lax
from jax.experimental import pallas as pl
from jax.experimental.pallas import tpu as pltpu
from jax.sharding import PartitionSpec as P

MESH = pl.DeviceIdType.MESH

C = 1024
H = 512
DILATION_SIZE = 4
Z_HI = 4
PIECES = 2


def all_reduce_kernel(axis, n, x_ref, out_ref, gathered, summed, send_sems, recv_sems, out_send, out_recv):
    me = lax.axis_index(axis)
    barrier = pltpu.get_barrier_semaphore()
    for k in range(1, n):
        peer = lax.rem(me + k, n)
        pl.semaphore_signal(barrier, inc=1, device_id={axis: peer}, device_id_type=MESH)
    pl.semaphore_wait(barrier, n - 1)
    sends = []
    for k in range(1, n):
        peer = lax.rem(me + k, n)
        copy = pltpu.make_async_remote_copy(
            src_ref=x_ref.at[peer],
            dst_ref=gathered.at[me],
            send_sem=send_sems.at[peer],
            recv_sem=recv_sems.at[me],
            device_id={axis: peer},
            device_id_type=MESH,
        )
        copy.start()
        sends.append(copy)
    gathered[me] = x_ref[me]
    for k in range(1, n):
        peer = lax.rem(me + k, n)
        pltpu.make_async_remote_copy(
            src_ref=x_ref.at[peer],
            dst_ref=gathered.at[peer],
            send_sem=send_sems.at[peer],
            recv_sem=recv_sems.at[peer],
            device_id={axis: peer},
            device_id_type=MESH,
        ).wait_recv()
    for copy in sends:
        copy.wait_send()
    total = gathered[0]
    for k in range(1, n):
        total = total + gathered[k]
    summed[...] = total
    out_ref[me] = total
    shares = []
    for k in range(1, n):
        peer = lax.rem(me + k, n)
        copy = pltpu.make_async_remote_copy(
            src_ref=summed,
            dst_ref=out_ref.at[me],
            send_sem=out_send.at[peer],
            recv_sem=out_recv.at[me],
            device_id={axis: peer},
            device_id_type=MESH,
        )
        copy.start()
        shares.append(copy)
    for k in range(1, n):
        peer = lax.rem(me + k, n)
        pltpu.make_async_remote_copy(
            src_ref=summed,
            dst_ref=out_ref.at[peer],
            send_sem=out_send.at[peer],
            recv_sem=out_recv.at[peer],
            device_id={axis: peer},
            device_id_type=MESH,
        ).wait_recv()
    for copy in shares:
        copy.wait_send()


def all_reduce(x, axis):
    n = lax.axis_size(axis)
    shape = x.shape
    blocks = x.reshape(n, -1, 128)
    block_shape = blocks.shape[1:]
    out = pl.pallas_call(
        functools.partial(all_reduce_kernel, axis, n),
        out_shape=jax.ShapeDtypeStruct(blocks.shape, x.dtype),
        in_specs=[pl.BlockSpec(memory_space=pltpu.VMEM)],
        out_specs=pl.BlockSpec(memory_space=pltpu.VMEM),
        scratch_shapes=[
            pltpu.VMEM(blocks.shape, x.dtype),
            pltpu.VMEM(block_shape, x.dtype),
            pltpu.SemaphoreType.DMA((n,)),
            pltpu.SemaphoreType.DMA((n,)),
            pltpu.SemaphoreType.DMA((n,)),
            pltpu.SemaphoreType.DMA((n,)),
        ],
        compiler_params=pltpu.CompilerParams(collective_id=0, has_side_effects=True),
    )(blocks)
    return out.reshape(shape)


def grad_reduce_kernel(z_hi, scale, p_ref, back_ref, out_ref, back_out, recv_c, s1b, recv_x, s2, own, recv_z, s3, recv_y, g16,
                       core_sems, x_send, x_recv, z_send, z_recv, y_send, y_recv, g_send, g_recv, pair_sems,
                       back_sems):
    n_x = recv_x.shape[0]
    n_z = 2 * z_hi
    n_y = recv_y.shape[0]
    band = recv_c.shape[1]
    half = s2.shape[1]
    width = recv_y.shape[2]
    f = lax.axis_index("fsdp")
    d = lax.axis_index("dp")
    c = lax.rem(f, 2)
    zh = lax.rem(f // 2, z_hi)
    x = f // (2 * z_hi)
    zl = lax.rem(d, 2)
    y = d // 2
    z = zh * 2 + zl

    def device(x_, zh_, c_, y_, zl_):
        return {"dp": y_ * 2 + zl_, "fsdp": (x_ * z_hi + zh_) * 2 + c_}

    partner = device(x, zh, 1 - c, y, zl)
    x_peers = [lax.rem(x + k, n_x) for k in range(1, n_x)]
    z_peers = [lax.rem(z + k, n_z) for k in range(1, n_z)]
    y_peers = [lax.rem(y + k, n_y) for k in range(1, n_y)]
    n_f = back_ref.shape[0]
    f_peers = [lax.rem(f + k, n_f) for k in range(1, n_f)]
    everyone = [{"dp": d, "fsdp": fp} for fp in f_peers]
    everyone += [device(x, zp // 2, c, y, lax.rem(zp, 2)) for k, zp in enumerate(z_peers, 1) if k % 2]
    everyone += [device(x, zh, c, yp, zl) for yp in y_peers]
    barrier = pltpu.get_barrier_semaphore()
    for peer in everyone:
        pl.semaphore_signal(barrier, inc=1, device_id=peer, device_id_type=MESH)
    pl.semaphore_wait(barrier, len(everyone))

    def start_exchange(src_of, dst_of, send_sems, recv_sems, peers, mine, device_of):
        sends, arrivals = [], []
        for p in peers:
            copy = pltpu.make_async_remote_copy(
                src_ref=src_of(p), dst_ref=dst_of(mine), send_sem=send_sems.at[p],
                recv_sem=recv_sems.at[mine], device_id=device_of(p), device_id_type=MESH)
            copy.start()
            sends.append(copy)
            arrivals.append(pltpu.make_async_remote_copy(
                src_ref=src_of(p), dst_ref=dst_of(p), send_sem=send_sems.at[p],
                recv_sem=recv_sems.at[p], device_id=device_of(p), device_id_type=MESH))
        return sends, arrivals

    def finish_exchange(pending):
        sends, arrivals = pending
        for copy in arrivals:
            copy.wait_recv()
        for copy in sends:
            copy.wait_send()

    def exchange(*args):
        finish_exchange(start_exchange(*args))

    back_pending = start_exchange(lambda p: back_ref.at[p], lambda p: back_out.at[p], back_sems.at[0],
                                  back_sems.at[1], f_peers, f, lambda p: {"dp": d, "fsdp": p})
    back_out[f] = back_ref[f]
    rows = 32
    chunks = band // rows

    pieces = x_send.shape[0]
    span = s1b.shape[2] // pieces

    def piece(k):
        return pl.ds(k * span, span)

    def core_stage(k):
        copy = pltpu.make_async_remote_copy(
            src_ref=p_ref.at[1 - c, :, :, piece(k)], dst_ref=recv_c.at[:, :, piece(k)],
            send_sem=core_sems.at[0, k], recv_sem=core_sems.at[1, k], device_id=partner,
            device_id_type=MESH)
        copy.start()
        return copy

    def round_two_sums(k):
        def body(i, carry):
            xi, r = i // chunks, lax.rem(i, chunks)
            at = pl.ds(pl.multiple_of(r * rows, rows), rows)
            both = (p_ref[c, xi, at, piece(k)].astype(jnp.float32)
                    + recv_c[xi, at, piece(k)].astype(jnp.float32))
            s1b[xi, at, piece(k)] = both.astype(s1b.dtype)
            return carry
        lax.fori_loop(0, n_x * chunks, body, 0)

    def x_stage(k):
        return start_exchange(lambda p: s1b.at[p, :, piece(k)], lambda p: recv_x.at[p, :, piece(k)],
                              x_send.at[k], x_recv.at[k], x_peers, x, lambda p: device(p, zh, c, y, zl))

    def z_stage(k):
        return start_exchange(lambda p: s2.at[p, :, piece(k)], lambda p: recv_z.at[p, :, piece(k)],
                              z_send.at[k], z_recv.at[k], z_peers, z,
                              lambda p: device(x, p // 2, c, y, lax.rem(p, 2)))

    def sum_x(k):
        def body(j, carry):
            at = pl.ds(pl.multiple_of(j * half, half), half)
            total = (p_ref[c, x, at, piece(k)].astype(jnp.float32)
                     + recv_c[x, at, piece(k)].astype(jnp.float32))
            for p in x_peers:
                total = total + recv_x[p, at, piece(k)].astype(jnp.float32)
            s2[j, :, piece(k)] = total.astype(s2.dtype)
            own[j, :, piece(k)] = total
            return carry
        lax.fori_loop(0, n_z, body, 0)

    core_copy = core_stage(0)
    core_copy.wait()
    round_two_sums(0)
    x_pending = x_stage(0)
    if pieces > 1:
        core_copy = core_stage(1)
    z_pending = []
    for k in range(pieces):
        if k + 1 < pieces:
            core_copy.wait()
            round_two_sums(k + 1)
        finish_exchange(x_pending)
        sum_x(k)
        z_pending.append(z_stage(k))
        if k + 1 < pieces:
            x_pending = x_stage(k + 1)
            if k + 2 < pieces:
                core_copy = core_stage(k + 2)
    def cols(p):
        return pl.ds(pl.multiple_of(p * width, 128), width)

    per_piece = span // width
    for k in range(pieces):
        finish_exchange(z_pending[k])
        total = own[z, :, piece(k)]
        for p in z_peers:
            total = total + recv_z[p, :, piece(k)].astype(jnp.float32)
        s3[:, piece(k)] = total
        for b in range(k * per_piece, (k + 1) * per_piece):
            @pl.when(b != y)
            def _():
                pltpu.make_async_remote_copy(
                    src_ref=s3.at[:, pl.ds(b * width, width)], dst_ref=recv_y.at[y], send_sem=y_send.at[b],
                    recv_sem=y_recv.at[y], device_id=device(x, zh, c, b, zl), device_id_type=MESH).start()
    for p in y_peers:
        pltpu.make_async_remote_copy(
            src_ref=s3.at[:, cols(p)], dst_ref=recv_y.at[p], send_sem=y_send.at[p],
            recv_sem=y_recv.at[p], device_id=device(x, zh, c, p, zl), device_id_type=MESH).wait_recv()
    for b in range(n_y):
        @pl.when(b != y)
        def _():
            pltpu.make_async_remote_copy(
                src_ref=s3.at[:, pl.ds(b * width, width)], dst_ref=recv_y.at[y], send_sem=y_send.at[b],
                recv_sem=y_recv.at[y], device_id=device(x, zh, c, b, zl), device_id_type=MESH).wait_send()
    total = s3[:, cols(y)]
    for p in y_peers:
        total = total + recv_y[p]
    g16[:, cols(y)] = total * scale
    exchange(lambda p: g16.at[:, cols(y)], lambda p: g16.at[:, cols(p)], g_send, g_recv, y_peers, y,
             lambda p: device(x, zh, c, p, zl))
    out_ref[zl] = g16[...]
    pair_copy = pltpu.make_async_remote_copy(
        src_ref=g16, dst_ref=out_ref.at[zl], send_sem=pair_sems.at[0], recv_sem=pair_sems.at[1],
        device_id=device(x, zh, c, y, 1 - zl), device_id_type=MESH)
    pair_copy.start()
    pltpu.make_async_remote_copy(
        src_ref=g16, dst_ref=out_ref.at[1 - zl], send_sem=pair_sems.at[0], recv_sem=pair_sems.at[1],
        device_id=device(x, zh, c, y, 1 - zl), device_id_type=MESH).wait_recv()
    pair_copy.wait_send()
    finish_exchange(back_pending)


def grad_reduce(partial_rows, back, z_hi, scale):
    n_x = partial_rows.shape[1]
    n_y = lax.axis_size("dp") // 2
    cols = partial_rows.shape[3]
    shard = partial_rows.shape[2] // z_hi
    half = shard // 2
    band = partial_rows.shape[2]
    f32 = jnp.float32
    return pl.pallas_call(
        functools.partial(grad_reduce_kernel, z_hi, scale),
        out_shape=(jax.ShapeDtypeStruct((2, half, cols), f32), jax.ShapeDtypeStruct(back.shape, back.dtype)),
        in_specs=[pl.BlockSpec(memory_space=pltpu.VMEM)] * 2,
        out_specs=(pl.BlockSpec(memory_space=pltpu.VMEM),) * 2,
        scratch_shapes=[
            pltpu.VMEM((n_x, band, cols), partial_rows.dtype),
            pltpu.VMEM((n_x, band, cols), partial_rows.dtype),
            pltpu.VMEM((n_x, band, cols), partial_rows.dtype),
            pltpu.VMEM((2 * z_hi, half, cols), partial_rows.dtype),
            pltpu.VMEM((2 * z_hi, half, cols), f32),
            pltpu.VMEM((2 * z_hi, half, cols), partial_rows.dtype),
            pltpu.VMEM((half, cols), f32),
            pltpu.VMEM((n_y, half, cols // n_y), f32),
            pltpu.VMEM((half, cols), f32),
            pltpu.SemaphoreType.DMA((2, PIECES)),
            pltpu.SemaphoreType.DMA((PIECES, n_x)),
            pltpu.SemaphoreType.DMA((PIECES, n_x)),
            pltpu.SemaphoreType.DMA((PIECES, 2 * z_hi)),
            pltpu.SemaphoreType.DMA((PIECES, 2 * z_hi)),
            pltpu.SemaphoreType.DMA((n_y,)),
            pltpu.SemaphoreType.DMA((n_y,)),
            pltpu.SemaphoreType.DMA((n_y,)),
            pltpu.SemaphoreType.DMA((n_y,)),
            pltpu.SemaphoreType.DMA((2,)),
            pltpu.SemaphoreType.DMA((2, back.shape[0])),
        ],
        compiler_params=pltpu.CompilerParams(
            collective_id=1, has_side_effects=True, vmem_limit_bytes=48 * 1024 * 1024),
    )(partial_rows, back)


def tap_starts(context_row_block):
    return [context_row_block - (2 - selected_index) * DILATION_SIZE for selected_index in range(3)]


def per_device(signal, grad_gated, conv_weight, source_seg):
    peer_count = lax.axis_size("fsdp")
    seg_count = source_seg.shape[1]
    row_count = signal.shape[0]
    seg_rows = row_count // seg_count
    context_row_block = 2 * DILATION_SIZE
    starts = tap_starts(context_row_block)
    segments = signal.reshape(seg_count, seg_rows, C)
    sources = source_seg[0]
    source_dev = jnp.where(sources >= 0, sources // seg_count, -1)
    peers = jnp.arange(peer_count, dtype=jnp.int32)
    request_mask = (source_dev[None, :] == peers[:, None]).astype(jnp.int32)
    asked = lax.all_to_all(request_mask, "fsdp", split_axis=0, concat_axis=0, tiled=True)
    send_table = asked.astype(jnp.bfloat16)
    recv_table = (source_dev[:, None] == peers[None, :]).astype(jnp.bfloat16)
    outgoing = jnp.einsum(
        "ns,slc->nlc", send_table, segments, preferred_element_type=jnp.float32
    ).astype(jnp.bfloat16)
    incoming = lax.all_to_all(outgoing, "fsdp", split_axis=0, concat_axis=0, tiled=True)
    carries = jnp.einsum(
        "sn,nlc->slc", recv_table, incoming, preferred_element_type=jnp.float32
    ).astype(jnp.bfloat16)
    extended = jnp.concatenate([carries, segments], axis=1)
    full_weight = lax.all_gather(conv_weight, "fsdp", axis=0, tiled=True)
    contract_final_axis = (((1,), (1,)), ((), ()))
    contract_first = (((0,), (0,)), ((), ()))
    windows = [extended[:, start : start + seg_rows, :].reshape(row_count, C) for start in starts]
    stacked = jnp.concatenate(windows, axis=1)
    preact = lax.dot_general(
        stacked, full_weight, contract_final_axis, preferred_element_type=jnp.float32
    )
    filter_act = jnp.tanh(preact[:, :H])
    gate_act = jax.nn.sigmoid(preact[:, H:])
    gated_out = (filter_act * gate_act).astype(jnp.bfloat16)
    upstream_wide = grad_gated.astype(jnp.float32)
    grad_pre = jnp.concatenate(
        [
            upstream_wide * gate_act * (1.0 - filter_act * filter_act),
            upstream_wide * filter_act * gate_act * (1.0 - gate_act),
        ],
        axis=1,
    ).astype(jnp.bfloat16)
    z_hi = Z_HI
    n_x = peer_count // (2 * z_hi)
    shard = conv_weight.shape[0]
    routed = (
        grad_pre.reshape(row_count, n_x, z_hi, 2, shard)
        .transpose(0, 3, 1, 2, 4)
        .reshape(row_count, 2 * H)
    )
    partial_value = lax.dot_general(
        routed, stacked, contract_first, preferred_element_type=jnp.float32
    ).astype(jnp.bfloat16)
    back_proj = jnp.dot(grad_pre, full_weight, preferred_element_type=jnp.float32)
    back_proj = back_proj.reshape(seg_count, seg_rows, 3 * C)
    grad_ext = jnp.zeros((seg_count, context_row_block + seg_rows, C), jnp.float32)
    for selected_index, start in enumerate(starts):
        grad_ext = grad_ext.at[:, start : start + seg_rows, :].add(
            back_proj[:, :, selected_index * C : (selected_index + 1) * C]
        )
    outgoing_grad = jnp.einsum(
        "sn,slc->nlc",
        recv_table,
        grad_ext[:, :context_row_block, :].astype(jnp.bfloat16),
        preferred_element_type=jnp.float32,
    ).astype(jnp.bfloat16)
    total_token_count = row_count * peer_count * lax.axis_size("dp")
    reduced, incoming_grad = grad_reduce(
        partial_value.reshape(2, n_x, z_hi * shard, 3 * C),
        outgoing_grad,
        z_hi,
        1.0 / math.sqrt(total_token_count),
    )
    grad_weight = reduced.reshape(shard, 3 * C)
    tail_grad = jnp.einsum(
        "ns,nlc->slc",
        send_table,
        incoming_grad,
        preferred_element_type=jnp.float32,
    )
    grad_in = (
        grad_ext[:, context_row_block:, :].at[:, seg_rows - context_row_block :, :].add(tail_grad)
    )
    grad_in = grad_in.reshape(row_count, C).astype(jnp.bfloat16)
    return (gated_out, grad_in, grad_weight)


def solution(mesh):
    placed = (
        P(("dp", "fsdp"), None),
        P(("dp", "fsdp"), None),
        P("fsdp", None),
        P(("dp", "fsdp"), None),
    )
    return jax.shard_map(
        per_device,
        mesh=mesh,
        in_specs=placed,
        out_specs=(P(("dp", "fsdp"), None), P(("dp", "fsdp"), None), P("fsdp", None)),
        check_vma=False,
    )
```

```python
import functools
import math

import jax
import jax.numpy as jnp
from jax import lax
from jax.experimental import pallas as pl
from jax.experimental.pallas import tpu as pltpu
from jax.sharding import PartitionSpec as P

MESH = pl.DeviceIdType.MESH

C = 1024
H = 512
DILATION_SIZE = 4
Z_HI = 4
PIECES = 2


def all_reduce_kernel(axis, n, x_ref, out_ref, gathered, summed, send_sems, recv_sems, out_send, out_recv):
    me = lax.axis_index(axis)
    barrier = pltpu.get_barrier_semaphore()
    for k in range(1, n):
        peer = lax.rem(me + k, n)
        pl.semaphore_signal(barrier, inc=1, device_id={axis: peer}, device_id_type=MESH)
    pl.semaphore_wait(barrier, n - 1)
    sends = []
    for k in range(1, n):
        peer = lax.rem(me + k, n)
        copy = pltpu.make_async_remote_copy(
            src_ref=x_ref.at[peer],
            dst_ref=gathered.at[me],
            send_sem=send_sems.at[peer],
            recv_sem=recv_sems.at[me],
            device_id={axis: peer},
            device_id_type=MESH,
        )
        copy.start()
        sends.append(copy)
    gathered[me] = x_ref[me]
    for k in range(1, n):
        peer = lax.rem(me + k, n)
        pltpu.make_async_remote_copy(
            src_ref=x_ref.at[peer],
            dst_ref=gathered.at[peer],
            send_sem=send_sems.at[peer],
            recv_sem=recv_sems.at[peer],
            device_id={axis: peer},
            device_id_type=MESH,
        ).wait_recv()
    for copy in sends:
        copy.wait_send()
    total = gathered[0]
    for k in range(1, n):
        total = total + gathered[k]
    summed[...] = total
    out_ref[me] = total
    shares = []
    for k in range(1, n):
        peer = lax.rem(me + k, n)
        copy = pltpu.make_async_remote_copy(
            src_ref=summed,
            dst_ref=out_ref.at[me],
            send_sem=out_send.at[peer],
            recv_sem=out_recv.at[me],
            device_id={axis: peer},
            device_id_type=MESH,
        )
        copy.start()
        shares.append(copy)
    for k in range(1, n):
        peer = lax.rem(me + k, n)
        pltpu.make_async_remote_copy(
            src_ref=summed,
            dst_ref=out_ref.at[peer],
            send_sem=out_send.at[peer],
            recv_sem=out_recv.at[peer],
            device_id={axis: peer},
            device_id_type=MESH,
        ).wait_recv()
    for copy in shares:
        copy.wait_send()


def all_reduce(x, axis):
    n = lax.axis_size(axis)
    shape = x.shape
    blocks = x.reshape(n, -1, 128)
    block_shape = blocks.shape[1:]
    out = pl.pallas_call(
        functools.partial(all_reduce_kernel, axis, n),
        out_shape=jax.ShapeDtypeStruct(blocks.shape, x.dtype),
        in_specs=[pl.BlockSpec(memory_space=pltpu.VMEM)],
        out_specs=pl.BlockSpec(memory_space=pltpu.VMEM),
        scratch_shapes=[
            pltpu.VMEM(blocks.shape, x.dtype),
            pltpu.VMEM(block_shape, x.dtype),
            pltpu.SemaphoreType.DMA((n,)),
            pltpu.SemaphoreType.DMA((n,)),
            pltpu.SemaphoreType.DMA((n,)),
            pltpu.SemaphoreType.DMA((n,)),
        ],
        compiler_params=pltpu.CompilerParams(collective_id=0, has_side_effects=True),
    )(blocks)
    return out.reshape(shape)


def grad_reduce_kernel(z_hi, scale, p_ref, back_ref, out_ref, back_out, recv_c, s1b, recv_x, s2, own, recv_z, s3, recv_y, g16,
                       core_sems, x_send, x_recv, z_send, z_recv, y_send, y_recv, g_send, g_recv, pair_sems,
                       back_sems):
    n_x = recv_x.shape[0]
    n_z = 2 * z_hi
    n_y = recv_y.shape[0]
    band = recv_c.shape[1]
    half = s2.shape[1]
    width = recv_y.shape[2]
    f = lax.axis_index("fsdp")
    d = lax.axis_index("dp")
    c = lax.rem(f, 2)
    zh = lax.rem(f // 2, z_hi)
    x = f // (2 * z_hi)
    zl = lax.rem(d, 2)
    y = d // 2
    z = zh * 2 + zl

    def device(x_, zh_, c_, y_, zl_):
        return {"dp": y_ * 2 + zl_, "fsdp": (x_ * z_hi + zh_) * 2 + c_}

    partner = device(x, zh, 1 - c, y, zl)
    x_peers = [lax.rem(x + k, n_x) for k in range(1, n_x)]
    z_peers = [lax.rem(z + k, n_z) for k in range(1, n_z)]
    y_peers = [lax.rem(y + k, n_y) for k in range(1, n_y)]
    n_f = back_ref.shape[0]
    f_peers = [lax.rem(f + k, n_f) for k in range(1, n_f)]
    everyone = [{"dp": d, "fsdp": fp} for fp in f_peers]
    everyone += [device(x, zp // 2, c, y, lax.rem(zp, 2)) for k, zp in enumerate(z_peers, 1) if k % 2]
    everyone += [device(x, zh, c, yp, zl) for yp in y_peers]
    barrier = pltpu.get_barrier_semaphore()
    for peer in everyone:
        pl.semaphore_signal(barrier, inc=1, device_id=peer, device_id_type=MESH)
    pl.semaphore_wait(barrier, len(everyone))

    def start_exchange(src_of, dst_of, send_sems, recv_sems, peers, mine, device_of):
        sends, arrivals = [], []
        for p in peers:
            copy = pltpu.make_async_remote_copy(
                src_ref=src_of(p), dst_ref=dst_of(mine), send_sem=send_sems.at[p],
                recv_sem=recv_sems.at[mine], device_id=device_of(p), device_id_type=MESH)
            copy.start()
            sends.append(copy)
            arrivals.append(pltpu.make_async_remote_copy(
                src_ref=src_of(p), dst_ref=dst_of(p), send_sem=send_sems.at[p],
                recv_sem=recv_sems.at[p], device_id=device_of(p), device_id_type=MESH))
        return sends, arrivals

    def finish_exchange(pending):
        sends, arrivals = pending
        for copy in arrivals:
            copy.wait_recv()
        for copy in sends:
            copy.wait_send()

    def exchange(*args):
        finish_exchange(start_exchange(*args))

    back_pending = start_exchange(lambda p: back_ref.at[p], lambda p: back_out.at[p], back_sems.at[0],
                                  back_sems.at[1], f_peers, f, lambda p: {"dp": d, "fsdp": p})
    back_out[f] = back_ref[f]
    rows = 32
    chunks = band // rows

    pieces = x_send.shape[0]
    span = s1b.shape[2] // pieces

    def piece(k):
        return pl.ds(k * span, span)

    def core_stage(k):
        copy = pltpu.make_async_remote_copy(
            src_ref=p_ref.at[1 - c, :, :, piece(k)], dst_ref=recv_c.at[:, :, piece(k)],
            send_sem=core_sems.at[0, k], recv_sem=core_sems.at[1, k], device_id=partner,
            device_id_type=MESH)
        copy.start()
        return copy

    def round_two_sums(k):
        def body(i, carry):
            xi, r = i // chunks, lax.rem(i, chunks)
            at = pl.ds(pl.multiple_of(r * rows, rows), rows)
            both = (p_ref[c, xi, at, piece(k)].astype(jnp.float32)
                    + recv_c[xi, at, piece(k)].astype(jnp.float32))
            s1b[xi, at, piece(k)] = both.astype(s1b.dtype)
            return carry
        lax.fori_loop(0, n_x * chunks, body, 0)

    def x_stage(k):
        return start_exchange(lambda p: s1b.at[p, :, piece(k)], lambda p: recv_x.at[p, :, piece(k)],
                              x_send.at[k], x_recv.at[k], x_peers, x, lambda p: device(p, zh, c, y, zl))

    def z_stage(k):
        return start_exchange(lambda p: s2.at[p, :, piece(k)], lambda p: recv_z.at[p, :, piece(k)],
                              z_send.at[k], z_recv.at[k], z_peers, z,
                              lambda p: device(x, p // 2, c, y, lax.rem(p, 2)))

    def sum_x(k):
        def body(j, carry):
            at = pl.ds(pl.multiple_of(j * half, half), half)
            total = (p_ref[c, x, at, piece(k)].astype(jnp.float32)
                     + recv_c[x, at, piece(k)].astype(jnp.float32))
            for p in x_peers:
                total = total + recv_x[p, at, piece(k)].astype(jnp.float32)
            s2[j, :, piece(k)] = total.astype(s2.dtype)
            own[j, :, piece(k)] = total
            return carry
        lax.fori_loop(0, n_z, body, 0)

    core_copy = core_stage(0)
    core_copy.wait()
    round_two_sums(0)
    x_pending = x_stage(0)
    if pieces > 1:
        core_copy = core_stage(1)
    z_pending = []
    for k in range(pieces):
        if k + 1 < pieces:
            core_copy.wait()
            round_two_sums(k + 1)
        finish_exchange(x_pending)
        sum_x(k)
        z_pending.append(z_stage(k))
        if k + 1 < pieces:
            x_pending = x_stage(k + 1)
            if k + 2 < pieces:
                core_copy = core_stage(k + 2)
    def cols(p):
        return pl.ds(pl.multiple_of(p * width, 128), width)

    per_piece = span // width
    for k in range(pieces):
        finish_exchange(z_pending[k])
        total = own[z, :, piece(k)]
        for p in z_peers:
            total = total + recv_z[p, :, piece(k)].astype(jnp.float32)
        s3[:, piece(k)] = total
        for b in range(k * per_piece, (k + 1) * per_piece):
            @pl.when(b != y)
            def _():
                pltpu.make_async_remote_copy(
                    src_ref=s3.at[:, pl.ds(b * width, width)], dst_ref=recv_y.at[y], send_sem=y_send.at[b],
                    recv_sem=y_recv.at[y], device_id=device(x, zh, c, b, zl), device_id_type=MESH).start()
    for p in y_peers:
        pltpu.make_async_remote_copy(
            src_ref=s3.at[:, cols(p)], dst_ref=recv_y.at[p], send_sem=y_send.at[p],
            recv_sem=y_recv.at[p], device_id=device(x, zh, c, p, zl), device_id_type=MESH).wait_recv()
    for b in range(n_y):
        @pl.when(b != y)
        def _():
            pltpu.make_async_remote_copy(
                src_ref=s3.at[:, pl.ds(b * width, width)], dst_ref=recv_y.at[y], send_sem=y_send.at[b],
                recv_sem=y_recv.at[y], device_id=device(x, zh, c, b, zl), device_id_type=MESH).wait_send()
    total = s3[:, cols(y)]
    for p in y_peers:
        total = total + recv_y[p]
    g16[:, cols(y)] = total * scale
    exchange(lambda p: g16.at[:, cols(y)], lambda p: g16.at[:, cols(p)], g_send, g_recv, y_peers, y,
             lambda p: device(x, zh, c, p, zl))
    out_ref[zl] = g16[...]
    pair_copy = pltpu.make_async_remote_copy(
        src_ref=g16, dst_ref=out_ref.at[zl], send_sem=pair_sems.at[0], recv_sem=pair_sems.at[1],
        device_id=device(x, zh, c, y, 1 - zl), device_id_type=MESH)
    pair_copy.start()
    pltpu.make_async_remote_copy(
        src_ref=g16, dst_ref=out_ref.at[1 - zl], send_sem=pair_sems.at[0], recv_sem=pair_sems.at[1],
        device_id=device(x, zh, c, y, 1 - zl), device_id_type=MESH).wait_recv()
    pair_copy.wait_send()
    finish_exchange(back_pending)


def grad_reduce(partial_rows, back, z_hi, scale):
    n_x = partial_rows.shape[1]
    n_y = lax.axis_size("dp") // 2
    cols = partial_rows.shape[3]
    shard = partial_rows.shape[2] // z_hi
    half = shard // 2
    band = partial_rows.shape[2]
    f32 = jnp.float32
    return pl.pallas_call(
        functools.partial(grad_reduce_kernel, z_hi, scale),
        out_shape=(jax.ShapeDtypeStruct((2, half, cols), f32), jax.ShapeDtypeStruct(back.shape, back.dtype)),
        in_specs=[pl.BlockSpec(memory_space=pltpu.VMEM)] * 2,
        out_specs=(pl.BlockSpec(memory_space=pltpu.VMEM),) * 2,
        scratch_shapes=[
            pltpu.VMEM((n_x, band, cols), partial_rows.dtype),
            pltpu.VMEM((n_x, band, cols), partial_rows.dtype),
            pltpu.VMEM((n_x, band, cols), partial_rows.dtype),
            pltpu.VMEM((2 * z_hi, half, cols), partial_rows.dtype),
            pltpu.VMEM((2 * z_hi, half, cols), f32),
            pltpu.VMEM((2 * z_hi, half, cols), partial_rows.dtype),
            pltpu.VMEM((half, cols), f32),
            pltpu.VMEM((n_y, half, cols // n_y), f32),
            pltpu.VMEM((half, cols), f32),
            pltpu.SemaphoreType.DMA((2, PIECES)),
            pltpu.SemaphoreType.DMA((PIECES, n_x)),
            pltpu.SemaphoreType.DMA((PIECES, n_x)),
            pltpu.SemaphoreType.DMA((PIECES, 2 * z_hi)),
            pltpu.SemaphoreType.DMA((PIECES, 2 * z_hi)),
            pltpu.SemaphoreType.DMA((n_y,)),
            pltpu.SemaphoreType.DMA((n_y,)),
            pltpu.SemaphoreType.DMA((n_y,)),
            pltpu.SemaphoreType.DMA((n_y,)),
            pltpu.SemaphoreType.DMA((2,)),
            pltpu.SemaphoreType.DMA((2, back.shape[0])),
        ],
        compiler_params=pltpu.CompilerParams(
            collective_id=1, has_side_effects=True, vmem_limit_bytes=48 * 1024 * 1024),
    )(partial_rows, back)


def tap_starts(context_row_block):
    return [context_row_block - (2 - selected_index) * DILATION_SIZE for selected_index in range(3)]


def per_device(signal, grad_gated, conv_weight, source_seg):
    peer_count = lax.axis_size("fsdp")
    seg_count = source_seg.shape[1]
    row_count = signal.shape[0]
    seg_rows = row_count // seg_count
    context_row_block = 2 * DILATION_SIZE
    starts = tap_starts(context_row_block)
    segments = signal.reshape(seg_count, seg_rows, C)
    sources = source_seg[0]
    source_dev = jnp.where(sources >= 0, sources // seg_count, -1)
    peers = jnp.arange(peer_count, dtype=jnp.int32)
    request_mask = (source_dev[None, :] == peers[:, None]).astype(jnp.int32)
    asked = lax.all_to_all(request_mask, "fsdp", split_axis=0, concat_axis=0, tiled=True)
    send_table = asked.astype(jnp.bfloat16)
    recv_table = (source_dev[:, None] == peers[None, :]).astype(jnp.bfloat16)
    outgoing = jnp.einsum(
        "ns,slc->nlc", send_table, segments, preferred_element_type=jnp.float32
    ).astype(jnp.bfloat16)
    incoming = lax.all_to_all(outgoing, "fsdp", split_axis=0, concat_axis=0, tiled=True)
    carries = jnp.einsum(
        "sn,nlc->slc", recv_table, incoming, preferred_element_type=jnp.float32
    ).astype(jnp.bfloat16)
    extended = jnp.concatenate([carries, segments], axis=1)
    half_cols = conv_weight.shape[1] // 2
    weight_halves = [
        lax.all_gather(conv_weight[:, :half_cols], "fsdp", axis=0, tiled=True),
        lax.all_gather(conv_weight[:, half_cols:], "fsdp", axis=0, tiled=True),
    ]
    full_weight = jnp.concatenate(weight_halves, axis=1)
    contract_final_axis = (((1,), (1,)), ((), ()))
    contract_first = (((0,), (0,)), ((), ()))
    windows = [extended[:, start : start + seg_rows, :].reshape(row_count, C) for start in starts]
    stacked = jnp.concatenate(windows, axis=1)
    preact = sum(
        lax.dot_general(
            stacked[:, k * half_cols : (k + 1) * half_cols],
            weight_halves[k],
            contract_final_axis,
            preferred_element_type=jnp.float32,
        )
        for k in range(2)
    )
    filter_act = jnp.tanh(preact[:, :H])
    gate_act = jax.nn.sigmoid(preact[:, H:])
    gated_out = (filter_act * gate_act).astype(jnp.bfloat16)
    upstream_wide = grad_gated.astype(jnp.float32)
    grad_pre = jnp.concatenate(
        [
            upstream_wide * gate_act * (1.0 - filter_act * filter_act),
            upstream_wide * filter_act * gate_act * (1.0 - gate_act),
        ],
        axis=1,
    ).astype(jnp.bfloat16)
    z_hi = Z_HI
    n_x = peer_count // (2 * z_hi)
    shard = conv_weight.shape[0]
    routed = (
        grad_pre.reshape(row_count, n_x, z_hi, 2, shard)
        .transpose(0, 3, 1, 2, 4)
        .reshape(row_count, 2 * H)
    )
    partial_value = lax.dot_general(
        routed, stacked, contract_first, preferred_element_type=jnp.float32
    ).astype(jnp.bfloat16)
    back_proj = jnp.dot(grad_pre, full_weight, preferred_element_type=jnp.float32)
    back_proj = back_proj.reshape(seg_count, seg_rows, 3 * C)
    grad_ext = jnp.zeros((seg_count, context_row_block + seg_rows, C), jnp.float32)
    for selected_index, start in enumerate(starts):
        grad_ext = grad_ext.at[:, start : start + seg_rows, :].add(
            back_proj[:, :, selected_index * C : (selected_index + 1) * C]
        )
    outgoing_grad = jnp.einsum(
        "sn,slc->nlc",
        recv_table,
        grad_ext[:, :context_row_block, :].astype(jnp.bfloat16),
        preferred_element_type=jnp.float32,
    ).astype(jnp.bfloat16)
    total_token_count = row_count * peer_count * lax.axis_size("dp")
    reduced, incoming_grad = grad_reduce(
        partial_value.reshape(2, n_x, z_hi * shard, 3 * C),
        outgoing_grad,
        z_hi,
        1.0 / math.sqrt(total_token_count),
    )
    grad_weight = reduced.reshape(shard, 3 * C)
    tail_grad = jnp.einsum(
        "ns,nlc->slc",
        send_table,
        incoming_grad,
        preferred_element_type=jnp.float32,
    )
    grad_in = (
        grad_ext[:, context_row_block:, :].at[:, seg_rows - context_row_block :, :].add(tail_grad)
    )
    grad_in = grad_in.reshape(row_count, C).astype(jnp.bfloat16)
    return (gated_out, grad_in, grad_weight)


def solution(mesh):
    placed = (
        P(("dp", "fsdp"), None),
        P(("dp", "fsdp"), None),
        P("fsdp", None),
        P(("dp", "fsdp"), None),
    )
    return jax.shard_map(
        per_device,
        mesh=mesh,
        in_specs=placed,
        out_specs=(P(("dp", "fsdp"), None), P(("dp", "fsdp"), None), P("fsdp", None)),
        check_vma=False,
    )
```

```python
import functools
import math

import jax
import jax.numpy as jnp
from jax import lax
from jax.experimental import pallas as pl
from jax.experimental.pallas import tpu as pltpu
from jax.sharding import PartitionSpec as P

MESH = pl.DeviceIdType.MESH

C = 1024
H = 512
DILATION_SIZE = 4
Z_HI = 4
PIECES = 2


def all_reduce_kernel(axis, n, x_ref, out_ref, gathered, summed, send_sems, recv_sems, out_send, out_recv):
    me = lax.axis_index(axis)
    barrier = pltpu.get_barrier_semaphore()
    for k in range(1, n):
        peer = lax.rem(me + k, n)
        pl.semaphore_signal(barrier, inc=1, device_id={axis: peer}, device_id_type=MESH)
    pl.semaphore_wait(barrier, n - 1)
    sends = []
    for k in range(1, n):
        peer = lax.rem(me + k, n)
        copy = pltpu.make_async_remote_copy(
            src_ref=x_ref.at[peer],
            dst_ref=gathered.at[me],
            send_sem=send_sems.at[peer],
            recv_sem=recv_sems.at[me],
            device_id={axis: peer},
            device_id_type=MESH,
        )
        copy.start()
        sends.append(copy)
    gathered[me] = x_ref[me]
    for k in range(1, n):
        peer = lax.rem(me + k, n)
        pltpu.make_async_remote_copy(
            src_ref=x_ref.at[peer],
            dst_ref=gathered.at[peer],
            send_sem=send_sems.at[peer],
            recv_sem=recv_sems.at[peer],
            device_id={axis: peer},
            device_id_type=MESH,
        ).wait_recv()
    for copy in sends:
        copy.wait_send()
    total = gathered[0]
    for k in range(1, n):
        total = total + gathered[k]
    summed[...] = total
    out_ref[me] = total
    shares = []
    for k in range(1, n):
        peer = lax.rem(me + k, n)
        copy = pltpu.make_async_remote_copy(
            src_ref=summed,
            dst_ref=out_ref.at[me],
            send_sem=out_send.at[peer],
            recv_sem=out_recv.at[me],
            device_id={axis: peer},
            device_id_type=MESH,
        )
        copy.start()
        shares.append(copy)
    for k in range(1, n):
        peer = lax.rem(me + k, n)
        pltpu.make_async_remote_copy(
            src_ref=summed,
            dst_ref=out_ref.at[peer],
            send_sem=out_send.at[peer],
            recv_sem=out_recv.at[peer],
            device_id={axis: peer},
            device_id_type=MESH,
        ).wait_recv()
    for copy in shares:
        copy.wait_send()


def all_reduce(x, axis):
    n = lax.axis_size(axis)
    shape = x.shape
    blocks = x.reshape(n, -1, 128)
    block_shape = blocks.shape[1:]
    out = pl.pallas_call(
        functools.partial(all_reduce_kernel, axis, n),
        out_shape=jax.ShapeDtypeStruct(blocks.shape, x.dtype),
        in_specs=[pl.BlockSpec(memory_space=pltpu.VMEM)],
        out_specs=pl.BlockSpec(memory_space=pltpu.VMEM),
        scratch_shapes=[
            pltpu.VMEM(blocks.shape, x.dtype),
            pltpu.VMEM(block_shape, x.dtype),
            pltpu.SemaphoreType.DMA((n,)),
            pltpu.SemaphoreType.DMA((n,)),
            pltpu.SemaphoreType.DMA((n,)),
            pltpu.SemaphoreType.DMA((n,)),
        ],
        compiler_params=pltpu.CompilerParams(collective_id=0, has_side_effects=True),
    )(blocks)
    return out.reshape(shape)


def grad_reduce_kernel(z_hi, scale, p_ref, back_ref, out_ref, back_out, recv_c, s1b, recv_x, s2, own, recv_z, s3, recv_y, g16,
                       core_sems, x_send, x_recv, z_send, z_recv, y_send, y_recv, g_send, g_recv, pair_sems,
                       back_sems):
    n_x = recv_x.shape[0]
    n_z = 2 * z_hi
    n_y = recv_y.shape[0]
    band = recv_c.shape[1]
    half = s2.shape[1]
    width = recv_y.shape[2]
    f = lax.axis_index("fsdp")
    d = lax.axis_index("dp")
    c = lax.rem(f, 2)
    zh = lax.rem(f // 2, z_hi)
    x = f // (2 * z_hi)
    zl = lax.rem(d, 2)
    y = d // 2
    z = zh * 2 + zl

    def device(x_, zh_, c_, y_, zl_):
        return {"dp": y_ * 2 + zl_, "fsdp": (x_ * z_hi + zh_) * 2 + c_}

    partner = device(x, zh, 1 - c, y, zl)
    x_peers = [lax.rem(x + k, n_x) for k in range(1, n_x)]
    z_peers = [lax.rem(z + k, n_z) for k in range(1, n_z)]
    y_peers = [lax.rem(y + k, n_y) for k in range(1, n_y)]
    n_f = back_ref.shape[0]
    f_peers = [lax.rem(f + k, n_f) for k in range(1, n_f)]
    everyone = [{"dp": d, "fsdp": fp} for fp in f_peers]
    everyone += [device(x, zp // 2, c, y, lax.rem(zp, 2)) for k, zp in enumerate(z_peers, 1) if k % 2]
    everyone += [device(x, zh, c, yp, zl) for yp in y_peers]
    barrier = pltpu.get_barrier_semaphore()
    for peer in everyone:
        pl.semaphore_signal(barrier, inc=1, device_id=peer, device_id_type=MESH)
    pl.semaphore_wait(barrier, len(everyone))

    def start_exchange(src_of, dst_of, send_sems, recv_sems, peers, mine, device_of):
        sends, arrivals = [], []
        for p in peers:
            copy = pltpu.make_async_remote_copy(
                src_ref=src_of(p), dst_ref=dst_of(mine), send_sem=send_sems.at[p],
                recv_sem=recv_sems.at[mine], device_id=device_of(p), device_id_type=MESH)
            copy.start()
            sends.append(copy)
            arrivals.append(pltpu.make_async_remote_copy(
                src_ref=src_of(p), dst_ref=dst_of(p), send_sem=send_sems.at[p],
                recv_sem=recv_sems.at[p], device_id=device_of(p), device_id_type=MESH))
        return sends, arrivals

    def finish_exchange(pending):
        sends, arrivals = pending
        for copy in arrivals:
            copy.wait_recv()
        for copy in sends:
            copy.wait_send()

    def exchange(*args):
        finish_exchange(start_exchange(*args))

    back_pending = start_exchange(lambda p: back_ref.at[p], lambda p: back_out.at[p], back_sems.at[0],
                                  back_sems.at[1], f_peers, f, lambda p: {"dp": d, "fsdp": p})
    back_out[f] = back_ref[f]
    rows = 32
    chunks = band // rows

    pieces = x_send.shape[0]
    span = s1b.shape[2] // pieces

    def piece(k):
        return pl.ds(k * span, span)

    def core_stage(k):
        copy = pltpu.make_async_remote_copy(
            src_ref=p_ref.at[1 - c, :, :, piece(k)], dst_ref=recv_c.at[:, :, piece(k)],
            send_sem=core_sems.at[0, k], recv_sem=core_sems.at[1, k], device_id=partner,
            device_id_type=MESH)
        copy.start()
        return copy

    def round_two_sums(k):
        def body(i, carry):
            xi, r = i // chunks, lax.rem(i, chunks)
            at = pl.ds(pl.multiple_of(r * rows, rows), rows)
            both = (p_ref[c, xi, at, piece(k)].astype(jnp.float32)
                    + recv_c[xi, at, piece(k)].astype(jnp.float32))
            s1b[xi, at, piece(k)] = both.astype(s1b.dtype)
            return carry
        lax.fori_loop(0, n_x * chunks, body, 0)

    def x_stage(k):
        return start_exchange(lambda p: s1b.at[p, :, piece(k)], lambda p: recv_x.at[p, :, piece(k)],
                              x_send.at[k], x_recv.at[k], x_peers, x, lambda p: device(p, zh, c, y, zl))

    def z_stage(k):
        return start_exchange(lambda p: s2.at[p, :, piece(k)], lambda p: recv_z.at[p, :, piece(k)],
                              z_send.at[k], z_recv.at[k], z_peers, z,
                              lambda p: device(x, p // 2, c, y, lax.rem(p, 2)))

    def sum_x(k):
        def body(j, carry):
            at = pl.ds(pl.multiple_of(j * half, half), half)
            total = (p_ref[c, x, at, piece(k)].astype(jnp.float32)
                     + recv_c[x, at, piece(k)].astype(jnp.float32))
            for p in x_peers:
                total = total + recv_x[p, at, piece(k)].astype(jnp.float32)
            s2[j, :, piece(k)] = total.astype(s2.dtype)
            own[j, :, piece(k)] = total
            return carry
        lax.fori_loop(0, n_z, body, 0)

    core_copy = core_stage(0)
    core_copy.wait()
    round_two_sums(0)
    x_pending = x_stage(0)
    if pieces > 1:
        core_copy = core_stage(1)
    z_pending = []
    for k in range(pieces):
        if k + 1 < pieces:
            core_copy.wait()
            round_two_sums(k + 1)
        finish_exchange(x_pending)
        sum_x(k)
        z_pending.append(z_stage(k))
        if k + 1 < pieces:
            x_pending = x_stage(k + 1)
            if k + 2 < pieces:
                core_copy = core_stage(k + 2)
    def cols(p):
        return pl.ds(pl.multiple_of(p * width, 128), width)

    per_piece = span // width
    for k in range(pieces):
        finish_exchange(z_pending[k])
        total = own[z, :, piece(k)]
        for p in z_peers:
            total = total + recv_z[p, :, piece(k)].astype(jnp.float32)
        s3[:, piece(k)] = total
        for b in range(k * per_piece, (k + 1) * per_piece):
            @pl.when(b != y)
            def _():
                pltpu.make_async_remote_copy(
                    src_ref=s3.at[:, pl.ds(b * width, width)], dst_ref=recv_y.at[y], send_sem=y_send.at[b],
                    recv_sem=y_recv.at[y], device_id=device(x, zh, c, b, zl), device_id_type=MESH).start()
    for p in y_peers:
        pltpu.make_async_remote_copy(
            src_ref=s3.at[:, cols(p)], dst_ref=recv_y.at[p], send_sem=y_send.at[p],
            recv_sem=y_recv.at[p], device_id=device(x, zh, c, p, zl), device_id_type=MESH).wait_recv()
    for b in range(n_y):
        @pl.when(b != y)
        def _():
            pltpu.make_async_remote_copy(
                src_ref=s3.at[:, pl.ds(b * width, width)], dst_ref=recv_y.at[y], send_sem=y_send.at[b],
                recv_sem=y_recv.at[y], device_id=device(x, zh, c, b, zl), device_id_type=MESH).wait_send()
    total = s3[:, cols(y)]
    for p in y_peers:
        total = total + recv_y[p]
    g16[:, cols(y)] = total * scale
    exchange(lambda p: g16.at[:, cols(y)], lambda p: g16.at[:, cols(p)], g_send, g_recv, y_peers, y,
             lambda p: device(x, zh, c, p, zl))
    out_ref[zl] = g16[...]
    pair_copy = pltpu.make_async_remote_copy(
        src_ref=g16, dst_ref=out_ref.at[zl], send_sem=pair_sems.at[0], recv_sem=pair_sems.at[1],
        device_id=device(x, zh, c, y, 1 - zl), device_id_type=MESH)
    pair_copy.start()
    pltpu.make_async_remote_copy(
        src_ref=g16, dst_ref=out_ref.at[1 - zl], send_sem=pair_sems.at[0], recv_sem=pair_sems.at[1],
        device_id=device(x, zh, c, y, 1 - zl), device_id_type=MESH).wait_recv()
    pair_copy.wait_send()
    finish_exchange(back_pending)


def grad_reduce(partial_rows, back, z_hi, scale):
    n_x = partial_rows.shape[1]
    n_y = lax.axis_size("dp") // 2
    cols = partial_rows.shape[3]
    shard = partial_rows.shape[2] // z_hi
    half = shard // 2
    band = partial_rows.shape[2]
    f32 = jnp.float32
    return pl.pallas_call(
        functools.partial(grad_reduce_kernel, z_hi, scale),
        out_shape=(jax.ShapeDtypeStruct((2, half, cols), f32), jax.ShapeDtypeStruct(back.shape, back.dtype)),
        in_specs=[pl.BlockSpec(memory_space=pltpu.VMEM)] * 2,
        out_specs=(pl.BlockSpec(memory_space=pltpu.VMEM),) * 2,
        scratch_shapes=[
            pltpu.VMEM((n_x, band, cols), partial_rows.dtype),
            pltpu.VMEM((n_x, band, cols), partial_rows.dtype),
            pltpu.VMEM((n_x, band, cols), partial_rows.dtype),
            pltpu.VMEM((2 * z_hi, half, cols), partial_rows.dtype),
            pltpu.VMEM((2 * z_hi, half, cols), f32),
            pltpu.VMEM((2 * z_hi, half, cols), partial_rows.dtype),
            pltpu.VMEM((half, cols), f32),
            pltpu.VMEM((n_y, half, cols // n_y), f32),
            pltpu.VMEM((half, cols), f32),
            pltpu.SemaphoreType.DMA((2, PIECES)),
            pltpu.SemaphoreType.DMA((PIECES, n_x)),
            pltpu.SemaphoreType.DMA((PIECES, n_x)),
            pltpu.SemaphoreType.DMA((PIECES, 2 * z_hi)),
            pltpu.SemaphoreType.DMA((PIECES, 2 * z_hi)),
            pltpu.SemaphoreType.DMA((n_y,)),
            pltpu.SemaphoreType.DMA((n_y,)),
            pltpu.SemaphoreType.DMA((n_y,)),
            pltpu.SemaphoreType.DMA((n_y,)),
            pltpu.SemaphoreType.DMA((2,)),
            pltpu.SemaphoreType.DMA((2, back.shape[0])),
        ],
        compiler_params=pltpu.CompilerParams(
            collective_id=1, has_side_effects=True, vmem_limit_bytes=48 * 1024 * 1024),
    )(partial_rows, back)


def tap_starts(context_row_block):
    return [context_row_block - (2 - selected_index) * DILATION_SIZE for selected_index in range(3)]


def per_device(signal, grad_gated, conv_weight, source_seg):
    peer_count = lax.axis_size("fsdp")
    seg_count = source_seg.shape[1]
    row_count = signal.shape[0]
    seg_rows = row_count // seg_count
    context_row_block = 2 * DILATION_SIZE
    starts = tap_starts(context_row_block)
    segments = signal.reshape(seg_count, seg_rows, C)
    sources = source_seg[0]
    source_dev = jnp.where(sources >= 0, sources // seg_count, -1)
    peers = jnp.arange(peer_count, dtype=jnp.int32)
    request_mask = (source_dev[None, :] == peers[:, None]).astype(jnp.int32)
    asked = lax.all_to_all(request_mask, "fsdp", split_axis=0, concat_axis=0, tiled=True)
    send_table = asked.astype(jnp.bfloat16)
    recv_table = (source_dev[:, None] == peers[None, :]).astype(jnp.bfloat16)
    outgoing = jnp.einsum(
        "ns,slc->nlc", send_table, segments, preferred_element_type=jnp.float32
    ).astype(jnp.bfloat16)
    incoming = lax.all_to_all(outgoing, "fsdp", split_axis=0, concat_axis=0, tiled=True)
    carries = jnp.einsum(
        "sn,nlc->slc", recv_table, incoming, preferred_element_type=jnp.float32
    ).astype(jnp.bfloat16)
    extended = jnp.concatenate([carries, segments], axis=1)
    full_weight = lax.all_gather(conv_weight, "fsdp", axis=0, tiled=True)
    contract_final_axis = (((1,), (1,)), ((), ()))
    contract_first = (((0,), (0,)), ((), ()))
    windows = [extended[:, start : start + seg_rows, :].reshape(row_count, C) for start in starts]
    stacked = jnp.concatenate(windows, axis=1)
    preact = lax.dot_general(
        stacked, full_weight, contract_final_axis, preferred_element_type=jnp.float32
    )
    filter_act = jnp.tanh(preact[:, :H])
    gate_act = jax.nn.sigmoid(preact[:, H:])
    gated_out = (filter_act * gate_act).astype(jnp.bfloat16)
    upstream_wide = grad_gated.astype(jnp.float32)
    grad_pre = jnp.concatenate(
        [
            upstream_wide * gate_act * (1.0 - filter_act * filter_act),
            upstream_wide * filter_act * gate_act * (1.0 - gate_act),
        ],
        axis=1,
    ).astype(jnp.bfloat16)
    z_hi = Z_HI
    n_x = peer_count // (2 * z_hi)
    shard = conv_weight.shape[0]
    routed = (
        grad_pre.reshape(row_count, n_x, z_hi, 2, shard)
        .transpose(0, 3, 1, 2, 4)
        .reshape(row_count, 2 * H)
    )
    partial_value = lax.dot_general(
        routed, stacked, contract_first, preferred_element_type=jnp.float32
    ).astype(jnp.bfloat16)
    back_proj = jnp.dot(grad_pre, full_weight, preferred_element_type=jnp.float32)
    row_in_seg = lax.rem(lax.broadcasted_iota(jnp.int32, (row_count, 1), 0), seg_rows)
    taps = [back_proj[:, selected_index * C : (selected_index + 1) * C] for selected_index in range(3)]

    def extended_rows(first):
        total = None
        for selected_index, start in enumerate(starts):
            shift = first - start
            if shift <= -seg_rows or shift >= seg_rows:
                continue
            term = taps[selected_index]
            if shift != 0:
                inside = (row_in_seg + shift >= 0) & (row_in_seg + shift < seg_rows)
                term = jnp.where(inside, jnp.roll(term, -shift, axis=0), 0.0)
            total = term if total is None else total + term
        return total

    carry_rows = extended_rows(0).reshape(seg_count, seg_rows, C)
    outgoing_grad = jnp.einsum(
        "sn,slc->nlc",
        recv_table,
        carry_rows.astype(jnp.bfloat16),
        preferred_element_type=jnp.float32,
    ).astype(jnp.bfloat16)
    total_token_count = row_count * peer_count * lax.axis_size("dp")
    reduced, incoming_grad = grad_reduce(
        partial_value.reshape(2, n_x, z_hi * shard, 3 * C),
        outgoing_grad,
        z_hi,
        1.0 / math.sqrt(total_token_count),
    )
    grad_weight = reduced.reshape(shard, 3 * C)
    tail_grad = jnp.einsum(
        "ns,nlc->slc",
        send_table,
        incoming_grad,
        preferred_element_type=jnp.float32,
    )
    grad_in = extended_rows(context_row_block) + tail_grad.reshape(row_count, C)
    grad_in = grad_in.astype(jnp.bfloat16)
    return (gated_out, grad_in, grad_weight)


def solution(mesh):
    placed = (
        P(("dp", "fsdp"), None),
        P(("dp", "fsdp"), None),
        P("fsdp", None),
        P(("dp", "fsdp"), None),
    )
    return jax.shard_map(
        per_device,
        mesh=mesh,
        in_specs=placed,
        out_specs=(P(("dp", "fsdp"), None), P(("dp", "fsdp"), None), P("fsdp", None)),
        check_vma=False,
    )
```
